128 devices in a mesh: row: 8 (over z_hi, y), col: 16 (over z_lo, x, core).
Axes of the slice: x: 4, y: 4, z: 4 (z_hi: 2, z_lo: 2; z = z_hi * 2 + z_lo), core: 2. Of those that a mesh axis runs over, the one named last changes fastest.
Arguments:
- node_features: bfloat16 [6144, 1024], P('row'), may hold values from -28 to 28
- edge_weight: bfloat16 [6144, 6144], P('row', 'col'), may hold values from -0.078125 to 0.078125
- pattern: int32 [48, 48], P('row', 'col'), may hold values from 0 to 1, as said below
- w_qkv: bfloat16 [1024, 3072], replicated, may hold values from -0.1875 to 0.1875
- w_out: bfloat16 [1024, 1024], P(None, 'col'), may hold values from -0.1875 to 0.1875
- bias_gain: float32 [16], replicated, may hold values from -2 to 2
- bias_rate: float32 [16], replicated, may hold values from 2 to 12
Outputs:
- mixed: bfloat16 [6144, 1024], P('row', 'col')
The draws below stay inside these ranges and needn't reach their ends.
Inputs may be any that keep to these rules, and one draw needn't show every extreme that they name: pattern[i][i] is 1 for every i; the share of ones differs from block-row to block-row.
All inputs are finite; a program needn't handle non-finite values.
Results may differ from the reference program's by a relative error of at most 0.02.
Values may be sent and summed in bfloat16 or wider, within the bound.
A program may use at most 128 MiB of HBM per device.

```python
import math
import jax
import jax.numpy as jnp
from jax import lax

D = 1024
HEADS = 16
BLK = 128
SWEEPS = 3
HDIM = 64
NODES = 6144
NBLK = 48


def draw_pattern(key, part):
    first, second = jax.random.split(jax.random.fold_in(key, 11))
    density = jax.random.randint(first, (NBLK, 1), 2, 10)
    coins = jax.random.randint(second, (NBLK, NBLK), 0, 10)
    diagonal = jnp.arange(NBLK)[:, None] == jnp.arange(NBLK)[None, :]
    return jnp.where(diagonal | (coins < density), 1, 0).astype(jnp.int32)


def draw_node_features(key, part):
    first = jax.random.fold_in(jax.random.fold_in(key, 23), 0)
    values = jax.random.truncated_normal(first, -4.0, 4.0, (NODES, D), jnp.float32)
    return values.astype(jnp.bfloat16)


def level_of(stream_key, dims, cuts, least, top_value):
    level = 1.0
    for axis_at, parts in cuts:
        draws = jax.random.uniform(jax.random.fold_in(jax.random.fold_in(stream_key, 6), axis_at), (parts,), jnp.float32, least / len(cuts), top_value / len(cuts))
        level = level * jnp.repeat(jnp.exp(draws), dims[axis_at] // parts).reshape((-1,) + (1,) * (len(dims) - 1 - axis_at))
    return level


def normal_values(key, shape, spread, reach, shards=(), kind=jnp.bfloat16):
    level = level_of(key, shape, shards, -0.22, 0.18) if shards else 1.0
    array = jax.random.normal(key, shape, jnp.float32) * spread * level
    return jnp.minimum(jnp.maximum(array, -reach), reach).astype(kind)


def setup_inputs(seed: int = 0) -> dict:
    streams_of = jax.random.split(jax.random.key(seed), 8)
    return {
        "node_features": draw_node_features(jax.random.fold_in(streams_of[7], 71), 0),
        "edge_weight": normal_values(streams_of[1], (NODES, NODES), NODES ** -0.5, 0.078125, ((0, 8), (1, 16))),
        "pattern": draw_pattern(jax.random.fold_in(streams_of[7], 71), 0),
        "w_qkv": normal_values(streams_of[3], (D, 3 * D), D ** -0.5, 0.1875),
        "w_out": normal_values(streams_of[4], (D, D), D ** -0.5, 0.1875, ((1, 16),)),
        "bias_gain": jnp.clip(jax.random.uniform(streams_of[5], (HEADS,), jnp.float32, -2.0, 2.0), -2.0, 2.0),
        "bias_rate": jnp.clip(jnp.exp(jax.random.uniform(streams_of[6], (HEADS,), jnp.float32, math.log(2.0), math.log(12.0))), 2.0, 12.0),
    }


def expand_blocks(pattern):
    block_rows, block_cols = pattern.shape
    grid = jnp.broadcast_to(pattern[:, None, :, None] > 0, (block_rows, BLK, block_cols, BLK))
    return grid.reshape(block_rows * BLK, block_cols * BLK)

def reference(node_features, edge_weight, pattern, w_qkv, w_out, bias_gain, bias_rate):
    keep_mask = expand_blocks(pattern)
    adjacency = jnp.where(keep_mask, edge_weight, jnp.zeros_like(edge_weight))
    indices = lax.iota(jnp.int32, NODES)
    identity = (indices[:, None] == indices[None, :]).astype(jnp.float32)
    zero = jnp.zeros((), jnp.float32)
    ranks = jnp.where(keep_mask, 0.15 * identity + 0.1275 * adjacency.astype(jnp.float32), zero)
    for sweep_index in range(SWEEPS - 1):
        product = jnp.dot(adjacency, ranks.astype(jnp.bfloat16), preferred_element_type=jnp.float32)
        ranks = jnp.where(keep_mask, 0.15 * identity + 0.85 * product, zero)
    projected = jnp.dot(node_features, w_qkv, preferred_element_type=jnp.float32).astype(jnp.bfloat16)
    heads_query = projected[:, :D].reshape(NODES, HEADS, HDIM).transpose(1, 0, 2)
    heads_key = projected[:, D:2 * D].reshape(NODES, HEADS, HDIM).transpose(1, 0, 2)
    heads_value = projected[:, 2 * D:].reshape(NODES, HEADS, HDIM).transpose(1, 0, 2)
    root_nodes = math.sqrt(NODES)
    score_scale = 1.0 / math.sqrt(HDIM)

    def one_head(items):
        query, keys, values, gain, rate = items
        scores = jnp.dot(query, keys.T, preferred_element_type=jnp.float32) * score_scale
        scores = scores + gain * jnp.tanh(rate * root_nodes * ranks)
        masked = jnp.where(keep_mask, scores, -1e+30)
        peak = lax.optimization_barrier(jnp.max(masked, axis=1, keepdims=True))
        expo = jnp.where(keep_mask, jnp.exp(masked - peak), zero)
        totals = lax.optimization_barrier(jnp.sum(expo, axis=1, keepdims=True))
        numer = jnp.dot(expo.astype(jnp.bfloat16), values, preferred_element_type=jnp.float32)
        return (numer / totals).astype(jnp.bfloat16)
    attended = lax.map(one_head, (heads_query, heads_key, heads_value, bias_gain, bias_rate))
    attended = attended.transpose(1, 0, 2).reshape(NODES, D)
    return jnp.dot(attended, w_out, preferred_element_type=jnp.float32).astype(jnp.bfloat16)
```

```python
import math

import jax
import jax.numpy as jnp
from jax import lax
from jax.experimental import pallas as pl
from jax.experimental.pallas import tpu as pltpu
from jax.sharding import PartitionSpec as P

D = 1024
HEADS = 16
BLK = 128
HDIM = 64
NODES = 6144
ROWS = 768
HALF = 384
QC = 3
CLS = 4
PIECE = 32
LOG2E = 1.4426950408889634
BIG = 1e30
MESH = pl.DeviceIdType.MESH
F32 = jnp.float32
BF16 = jnp.bfloat16


class Place:
    def __init__(self):
        r = lax.axis_index("row")
        c = lax.axis_index("col")
        self.zh, self.y = r // 4, r % 4
        self.zl, self.x, self.core = c // 8, (c // 2) % 4, c % 2
        self.z = 2 * self.zh + self.zl

    def at(self, x=None, y=None, z=None, core=None):
        x = self.x if x is None else x
        y = self.y if y is None else y
        z = self.z if z is None else z
        core = self.core if core is None else core
        return ((z // 2) * 4 + y, ((z % 2) * 4 + x) * 2 + core)


def remote(src, dst, send, recv, device):
    return pltpu.make_async_remote_copy(
        src_ref=src, dst_ref=dst, send_sem=send, recv_sem=recv, device_id=device, device_id_type=MESH
    )


def greet(devices):
    barrier = pltpu.get_barrier_semaphore()
    for device in devices:
        pl.semaphore_signal(barrier, inc=1, device_id=device, device_id_type=MESH)
    pl.semaphore_wait(barrier, len(devices))


def ranks_kernel(
    adj, first, mask, feat, out, keys, panel, r1, r2, acc, staged, mrows,
    loc_sem, a_send, a_recv, on_send, on_recv, i_send, i_recv, m_send, m_recv,
    y_send, y_recv, s_send, s_recv, f_send, f_recv, o_send, o_recv,
):
    me = Place()
    x, y, z, zh, zl, core = me.x, me.y, me.z, me.zh, me.zl, me.core
    sibling = me.at(core=1 - core)
    far = (z + 2) % 4
    ring = {
        "x+": me.at(x=(x + 1) % 4), "x-": me.at(x=(x + 3) % 4),
        "y+": me.at(y=(y + 1) % 4), "y-": me.at(y=(y + 3) % 4),
        "z+": me.at(z=(z + 1) % 4), "z-": me.at(z=(z + 3) % 4),
    }
    turned = (zl * 4 + x, (zh * 4 + y) * 2 + core)
    turned_self = (zl == zh) & (x == y)
    friends = [sibling, *ring.values(), me.at(z=far, core=0), me.at(z=far, core=1)]
    barrier = pltpu.get_barrier_semaphore()
    for device in friends:
        pl.semaphore_signal(barrier, inc=1, device_id=device, device_id_type=MESH)

    @pl.when(jnp.logical_not(turned_self))
    def _():
        pl.semaphore_signal(barrier, inc=1, device_id=turned, device_id_type=MESH)

    pl.semaphore_wait(barrier, len(friends) + jnp.where(turned_self, 0, 1))

    sends = []

    def own(who):
        return panel.at[:, z, pl.ds(x * 3, 3), :, pl.ds(pl.multiple_of(who * 128, 128), 128)]

    here = pltpu.make_async_copy(adj.at[pl.ds(core * 12, 12)], own(core), loc_sem.at[0])
    here.start()
    over = remote(adj.at[pl.ds((1 - core) * 12, 12)], own(core), on_send.at[0], on_recv.at[0], sibling)
    over.start()
    sends.append(over)

    goal = 2 * core + zl
    for half in range(2):
        is_self = (core == zh) & (core == half)

        @pl.when(is_self)
        def _(half=half):
            pltpu.make_async_copy(first.at[half], r1.at[y, zh, :, half], i_recv.at[zh]).start()
            pltpu.make_async_copy(mask, mrows.at[zh], m_recv.at[zh]).start()

        @pl.when(jnp.logical_not(is_self))
        def _(half=half):
            target = me.at(z=goal, core=half)
            remote(first.at[half], r1.at[y, zh, :, half], i_send.at[half], i_recv.at[zh], target).start()
            remote(mask, mrows.at[zh], m_send.at[half], m_recv.at[zh], target).start()

    def key_half(who):
        return keys.at[pl.ds(pl.multiple_of(who * HALF, HALF), HALF)]

    my_rows = feat.at[pl.ds(pl.multiple_of(core * HALF, HALF), HALF)]

    @pl.when(turned_self)
    def _():
        pltpu.make_async_copy(my_rows, key_half(core), f_recv.at[0]).start()

    @pl.when(jnp.logical_not(turned_self))
    def _():
        remote(my_rows, key_half(core), f_send.at[0], f_recv.at[0], turned).start()

    here.wait()
    over.wait_recv()

    def a_step(q, cls, stage, arriving):
        sign = 1 if cls % 2 == 0 else -1
        mark = "+" if sign == 1 else "-"
        x_first = cls < 2
        short = stage < 3
        step = stage % 3
        along_x = x_first == short
        device = ring[("x" if along_x else "z") + mark]
        qc = q * CLS + cls

        def region(hop):
            if along_x:
                at_x = (x - sign * hop + 8) % 4
                if short:
                    return panel.at[qc, z, pl.ds(at_x * 3, 3)]
                return panel.at[qc, :, pl.ds(at_x * 3, 3)]
            at_z = (z - sign * hop + 8) % 4
            if short:
                return panel.at[qc, at_z, pl.ds(x * 3, 3)]
            return panel.at[qc, at_z]

        n = (q * CLS + cls) * 6 + stage
        ref = region(step + 1 if arriving else step)
        return remote(ref, ref, a_send.at[n], a_recv.at[n], device)

    def a_stage(q, stage):
        for cls in range(CLS):
            if stage > 0:
                a_step(q, cls, stage - 1, True).wait_recv()
            if stage < 6:
                send = a_step(q, cls, stage, False)
                send.start()
                sends.append(send)

    def y_step(base, cut, a, step, arriving):
        sign = 1 if a == 0 else -1
        n = base * 6 + a * 3 + step
        ref = cut((y - sign * (step + 1 if arriving else step) + 8) % 4, a, core)
        return remote(ref, ref, y_send.at[n], y_recv.at[n], ring["y+" if a == 0 else "y-"])

    def y_share(base, cut, a, step, arriving):
        sign = 1 if a == 0 else -1
        n = base * 8 + a * 4 + step
        ref = cut((y - sign * step + 8) % 4, a, 1 - core if arriving else core)
        return remote(ref, ref, s_send.at[n], s_recv.at[n], sibling)

    def y_stage(base, cut, step):
        for a in range(2):
            if step > 0:
                y_step(base, cut, a, step - 1, True).wait_recv()
            go = [y_step(base, cut, a, step, False)] if step < 3 else []
            for send in go + [y_share(base, cut, a, step, False)]:
                send.start()
                sends.append(send)

    def y_done(base, cut):
        for a in range(2):
            for step in range(4):
                y_share(base, cut, a, step, True).wait_recv()

    def cut1(at_y, a, who):
        return r1.at[at_y, a, :, who]

    def cut2(q):
        return lambda at_y, a, who: r2.at[at_y, a, q, who]

    def lhs(q, m, h, kc):
        top = panel[pl.ds(q * CLS, CLS), h, m * 3 + kc].reshape(BLK, 256)
        low = panel[pl.ds(q * CLS, CLS), 2 + h, m * 3 + kc].reshape(BLK, 256)
        return jnp.concatenate([top, low], axis=0)

    def diag(a, q):
        row = lax.broadcasted_iota(jnp.int32, (BLK, HALF), 0) + q * BLK
        col = lax.broadcasted_iota(jnp.int32, (BLK, HALF), 1)
        own_block = (zl == a) & (y == x) & (core == zh)
        return jnp.where((row == col) & own_block, F32(0.15), F32(0.0))

    def keep_row(a, q):
        return mrows[a, pl.ds(core * 3 + q, 1), :] > 0.5

    def sweep_one(q):
        def body(m, total):
            for h in range(2):
                for kc in range(3):
                    rhs = r1[m, h, kc].reshape(256, HALF)
                    total = total + jnp.dot(lhs(q, m, h, kc), rhs, preferred_element_type=F32)
            return total

        total = lax.fori_loop(0, 4, body, jnp.zeros((2 * BLK, HALF), F32))
        for a in range(2):
            value = diag(a, q) + 0.85 * total[a * BLK:(a + 1) * BLK]
            r2[y, a, q, core] = jnp.where(keep_row(a, q), value, 0.0).astype(BF16)

    def sweep_two(rows, kc, start):
        def body(m, _):
            for q in rows:
                total = None
                for h in range(2):
                    part = jnp.dot(lhs(q, m, h, kc), r2[m, h, kc].reshape(256, HALF), preferred_element_type=F32)
                    total = part if total is None else total + part
                acc[q] = acc[q] + total
            return 0

        if start:
            for q in rows:
                acc[q] = jnp.zeros((2 * BLK, HALF), F32)
        lax.fori_loop(0, 4, body, 0)

    events = []
    order = 0

    def plan(when, what):
        nonlocal order
        events.append((when, order, what))
        order += 1

    def start_ranks():
        for a in range(2):
            pltpu.make_async_copy(first.at[0], r1.at[y, a, :, core], i_recv.at[a]).wait()
        y_stage(0, cut1, 0)

    def share_keys():
        pltpu.make_async_copy(my_rows, key_half(core), f_recv.at[0]).wait()
        share = remote(key_half(core), key_half(core), f_send.at[1], f_recv.at[1], sibling)
        share.start()
        sends.append(share)

    plan(4.0, start_ranks)
    for step in range(1, 4):
        plan(4.0 + 7.0 * step, lambda step=step: y_stage(0, cut1, step))
    plan(20.0, share_keys)
    for q in range(QC):
        base = 3.0 + 14.0 * q
        for stage in range(7):
            when = base + (2.6 * stage if stage < 3 else 8.0 + 5.0 * (stage - 3))
            plan(when, lambda q=q, stage=stage: a_stage(q, stage))
        full = base + 23.0

        def first_sweep(q=q):
            if q == 0:
                y_done(0, cut1)
                for a in range(2):
                    pltpu.make_async_copy(mask, mrows.at[a], m_recv.at[a]).wait()
            sweep_one(q)
            y_stage(1 + q, cut2(q), 0)

        plan(max(full, 26.0) + 0.1, first_sweep)
        for step in range(1, 4):
            plan(full + 1.5 + 3.6 * step, lambda q=q, step=step: y_stage(1 + q, cut2(q), step))
        plan(full + 12.5, lambda q=q: y_done(1 + q, cut2(q)))
        if q == 0:
            plan(full + 14.2, lambda: sweep_two((0, 1), 0, True))
        if q == 1:
            plan(full + 14.2, lambda: sweep_two((2,), 0, True))
            plan(full + 14.3, lambda: sweep_two((0, 1, 2), 1, False))
        if q == 2:
            plan(full + 14.2, lambda: sweep_two((0, 1, 2), 2, False))
    for _, _, what in sorted(events, key=lambda e: e[:2]):
        what()

    for q in range(QC):
        for a in range(2):
            value = diag(a, q) + 0.85 * acc[q, a * BLK:(a + 1) * BLK]
            staged[a, q] = jnp.where(keep_row(a, q), value, F32(BIG)).astype(BF16)
    mine = pltpu.make_async_copy(staged.at[zh], out.at[zh], loc_sem.at[1])
    mine.start()
    swap = remote(staged.at[1 - zh], out.at[zh], o_send.at[0], o_recv.at[0], me.at(z=far))
    swap.start()
    mine.wait()
    swap.wait_recv()
    swap.wait_send()
    remote(key_half(1 - core), key_half(1 - core), f_send.at[1], f_recv.at[1], sibling).wait_recv()
    for send in sends:
        send.wait_send()
    for half in range(2):
        @pl.when(jnp.logical_not((core == zh) & (core == half)))
        def _(half=half):
            target = me.at(z=goal, core=half)
            remote(first.at[half], r1.at[y, zh, :, half], i_send.at[half], i_recv.at[zh], target).wait_send()
            remote(mask, mrows.at[zh], m_send.at[half], m_recv.at[zh], target).wait_send()

    @pl.when(jnp.logical_not(turned_self))
    def _():
        remote(my_rows, key_half(core), f_send.at[0], f_recv.at[0], turned).wait_send()


def ranks_call(adj, first, mask, feat):
    dma = pltpu.SemaphoreType.DMA
    anywhere = pl.BlockSpec(memory_space=pl.ANY)
    vmem = pl.BlockSpec(memory_space=pltpu.VMEM)
    return pl.pallas_call(
        ranks_kernel,
        name="ranks",
        out_shape=(
            jax.ShapeDtypeStruct((2, QC, BLK, HALF), BF16),
            jax.ShapeDtypeStruct((ROWS, D), BF16),
        ),
        in_specs=[anywhere] * 4,
        out_specs=(vmem, vmem),
        scratch_shapes=[
            pltpu.VMEM((QC * CLS, 4, 12, PIECE, 256), BF16),
            pltpu.VMEM((4, 2, 3, 2, BLK, HALF), BF16),
            pltpu.VMEM((4, 2, 3, 2, BLK, HALF), BF16),
            pltpu.VMEM((QC, 2 * BLK, HALF), F32),
            pltpu.VMEM((2, QC, BLK, HALF), BF16),
            pltpu.VMEM((2, 8, HALF), F32),
            dma((2,)),
            dma((QC * CLS * 6,)), dma((QC * CLS * 6,)),
            dma((1,)), dma((1,)),
            dma((2,)), dma((2,)),
            dma((2,)), dma((2,)),
            dma((24,)), dma((24,)),
            dma((32,)), dma((32,)),
            dma((2,)), dma((2,)),
            dma((1,)), dma((1,)),
        ],
        compiler_params=pltpu.CompilerParams(
            collective_id=0, has_side_effects=True, vmem_limit_bytes=48 * 1024 * 1024
        ),
    )(adj, first, mask, feat)


def attend_kernel(
    ranks, query, keys_t, values, w_out, gain, rate, out,
    bias_in, hide, numer, numer_all, stats, stats_all, att, att_all, w_both, mix,
    n_send, n_recv, t_send, t_recv, g_send, g_recv, w_send, w_recv, x_send, x_recv,
):
    me = Place()
    core = me.core
    sibling = me.at(core=1 - core)
    spot = me.zl * 4 + me.x

    def chip(k):
        other = (spot + k) % 8
        return other, me.at(x=other % 4, z=2 * me.zh + other // 4)

    greet([sibling] + [chip(k)[1] for k in range(1, 8)])
    sends = []
    w_copy = remote(w_out, w_both, w_send, w_recv, sibling)
    w_copy.start()
    sends.append(w_copy)

    for half in range(2):
        for q in range(QC):
            value = ranks[half, q].astype(F32)
            rows, cols = pl.ds(q * BLK, BLK), pl.ds(half * HALF, HALF)
            bias_in[rows, cols] = value * math.sqrt(NODES)
            hide[rows, cols] = jnp.where(value < 1e20, F32(0.0), F32(-BIG))

    lane = lax.broadcasted_iota(jnp.int32, (BLK, BLK), 1)

    def block(pair, row):
        cols = pl.ds(pl.multiple_of(pair * BLK, BLK), BLK)
        rows = pl.ds(pl.multiple_of(row * BLK, BLK), BLK)
        q2 = query[rows, cols]
        k2 = keys_t[cols, :]
        v2 = values[:, cols]
        spread = bias_in[rows, :]
        away = hide[rows, :]
        both = []
        kept = stats[rows, :]
        for side in range(2):
            head = pair * 2 + side
            q1 = jnp.where(lane // HDIM == side, q2, jnp.zeros_like(q2))
            s = jnp.dot(q1, k2, preferred_element_type=F32) * F32(LOG2E / math.sqrt(HDIM)) + away
            top = jnp.maximum(jnp.max(s, axis=1, keepdims=True), F32(-1e29))
            bias = (gain[head] * F32(LOG2E)) * jnp.tanh(spread * rate[head])
            e = jnp.exp2((s - top) + bias)
            total = jnp.sum(e, axis=1, keepdims=True)
            both.append(jnp.dot(e.astype(BF16), v2, preferred_element_type=F32))
            kept = jnp.where(lane == head, total, jnp.where(lane == HEADS + head, top, kept))
        stats[rows, :] = kept
        numer[rows, cols] = jnp.where(lane < HDIM, both[0], both[1]).astype(BF16)

    stats[...] = jnp.zeros_like(stats)

    def part(ref, row, g):
        return ref.at[pl.ds(pl.multiple_of(row * 48, 16), 48), pl.ds(g * 256, 256)]

    for g in range(4):
        def body(t, _, g=g):
            block(g * 2 + t // QC, t % QC)
            return 0

        lax.fori_loop(0, 2 * QC, body, 0)
        for k in range(1, 8):
            other, device = chip(k)
            n = g * 8 + k
            copy = remote(
                part(numer, other, g), numer_all.at[spot, :, pl.ds(g * 256, 256)],
                n_send.at[n], n_recv.at[n], device,
            )
            copy.start()
            sends.append(copy)
    for k in range(1, 8):
        other, device = chip(k)
        copy = remote(
            stats.at[pl.ds(pl.multiple_of(other * 48, 16), 48)], stats_all.at[spot],
            t_send.at[k], t_recv.at[k], device,
        )
        copy.start()
        sends.append(copy)

    own_rows = pl.ds(pl.multiple_of(spot * 48, 16), 48)
    stats_all[spot] = stats[own_rows, :]
    numer_all[spot] = numer[own_rows, :]
    for k in range(1, 8):
        source = (spot + 8 - k) % 8
        remote(stats_all.at[source], stats_all.at[source], t_send.at[k], t_recv.at[k], sibling).wait_recv()
        for g in range(4):
            ref = numer_all.at[source, :, pl.ds(g * 256, 256)]
            remote(ref, ref, n_send.at[g * 8 + k], n_recv.at[g * 8 + k], sibling).wait_recv()

    table = [stats_all[s] for s in range(8)]
    tops = [t[:, HEADS:2 * HEADS] for t in table]
    peak = tops[0]
    for t in tops[1:]:
        peak = jnp.maximum(peak, t)
    weights = [jnp.exp2(t - peak) for t in tops]
    total = weights[0] * table[0][:, :HEADS]
    for s in range(1, 8):
        total = total + weights[s] * table[s][:, :HEADS]
    weights = [w / total for w in weights]
    for pair in range(HEADS // 2):
        cols = pl.ds(pair * BLK, BLK)
        low = lax.broadcasted_iota(jnp.int32, (48, BLK), 1) < HDIM
        value = jnp.zeros((48, BLK), F32)
        for s in range(8):
            w = jnp.where(low, weights[s][:, 2 * pair:2 * pair + 1], weights[s][:, 2 * pair + 1:2 * pair + 2])
            value = value + w * numer_all[s, :, cols].astype(F32)
        att[:, cols] = value.astype(BF16)

    for k in range(1, 8):
        _, device = chip(k)
        copy = remote(att, att_all.at[spot], g_send.at[k], g_recv.at[k], device)
        copy.start()
        sends.append(copy)
    att_all[spot] = att[...]
    for k in range(1, 8):
        ref = att_all.at[(spot + 8 - k) % 8]
        remote(ref, ref, g_send.at[k], g_recv.at[k], sibling).wait_recv()
    w_copy.wait_recv()
    gathered = att_all[...].reshape(HALF, D)
    mix[...] = jnp.dot(gathered, w_both[...], preferred_element_type=F32).astype(BF16)
    there = remote(mix, out.at[core], x_send, x_recv, sibling)
    there.start()
    sends.append(there)
    out[core] = jnp.dot(gathered, w_out[...], preferred_element_type=F32).astype(BF16)
    remote(mix, out.at[1 - core], x_send, x_recv, sibling).wait_recv()
    for send in sends:
        send.wait_send()


def attend_call(ranks, query, keys_t, values, w_out, gain, rate):
    dma = pltpu.SemaphoreType.DMA
    vmem = pl.BlockSpec(memory_space=pltpu.VMEM)
    smem = pl.BlockSpec(memory_space=pltpu.SMEM)
    return pl.pallas_call(
        attend_kernel,
        name="attend",
        out_shape=jax.ShapeDtypeStruct((2, HALF, HDIM), BF16),
        in_specs=[vmem] * 5 + [smem] * 2,
        out_specs=vmem,
        scratch_shapes=[
            pltpu.VMEM((HALF, ROWS), F32),
            pltpu.VMEM((HALF, ROWS), F32),
            pltpu.VMEM((HALF, D), BF16),
            pltpu.VMEM((8, 48, D), BF16),
            pltpu.VMEM((HALF, BLK), F32),
            pltpu.VMEM((8, 48, BLK), F32),
            pltpu.VMEM((48, D), BF16),
            pltpu.VMEM((8, 48, D), BF16),
            pltpu.VMEM((D, HDIM), BF16),
            pltpu.VMEM((HALF, HDIM), BF16),
            dma((32,)), dma((32,)),
            dma((8,)), dma((8,)),
            dma((8,)), dma((8,)),
            dma, dma,
            dma, dma,
        ],
        compiler_params=pltpu.CompilerParams(
            collective_id=1, has_side_effects=True, vmem_limit_bytes=48 * 1024 * 1024
        ),
    )(ranks, query, keys_t, values, w_out, gain, rate)


def prepare(edge_weight, pattern):
    rows_here, cols_here = edge_weight.shape
    blocks = pattern > 0
    grid = jnp.broadcast_to(blocks[:, None, :, None], (rows_here // BLK, BLK, cols_here // BLK, BLK))
    keep = grid.reshape(rows_here, cols_here)
    adjacency = jnp.where(keep, edge_weight, jnp.zeros_like(edge_weight))
    row_ids = lax.axis_index("row") * rows_here + lax.iota(jnp.int32, rows_here)
    col_ids = lax.axis_index("col") * cols_here + lax.iota(jnp.int32, cols_here)
    identity = (row_ids[:, None] == col_ids[None, :]).astype(F32)
    first = jnp.where(keep, 0.15 * identity + 0.1275 * adjacency.astype(F32), F32(0.0)).astype(BF16)
    panel = adjacency.reshape(2 * QC * CLS, PIECE, 3, BLK).transpose(0, 2, 1, 3)
    mask = jnp.broadcast_to(blocks[:, :, None], (6, 3, BLK)).reshape(6, cols_here).astype(F32)
    return panel, first.reshape(2, QC, BLK, cols_here), jnp.pad(mask, ((0, 2), (0, 0)))


def shards(node_features, edge_weight, pattern, w_qkv, w_out, bias_gain, bias_rate):
    panel, first, mask = prepare(edge_weight, pattern)
    ranks, keys = ranks_call(panel, first, mask, node_features)
    core = lax.axis_index("col") % 2
    mine = lax.dynamic_slice_in_dim(node_features, core * HALF, HALF, 0)
    query = jnp.dot(mine, w_qkv[:, :D], preferred_element_type=F32).astype(BF16)
    keys_t = lax.dot_general(
        w_qkv[:, D:2 * D], keys, (((0,), (1,)), ((), ())), preferred_element_type=F32
    ).astype(BF16)
    values = jnp.dot(keys, w_qkv[:, 2 * D:], preferred_element_type=F32).astype(BF16)
    mixed = attend_call(ranks, query, keys_t, values, w_out, bias_gain, bias_rate)
    return mixed.reshape(2 * HALF, HDIM)


def solution(mesh):
    in_specs = (P("row", None), P("row", "col"), P("row", "col"), P(), P(None, "col"), P(), P())
    return jax.shard_map(shards, mesh=mesh, in_specs=in_specs, out_specs=P("row", "col"), check_vma=False)
```

```python
import math

import jax
import jax.numpy as jnp
from jax import lax
from jax.experimental import pallas as pl
from jax.experimental.pallas import tpu as pltpu
from jax.sharding import PartitionSpec as P

D = 1024
HEADS = 16
BLK = 128
HDIM = 64
NODES = 6144
ROWS = 768
HALF = 384
QC = 3
CHUNKS = 6
CLS = 4
PIECE = 16
KEYROWS = 48
LOG2E = 1.4426950408889634
BIG = 1e30
MESH = pl.DeviceIdType.MESH
F32 = jnp.float32
BF16 = jnp.bfloat16


class Place:
    def __init__(self):
        r = lax.axis_index("row")
        c = lax.axis_index("col")
        self.zh, self.y = r // 4, r % 4
        self.zl, self.x, self.core = c // 8, (c // 2) % 4, c % 2
        self.z = 2 * self.zh + self.zl

    def at(self, x=None, y=None, z=None, core=None):
        x = self.x if x is None else x
        y = self.y if y is None else y
        z = self.z if z is None else z
        core = self.core if core is None else core
        return ((z // 2) * 4 + y, ((z % 2) * 4 + x) * 2 + core)


def remote(src, dst, send, recv, device):
    return pltpu.make_async_remote_copy(
        src_ref=src, dst_ref=dst, send_sem=send, recv_sem=recv, device_id=device, device_id_type=MESH
    )


def fused_kernel(
    edge, pattern, feat, w_qkv, w_out_t, gain, rate, out,
    panel, r1, r2, acc, staged, landed, adj, first, mrows, mboth, keys, own_feat, w_all, edge_v,
    query, key_proj, value_proj, scores, bias_in, numer, numer_all, stats, stats_all, att, w_cols, mix,
    loc_sem, a_send, a_recv, on_send, on_recv, i_send, i_recv, m_send, m_recv,
    y_send, y_recv, s_send, s_recv, f_send, f_recv, o_send, o_recv,
    n_send, n_recv, t_send, t_recv, w_send, w_recv, x_send, x_recv,
):
    me = Place()
    x, y, z, zh, zl, core = me.x, me.y, me.z, me.zh, me.zl, me.core
    sibling = me.at(core=1 - core)
    far = (z + 2) % 4
    spot = zl * 4 + x
    ring = {
        "x+": me.at(x=(x + 1) % 4), "x-": me.at(x=(x + 3) % 4),
        "z+": me.at(z=(z + 1) % 4), "z-": me.at(z=(z + 3) % 4),
    }
    turned = (zl * 4 + x, (zh * 4 + y) * 2 + core)
    turned_self = (zl == zh) & (x == y)

    def chip(k, who=None):
        other = (spot + k) % 8
        return other, me.at(x=other % 4, z=2 * zh + other // 4, core=who)

    def y_peer(k):
        return me.at(y=(y + k) % 4)

    friends = [sibling, me.at(z=(z + 2 * zl + 3) % 4), me.at(z=far, core=0), me.at(z=far, core=1)]
    friends += [y_peer(k) for k in (1, 2, 3)]
    friends += [chip(k, who)[1] for k in range(1, 8) for who in (core, 1 - core)]
    barrier = pltpu.get_barrier_semaphore()
    for device in friends:
        pl.semaphore_signal(barrier, inc=1, device_id=device, device_id_type=MESH)

    @pl.when(jnp.logical_not(turned_self))
    def _():
        pl.semaphore_signal(barrier, inc=1, device_id=turned, device_id_type=MESH)

    sends = []

    def go(copy):
        copy.start()
        sends.append(copy)

    loads = {
        "edge": pltpu.make_async_copy(edge, edge_v, loc_sem.at[0]),
        "feat": pltpu.make_async_copy(
            feat.at[pl.ds(pl.multiple_of(core * HALF, HALF), HALF)], own_feat, loc_sem.at[1]
        ),
        "w": pltpu.make_async_copy(w_qkv, w_all, loc_sem.at[2]),
    }
    for load in loads.values():
        load.start()
    loads["edge"].wait()

    same = (zl * 4 + x == zh * 4 + y)
    for rb in range(6):
        for cb in range(3):
            on = jnp.where(pattern[rb, cb] > 0, F32(1.0), F32(0.0))
            kept = edge_v[pl.ds(rb * BLK, BLK), pl.ds(cb * BLK, BLK)] * on.astype(BF16)
            adj[pl.ds(rb * 8, 8), cb] = kept.reshape(8, PIECE, BLK)
            row = lax.broadcasted_iota(jnp.int32, (BLK, BLK), 0) + rb * BLK
            col = lax.broadcasted_iota(jnp.int32, (BLK, BLK), 1) + cb * BLK + core * HALF
            diagonal = jnp.where((row == col) & same, F32(0.15), F32(0.0))
            value = (diagonal + F32(0.1275) * kept.astype(F32)) * on
            first[rb // 3, rb % 3, :, pl.ds(cb * BLK, BLK)] = value.astype(BF16)
            mboth[core, pl.ds(rb, 1), pl.ds(cb * BLK, BLK)] = jnp.full((1, BLK), on, F32)
    mask = mboth.at[core]

    pl.semaphore_wait(barrier, len(friends) + jnp.where(turned_self, 0, 1))

    def own(who):
        return panel.at[:, z, pl.ds(x * 3, 3), :, pl.ds(pl.multiple_of(who * 128, 128), 128)]

    rows24 = CHUNKS * CLS
    here = pltpu.make_async_copy(adj.at[pl.ds(core * rows24, rows24)], own(core), loc_sem.at[3])
    here.start()
    over = remote(adj.at[pl.ds((1 - core) * rows24, rows24)], own(core), on_send.at[0], on_recv.at[0], sibling)
    go(over)

    goal = 2 * core + zl
    for half in range(2):
        is_self = (core == zh) & (core == half)

        @pl.when(is_self)
        def _(half=half):
            pltpu.make_async_copy(first.at[half], r1.at[y, zh, :, half], i_recv.at[zh]).start()
            pltpu.make_async_copy(mask, mrows.at[zh], m_recv.at[zh]).start()

        @pl.when(jnp.logical_not(is_self))
        def _(half=half):
            target = me.at(z=goal, core=half)
            remote(first.at[half], r1.at[y, zh, :, half], i_send.at[half], i_recv.at[zh], target).start()
            remote(mask, mrows.at[zh], m_send.at[half], m_recv.at[zh], target).start()

    go(remote(mask, mask, on_send.at[1], on_recv.at[1], sibling))

    mine = pl.ds(pl.multiple_of(spot * 2 * KEYROWS + core * KEYROWS, KEYROWS), KEYROWS)

    @pl.when(turned_self)
    def _():
        pltpu.make_async_copy(feat.at[mine], keys.at[zh, y, core], f_recv.at[0]).start()

    @pl.when(jnp.logical_not(turned_self))
    def _():
        remote(feat.at[mine], keys.at[zl, x, core], f_send.at[0], f_recv.at[0], turned).start()

    here.wait()
    over.wait_recv()

    def a_copy(j, cls, leg, kind, arriving):
        sign = 1 if cls % 2 == 0 else -1
        along_x = (cls < 2) == (leg == 0)
        head = sign if kind != 1 else -sign
        device = ring[("x" if along_x else "z") + ("+" if head == 1 else "-")]
        hop = {0: 0, 1: 0, 2: -sign}[kind] - (head if arriving else 0)
        jc = j * CLS + cls
        if along_x:
            at_x = (x + hop + 8) % 4
            cols = pl.ds(at_x * 3, 3)
            ref = panel.at[jc, z, cols] if leg == 0 else panel.at[jc, :, cols]
        else:
            at_z = (z + hop + 8) % 4
            ref = panel.at[jc, at_z, pl.ds(x * 3, 3)] if leg == 0 else panel.at[jc, at_z]
        n = jc * 6 + leg * 3 + kind
        return remote(ref, ref, a_send.at[n], a_recv.at[n], device)

    def a_stage(j, stage):
        for cls in range(CLS):
            if stage in (1, 3):
                leg = stage // 2
                a_copy(j, cls, leg, 0, True).wait_recv()
                go(a_copy(j, cls, leg, 2, False))
            else:
                if stage > 0:
                    a_copy(j, cls, stage // 2 - 1, 1, True).wait_recv()
                    a_copy(j, cls, stage // 2 - 1, 2, True).wait_recv()
                if stage < 4:
                    go(a_copy(j, cls, stage // 2, 0, False))
                    go(a_copy(j, cls, stage // 2, 1, False))

    def y_copy(base, cut, k, arriving):
        ref = cut((y - k + 4) % 4 if arriving else y, core)
        n = base * 3 + k - 1
        return remote(ref, ref, y_send.at[n], y_recv.at[n], y_peer(k))

    def y_share(base, cut, k, arriving):
        ref = cut((y - k + 4) % 4, 1 - core if arriving else core)
        n = base * 4 + k
        return remote(ref, ref, s_send.at[n], s_recv.at[n], sibling)

    def y_begin(base, cut):
        for k in (1, 3, 2):
            go(y_copy(base, cut, k, False))
        go(y_share(base, cut, 0, False))

    def y_pass(base, cut, k):
        y_copy(base, cut, k, True).wait_recv()
        go(y_share(base, cut, k, False))

    def y_done(base, cut):
        for k in range(4):
            y_share(base, cut, k, True).wait_recv()

    def cut1(at_y, who):
        return r1.at[at_y, :, :, who]

    def cut2(q):
        return lambda at_y, who: r2.at[at_y, :, q, who]

    def cutk(at_y, who):
        return keys.at[:, at_y, who]

    def lhs(q, m, h, kc):
        top = panel[pl.ds(q * 8, 8), h, m * 3 + kc].reshape(BLK, 256)
        low = panel[pl.ds(q * 8, 8), 2 + h, m * 3 + kc].reshape(BLK, 256)
        return jnp.concatenate([top, low], axis=0)

    def diag(a, q):
        row = lax.broadcasted_iota(jnp.int32, (BLK, HALF), 0) + q * BLK
        col = lax.broadcasted_iota(jnp.int32, (BLK, HALF), 1)
        own_block = (zl == a) & (y == x) & (core == zh)
        return jnp.where((row == col) & own_block, F32(0.15), F32(0.0))

    def masked_ranks(a, q, total):
        keep = mrows[a, pl.ds(core * 3 + q, 1), :] > 0.5
        return jnp.where(keep, diag(a, q) + 0.85 * total, 0.0).astype(BF16)

    def sweep_one(q):
        def body(m, total):
            for h in range(2):
                for kc in range(3):
                    rhs = r1[m, h, kc].reshape(256, HALF)
                    total = total + jnp.dot(lhs(q, m, h, kc), rhs, preferred_element_type=F32)
            return total

        total = lax.fori_loop(0, 4, body, jnp.zeros((2 * BLK, HALF), F32))
        for a in range(2):
            r2[y, a, q, core] = masked_ranks(a, q, total[a * BLK:(a + 1) * BLK])

    def sweep_two(rows, kc, start):
        def body(m, _):
            for q in rows:
                total = None
                for h in range(2):
                    part = jnp.dot(lhs(q, m, h, kc), r2[m, h, kc].reshape(256, HALF), preferred_element_type=F32)
                    total = part if total is None else total + part
                acc[q] = acc[q] + total
            return 0

        if start:
            for q in rows:
                acc[q] = jnp.zeros((2 * BLK, HALF), F32)
        lax.fori_loop(0, 4, body, 0)

    def project(dst, src, first_col, n):
        def body(t, _):
            cols = pl.ds(pl.multiple_of(t * 256, 256), 256)
            w = w_all[:, pl.ds(pl.multiple_of(first_col + t * 256, 256), 256)]
            dst[:, cols] = jnp.dot(src, w, preferred_element_type=F32).astype(BF16)
            return 0

        lax.fori_loop(n, n + 1, body, 0)

    lane = lax.broadcasted_iota(jnp.int32, (BLK, BLK), 1)

    def score_block(t):
        pair, row = t // QC, t % QC
        cols = pl.ds(pl.multiple_of(pair * BLK, BLK), BLK)
        rows = pl.ds(pl.multiple_of(row * BLK, BLK), BLK)
        q2 = query[rows, cols]
        k2 = key_proj[:, cols]
        away = [jnp.where(mboth[c, pl.ds(core * 3 + row, 1), :] > 0.5, F32(0.0), F32(-BIG)) for c in range(2)]
        away = jnp.concatenate(away, axis=1)
        kept = stats[rows, :]
        for side in range(2):
            head = pair * 2 + side
            q1 = jnp.where(lane // HDIM == side, q2, jnp.zeros_like(q2))
            s = lax.dot_general(q1, k2, (((1,), (1,)), ((), ())), preferred_element_type=F32)
            s = s * F32(LOG2E / math.sqrt(HDIM)) + away
            top = jnp.maximum(jnp.max(s, axis=1, keepdims=True), F32(-1e29))
            scores[head, rows, :] = s - top
            kept = jnp.where(lane == HEADS + head, top, kept)
        stats[rows, :] = kept

    def score_blocks(low, high):
        def body(t, _):
            score_block(t)
            return 0

        lax.fori_loop(low, high, body, 0)

    def expo_block(t):
        pair, row = t // QC, t % QC
        cols = pl.ds(pl.multiple_of(pair * BLK, BLK), BLK)
        rows = pl.ds(pl.multiple_of(row * BLK, BLK), BLK)
        v2 = value_proj[:, cols]
        spread = bias_in[rows, :]
        both = []
        kept = stats[rows, :]
        for side in range(2):
            head = pair * 2 + side
            bias = (gain[head] * F32(LOG2E)) * jnp.tanh(spread * rate[head])
            e = jnp.exp2(scores[head, rows, :] + bias)
            kept = jnp.where(lane == head, jnp.sum(e, axis=1, keepdims=True), kept)
            both.append(jnp.dot(e.astype(BF16), v2, preferred_element_type=F32))
        stats[rows, :] = kept
        numer[rows, cols] = jnp.where(lane < HDIM, both[0], both[1]).astype(BF16)

    events = []

    def plan(when, what):
        events.append((when, len(events), what))

    def load_weights():
        loads["feat"].wait()
        loads["w"].wait()
        stats[...] = jnp.zeros_like(stats)

    def begin_ranks():
        for a in range(2):
            pltpu.make_async_copy(first.at[0], r1.at[y, a, :, core], i_recv.at[a]).wait()
        y_begin(0, cut1)

    def begin_keys():
        pltpu.make_async_copy(feat.at[mine], keys.at[zh, y, core], f_recv.at[0]).wait()
        ref = keys.at[zh, y, core]
        go(remote(ref, ref, f_send.at[1], f_recv.at[1], me.at(z=far)))

    def spread_keys():
        ref = keys.at[1 - zh, y, core]
        remote(ref, ref, f_send.at[1], f_recv.at[1], me.at(z=far)).wait_recv()
        y_begin(4, cutk)

    plan(7.0, load_weights)
    for n in range(4):
        plan(7.5 + 0.1 * n, lambda n=n: project(query, own_feat[...], 0, n))
    plan(9.0, begin_ranks)
    for k, when in ((1, 26.0), (3, 26.0), (2, 35.0)):
        plan(when, lambda k=k: y_pass(0, cut1, k))
    plan(10.0, begin_keys)
    plan(14.0, spread_keys)
    for k, when in ((1, 24.0), (3, 24.0), (2, 25.0)):
        plan(when, lambda k=k: y_pass(4, cutk, k))
    plan(27.0, lambda: y_done(4, cutk))
    for n in range(4):
        plan(27.5 + n, lambda n=n: project(key_proj, keys[...].reshape(ROWS, D), D, n))
        plan(31.5 + n, lambda n=n: project(value_proj, keys[...].reshape(ROWS, D), 2 * D, n))
    for j in range(CHUNKS):
        long = 13.0 + 7.9 * j
        for stage, when in enumerate((6.0 + 0.8 * j, 9.0 + 0.8 * j, long, long + 6.0, long + 13.0)):
            plan(when, lambda j=j, stage=stage: a_stage(j, stage))

    def ready():
        y_done(0, cut1)
        for a in range(2):
            pltpu.make_async_copy(mask, mrows.at[a], m_recv.at[a]).wait()

    plan(35.9, lambda: remote(mask, mboth.at[1 - core], on_send.at[1], on_recv.at[1], sibling).wait_recv())
    for n in range(8):
        plan(36.0 + 3.2 * n, lambda n=n: score_blocks(3 * n, 3 * n + 3))
    plan(38.4, ready)
    for q, when in enumerate((38.5, 50.0, 65.7)):
        def first_sweep(q=q):
            sweep_one(q)
            y_begin(1 + q, cut2(q))

        plan(when, first_sweep)
        for k, late in ((1, 5.0), (3, 5.0), (2, 6.0)):
            plan(when + late, lambda q=q, k=k: y_pass(1 + q, cut2(q), k))
        plan(when + 8.0, lambda q=q: y_done(1 + q, cut2(q)))
    plan(50.5, lambda: sweep_two((0, 1), 0, True))
    plan(59.0, lambda: sweep_two((0, 1), 1, False))
    plan(66.0, lambda: sweep_two((2,), 0, True))
    plan(66.1, lambda: sweep_two((2,), 1, False))
    plan(74.0, lambda: sweep_two((0, 1, 2), 2, False))

    def send_weights():
        for k in range(8):
            _, device = chip(k, 1 - core if k == 0 else None)
            go(remote(w_out_t, w_cols.at[spot, core], w_send.at[k], w_recv.at[k], device))
        pltpu.make_async_copy(w_out_t, w_cols.at[spot, core], loc_sem.at[4]).start()

    plan(66.2, send_weights)
    for _, _, what in sorted(events, key=lambda e: e[:2]):
        what()

    for a in range(2):
        for q in range(QC):
            staged[a, q] = masked_ranks(a, q, acc[q, a * BLK:(a + 1) * BLK])
    swap = remote(staged.at[1 - zh], landed, o_send.at[0], o_recv.at[0], me.at(z=far))
    go(swap)

    pltpu.make_async_copy(w_out_t, w_cols.at[spot, core], loc_sem.at[4]).wait()
    for k in range(1, 8):
        source = (spot + 8 - k) % 8
        ref = w_cols.at[source, core]
        remote(ref, ref, w_send.at[k], w_recv.at[k], sibling).wait_recv()
        go(remote(ref, ref, w_send.at[7 + k], w_recv.at[7 + k], sibling))

    def widen(ref, half):
        for q in range(QC):
            cols = pl.ds(pl.multiple_of(half * HALF, HALF), HALF)
            bias_in[pl.ds(q * BLK, BLK), cols] = ref[q].astype(F32) * F32(math.sqrt(NODES))

    widen(staged.at[zh], zh)
    swap.wait_recv()
    widen(landed, 1 - zh)

    def part(ref, row, g):
        return ref.at[pl.ds(pl.multiple_of(row * KEYROWS, KEYROWS), KEYROWS), pl.ds(g * 256, 256)]

    for g in range(4):
        def body(t, _, g=g):
            expo_block(g * 2 * QC + t)
            return 0

        lax.fori_loop(0, 2 * QC, body, 0)
        for k in range(1, 8):
            other, device = chip(k)
            n = g * 8 + k
            dst = numer_all.at[spot, :, pl.ds(g * 256, 256)]
            go(remote(part(numer, other, g), dst, n_send.at[n], n_recv.at[n], device))
    for k in range(1, 8):
        other, device = chip(k)
        rows = stats.at[pl.ds(pl.multiple_of(other * KEYROWS, KEYROWS), KEYROWS)]
        go(remote(rows, stats_all.at[spot], t_send.at[k], t_recv.at[k], device))

    own_rows = pl.ds(pl.multiple_of(spot * KEYROWS, KEYROWS), KEYROWS)
    stats_all[spot] = stats[own_rows, :]
    numer_all[spot] = numer[own_rows, :]
    for k in range(1, 8):
        source = (spot + 8 - k) % 8
        remote(stats_all.at[source], stats_all.at[source], t_send.at[k], t_recv.at[k], sibling).wait_recv()
        for g in range(4):
            ref = numer_all.at[source, :, pl.ds(g * 256, 256)]
            remote(ref, ref, n_send.at[g * 8 + k], n_recv.at[g * 8 + k], sibling).wait_recv()

    table = [stats_all[s] for s in range(8)]
    tops = [t[:, HEADS:2 * HEADS] for t in table]
    peak = tops[0]
    for t in tops[1:]:
        peak = jnp.maximum(peak, t)
    weights = [jnp.exp2(t - peak) for t in tops]
    total = weights[0] * table[0][:, :HEADS]
    for s in range(1, 8):
        total = total + weights[s] * table[s][:, :HEADS]
    weights = [w / total for w in weights]
    low = lax.broadcasted_iota(jnp.int32, (KEYROWS, BLK), 1) < HDIM
    for pair in range(HEADS // 2):
        cols = pl.ds(pair * BLK, BLK)
        value = jnp.zeros((KEYROWS, BLK), F32)
        for s in range(8):
            w = jnp.where(low, weights[s][:, 2 * pair:2 * pair + 1], weights[s][:, 2 * pair + 1:2 * pair + 2])
            value = value + w * numer_all[s, :, cols].astype(F32)
        att[:, cols] = value.astype(BF16)

    for k in range(8):
        ref = w_cols.at[(spot + 8 - k) % 8, 1 - core]
        n = 0 if k == 0 else 7 + k
        remote(ref, ref, w_send.at[n], w_recv.at[n], sibling).wait_recv()
    mixed = lax.dot_general(
        att[...], w_cols[...].reshape(D, D), (((1,), (1,)), ((), ())), preferred_element_type=F32
    ).astype(BF16)
    for c in range(2 * 8):
        mix[c // 2, c % 2] = mixed[:, c * HDIM:(c + 1) * HDIM]

    def rows_of(who, at):
        return out.at[pl.ds(pl.multiple_of(who * HALF + at * KEYROWS, KEYROWS), KEYROWS)]

    for k in range(8):
        for flip in range(2):
            if k == 0 and flip == 0:
                continue
            other, device = chip(k, (core + flip) % 2)
            n = k * 2 + flip
            go(remote(mix.at[other, (core + flip) % 2], rows_of(core, spot), x_send.at[n], x_recv.at[n], device))
    last = pltpu.make_async_copy(mix.at[spot, core], rows_of(core, spot), loc_sem.at[5])
    last.start()
    for k in range(8):
        for flip in range(2):
            if k == 0 and flip == 0:
                continue
            ref = rows_of((core + flip) % 2, (spot + 8 - k) % 8)
            remote(ref, ref, x_send.at[k * 2 + flip], x_recv.at[k * 2 + flip], sibling).wait_recv()
    last.wait()
    for send in sends:
        send.wait_send()
    for half in range(2):
        @pl.when(jnp.logical_not((core == zh) & (core == half)))
        def _(half=half):
            target = me.at(z=goal, core=half)
            remote(first.at[half], r1.at[y, zh, :, half], i_send.at[half], i_recv.at[zh], target).wait_send()
            remote(mask, mrows.at[zh], m_send.at[half], m_recv.at[zh], target).wait_send()

    @pl.when(jnp.logical_not(turned_self))
    def _():
        remote(feat.at[mine], keys.at[zl, x, core], f_send.at[0], f_recv.at[0], turned).wait_send()


def shards(node_features, edge_weight, pattern, w_qkv, w_out, bias_gain, bias_rate):
    dma = pltpu.SemaphoreType.DMA
    anywhere = pl.BlockSpec(memory_space=pl.ANY)
    vmem = pl.BlockSpec(memory_space=pltpu.VMEM)
    smem = pl.BlockSpec(memory_space=pltpu.SMEM)
    pairs = [6 * CHUNKS * CLS, 2, 2, 2, 15, 20, 2, 1, 32, 8, 15, 16]
    sems = [dma((n,)) for n in pairs for _ in range(2)]
    return pl.pallas_call(
        fused_kernel,
        name="fused",
        out_shape=jax.ShapeDtypeStruct((ROWS, HDIM), BF16),
        in_specs=[anywhere, smem, anywhere, anywhere, anywhere, smem, smem],
        out_specs=vmem,
        scratch_shapes=[
            pltpu.VMEM((CHUNKS * CLS, 4, 12, PIECE, 256), BF16),
            pltpu.VMEM((4, 2, QC, 2, BLK, HALF), BF16),
            pltpu.VMEM((4, 2, QC, 2, BLK, HALF), BF16),
            pltpu.VMEM((QC, 2 * BLK, HALF), F32),
            pltpu.VMEM((2, QC, BLK, HALF), BF16),
            pltpu.VMEM((QC, BLK, HALF), BF16),
            pltpu.VMEM((2 * CHUNKS * CLS, 3, PIECE, BLK), BF16),
            pltpu.VMEM((2, QC, BLK, HALF), BF16),
            pltpu.VMEM((2, 8, HALF), F32),
            pltpu.VMEM((2, 8, HALF), F32),
            pltpu.VMEM((2, 4, 2, KEYROWS, D), BF16),
            pltpu.VMEM((HALF, D), BF16),
            pltpu.VMEM((D, 3 * D), BF16),
            pltpu.VMEM((ROWS, HALF), BF16),
            pltpu.VMEM((HALF, D), BF16),
            pltpu.VMEM((ROWS, D), BF16),
            pltpu.VMEM((ROWS, D), BF16),
            pltpu.VMEM((HEADS, HALF, ROWS), F32),
            pltpu.VMEM((HALF, ROWS), F32),
            pltpu.VMEM((HALF, D), BF16),
            pltpu.VMEM((8, KEYROWS, D), BF16),
            pltpu.VMEM((HALF, BLK), F32),
            pltpu.VMEM((8, KEYROWS, BLK), F32),
            pltpu.VMEM((KEYROWS, D), BF16),
            pltpu.VMEM((8, 2, HDIM, D), BF16),
            pltpu.VMEM((8, 2, KEYROWS, HDIM), BF16),
            dma((6,)),
            *sems,
        ],
        compiler_params=pltpu.CompilerParams(
            collective_id=0, has_side_effects=True, vmem_limit_bytes=65 * 1000 * 1000
        ),
    )(edge_weight, pattern, node_features, w_qkv, w_out.T, bias_gain, bias_rate)


def solution(mesh):
    in_specs = (P("row", None), P("row", "col"), P("row", "col"), P(), P(None, "col"), P(), P())
    return jax.shard_map(shards, mesh=mesh, in_specs=in_specs, out_specs=P("row", "col"), check_vma=False)
```

```python
import math

import jax
import jax.numpy as jnp
from jax import lax
from jax.experimental import pallas as pl
from jax.experimental.pallas import tpu as pltpu
from jax.sharding import PartitionSpec as P

D = 1024
HEADS = 16
BLK = 128
HDIM = 64
NODES = 6144
ROWS = 768
HALF = 384
QC = 3
CHUNKS = 6
CLS = 4
X_FIRST = (2, 2, 2, 2, 2, 2)
RELAYED = ()
T_LOAD = 2.9
T_QUERY = (4.5, 3.5, 3.0, 4.0)
T_KEY = (27.5, 26.5, 25.0, 27.0)
T_VALUE = (29.5, 28.0, 33.5, 29.0)
T_FIRST = 0.0
T_OWN = (5.0, 11.5, 12.0, 13.5)
T_FAR = (5.5, 16.0, 15.5, 18.5)
T_FEAT = (2.5, 7.0, 21.5, 21.0, 23.5, 24.5)
T_PANEL = (
    (0.5, 1.0, 1.5, 2.0, 9.0, 10.0),
    (6.0, 6.5, 7.5, 8.0, 13.0, 14.5),
    (8.5, 9.5, 10.5, 11.0, 18.0, 20.5),
    (12.5, 14.0, 16.5, 17.0, 24.0, 28.5),
    (17.5, 19.5, 22.0, 22.5, 30.0, 34.0),
)
T_SCORE = (35.5, 36.0, 37.0, 38.5, 39.0, 41.0, 42.5, 43.5, 44.0, 44.5, 45.0, 46.0)
T_READY = 19.0
T_ONE = (
    (1, 0, (0, 128), 20.0), (2, 1, (0, 128), 23.0), (3, 2, (0, 64), 31.0), (6, 2, (64, 64), 34.5)
)
T_LATE = {
    1: (26.0, 25.5, 30.5, 31.5),
    2: (32.5, 33.0, 36.5, 39.5),
    3: (38.0, 37.5, 40.5, 43.0),
    6: (42.0, 41.5, 45.5, 46.5),
}
T_TWO = (((0, 1), 0, True, 32.0), ((2,), 0, True, 35.0), ((0, 1, 2), 1, False, 40.0))
FAMILY = (0, 1, 1, 1, 2, 0, 1)
PIECE = 16
KEYROWS = 48
OWNROWS = 16
LOG2E = 1.4426950408889634
BIG = 1e30
MESH = pl.DeviceIdType.MESH
F32 = jnp.float32
BF16 = jnp.bfloat16


class Place:
    def __init__(self):
        r = lax.axis_index("row")
        c = lax.axis_index("col")
        self.zh, self.y = r // 4, r % 4
        self.zl, self.x, self.core = c // 8, (c // 2) % 4, c % 2
        self.z = 2 * self.zh + self.zl

    def at(self, x=None, y=None, z=None, core=None):
        x = self.x if x is None else x
        y = self.y if y is None else y
        z = self.z if z is None else z
        core = self.core if core is None else core
        return ((z // 2) * 4 + y, ((z % 2) * 4 + x) * 2 + core)


def remote(src, dst, send, recv, device):
    return pltpu.make_async_remote_copy(
        src_ref=src, dst_ref=dst, send_sem=send, recv_sem=recv, device_id=device, device_id_type=MESH
    )


def fused_kernel(
    edge, pattern, feat, w_qkv, w_out_t, gain, rate, out,
    panel, r1, r2, acc, staged, landed, adj, first, mrows, mboth, keys, own_feat, w_all, edge_v,
    query, key_proj, value_proj, scores, bias_in, numer, numer_all, stats, stats_all, att, w_cols, mix,
    loc_sem, a_send, a_recv, on_send, on_recv, i_send, i_recv, m_send, m_recv,
    y_send, y_recv, s_send, s_recv, f_send, f_recv, o_send, o_recv,
    n_send, n_recv, t_send, t_recv, w_send, w_recv, x_send, x_recv,
):
    me = Place()
    x, y, z, zh, zl, core = me.x, me.y, me.z, me.zh, me.zl, me.core
    sibling = me.at(core=1 - core)
    spot = zl * 4 + x
    ring = {
        "x+": me.at(x=(x + 1) % 4), "x-": me.at(x=(x + 3) % 4),
        "z+": me.at(z=(z + 1) % 4), "z-": me.at(z=(z + 3) % 4),
    }
    turned = (zl * 4 + x, (zh * 4 + y) * 2 + core)
    turned_self = (zl == zh) & (x == y)

    def chip(k, who=None):
        other = (spot + k) % 8
        return other, me.at(x=other % 4, z=2 * zh + other // 4, core=who)

    def y_peer(k):
        return me.at(y=(y + k) % 4)

    cross = (z + 2 * zl + 3) % 4
    friends = [sibling, me.at(z=cross, core=0), me.at(z=cross, core=1)]
    friends += [((1 - zl) * 4 + x, (zh * 4 + y) * 2 + core), (zl * 4 + x, ((1 - zh) * 4 + y) * 2 + core)]
    friends += [y_peer(k) for k in (1, 2, 3)]
    friends += [chip(k, who)[1] for k in range(1, 8) for who in (core, 1 - core)]
    barrier = pltpu.get_barrier_semaphore()
    for device in friends:
        pl.semaphore_signal(barrier, inc=1, device_id=device, device_id_type=MESH)

    @pl.when(jnp.logical_not(turned_self))
    def _():
        pl.semaphore_signal(barrier, inc=1, device_id=turned, device_id_type=MESH)

    sends = []

    def go(copy):
        copy.start()
        sends.append(copy)

    def arrived(ref, sem):
        pltpu.make_async_copy(ref, ref, sem).wait()

    loads = {
        "edge": pltpu.make_async_copy(edge, edge_v, loc_sem.at[0]),
        "feat": pltpu.make_async_copy(
            feat.at[pl.ds(pl.multiple_of(core * HALF, HALF), HALF)], own_feat, loc_sem.at[1]
        ),
        "w": pltpu.make_async_copy(w_qkv, w_all, loc_sem.at[2]),
    }
    for load in loads.values():
        load.start()
    loads["edge"].wait()

    same = (zl * 4 + x == zh * 4 + y)
    for rb in range(6):
        for cb in range(3):
            on = jnp.where(pattern[cb, rb] > 0, F32(1.0), F32(0.0))
            kept = edge_v[pl.ds(rb * BLK, BLK), pl.ds(cb * BLK, BLK)] * on.astype(BF16)
            adj[pl.ds(rb * 8, 8), cb] = kept.reshape(8, PIECE, BLK)
            row = lax.broadcasted_iota(jnp.int32, (BLK, BLK), 0) + rb * BLK
            col = lax.broadcasted_iota(jnp.int32, (BLK, BLK), 1) + cb * BLK + core * HALF
            diagonal = jnp.where((row == col) & same, F32(0.15), F32(0.0))
            value = (diagonal + F32(0.1275) * kept.astype(F32)) * on
            first[rb // 3, rb % 3, :, pl.ds(cb * BLK, BLK)] = value.astype(BF16)
            mboth[core, pl.ds(rb, 1), pl.ds(cb * BLK, BLK)] = jnp.full((1, BLK), on, F32)
    mask = mboth.at[core]

    pl.semaphore_wait(barrier, len(friends) + jnp.where(turned_self, 0, 1))

    goal = 2 * core + 1 - zl

    def send_first(qc):
        for half in range(2):
            target = me.at(z=goal, core=half)
            src, dst = first.at[half, qc], r1.at[y, zh, qc, half]
            remote(src, dst, i_send.at[half], i_recv.at[zh], target).start()

    def first_sent():
        for half in range(2):
            target = me.at(z=goal, core=half)
            remote(first.at[half], r1.at[y, zh, :, half], i_send.at[half], i_recv.at[zh], target).wait_send()
            remote(mask, mrows.at[zh], m_send.at[half], m_recv.at[zh], target).wait_send()

    for half in range(2):
        remote(mask, mrows.at[zh], m_send.at[half], m_recv.at[zh], me.at(z=goal, core=half)).start()

    def own(who):
        return panel.at[:, z, pl.ds(x * 3, 3), :, pl.ds(pl.multiple_of(who * 128, 128), 128)]

    rows24 = CHUNKS * CLS
    here = pltpu.make_async_copy(adj.at[pl.ds(core * rows24, rows24)], own(core), loc_sem.at[3])
    here.start()
    over = remote(adj.at[pl.ds((1 - core) * rows24, rows24)], own(core), on_send.at[0], on_recv.at[0], sibling)
    go(over)
    go(remote(mask, mask, on_send.at[1], on_recv.at[1], sibling))

    mine = pl.ds(pl.multiple_of(spot * 2 * KEYROWS + core * KEYROWS, KEYROWS), KEYROWS)

    def scatter_keys(waiting=False):
        for block in range(2):
            is_self = turned_self & (zh == block)
            dst = keys.at[zl, x, core]
            if not waiting:
                @pl.when(is_self)
                def _():
                    pltpu.make_async_copy(feat.at[mine], dst, f_recv.at[zl]).start()

            @pl.when(jnp.logical_not(is_self))
            def _():
                device = (block * 4 + x, (zh * 4 + y) * 2 + core)
                copy = remote(feat.at[mine], dst, f_send.at[block], f_recv.at[zl], device)
                if waiting:
                    copy.wait_send()
                else:
                    copy.start()

    here.wait()
    over.wait_recv()

    def a_copy(j, cls, leg, kind):
        sign = 1 if cls % 2 == 0 else -1
        along_x = (cls < X_FIRST[j]) == (leg == 0)
        head = sign if kind != 1 else -sign
        device = ring[("x" if along_x else "z") + ("+" if head == 1 else "-")]
        hop = -sign if kind == 2 else 0
        jc = j * CLS + cls
        if along_x:
            at_x = (x + hop + 8) % 4
            cols = pl.ds(at_x * 3, 3)
            ref = panel.at[jc, z, cols] if leg == 0 else panel.at[jc, :, cols]
        else:
            at_z = (z + hop + 8) % 4
            ref = panel.at[jc, at_z, pl.ds(x * 3, 3)] if leg == 0 else panel.at[jc, at_z]
        step = j * 4 + leg * 2 + (0 if kind == 0 else 1)
        return remote(ref, ref, a_send.at[leg], a_recv.at[step], device)

    def a_stage(j, stage):
        if stage > 0:
            four = pl.ds(j * CLS, CLS)
            ref = {
                1: panel.at[four, 0, pl.ds(0, 3)], 2: panel.at[four, 0, pl.ds(0, 6)],
                3: panel.at[four, 0], 4: panel.at[four, pl.ds(0, 2)],
            }[stage]
            arrived(ref, a_recv.at[j * 4 + stage - 1])
        for cls in range(CLS):
            for kind in ((), (2,), (0, 1), (2,), ())[stage] if stage else (0, 1):
                a_copy(j, cls, stage // 2, kind).start()

    def y_copy(base, cut, k, arriving):
        ref = cut((y - k + 4) % 4 if arriving else y, core)
        return remote(ref, ref, y_send.at[FAMILY[base]], y_recv.at[base * 3 + k - 1], y_peer(k))

    def y_share(base, cut, k):
        ref = cut((y - k + 4) % 4, core)
        remote(ref, ref, s_send.at[FAMILY[base]], s_recv.at[base], sibling).start()

    def y_begin(base, cut, peers=(1, 3, 2)):
        for k in peers:
            y_copy(base, cut, k, False).start()
        y_share(base, cut, 0)

    def y_pass(base, cut, k, relay=None):
        y_copy(base, cut, k, True).wait_recv()
        if relay is not None:
            ref = relay((y - k + 4) % 4, core)
            remote(ref, ref, y_send.at[FAMILY[base]], y_recv.at[base * 3 + 1], y_peer(k)).start()
        y_share(base, cut, k)

    def y_done(base, ref):
        arrived(ref, s_recv.at[base])

    def cut1(a):
        return lambda at_y, who: r1.at[at_y, a, :, who]

    def cut2(q, part, a=slice(None)):
        rows = pl.ds(part[0], part[1])
        return lambda at_y, who: r2.at[at_y, a, q, who, rows]

    def cutk(at_y, who, a=slice(None)):
        return keys.at[a, at_y, who]

    def lhs(q, m, h, kc, part=(0, BLK)):
        pieces = pl.ds(q * 8 + part[0] // PIECE, part[1] // PIECE)
        top = panel[pieces, h, m * 3 + kc].reshape(part[1], 256)
        low = panel[pieces, 2 + h, m * 3 + kc].reshape(part[1], 256)
        return jnp.concatenate([top, low], axis=0)

    def diag(a, q, part):
        row = lax.broadcasted_iota(jnp.int32, (part[1], HALF), 0) + (q * BLK + part[0])
        col = lax.broadcasted_iota(jnp.int32, (part[1], HALF), 1)
        own_block = (1 - zl == a) & (y == x) & (core == zh)
        return jnp.where((row == col) & own_block, F32(0.15), F32(0.0))

    def masked_ranks(a, q, total, part=(0, BLK)):
        keep = mrows[a, pl.ds(core * 3 + q, 1), :] > 0.5
        return jnp.where(keep, diag(a, q, part) + 0.85 * total, 0.0).astype(BF16)

    def sweep_one(q, part):
        size = part[1]

        def body(m, total):
            for h in range(2):
                for kc in range(3):
                    rhs = r1[m, h, kc].reshape(256, HALF)
                    total = total + jnp.dot(lhs(q, m, h, kc, part), rhs, preferred_element_type=F32)
            return total

        total = lax.fori_loop(0, 4, body, jnp.zeros((2 * size, HALF), F32))
        for a in range(2):
            value = masked_ranks(a, q, total[a * size:(a + 1) * size], part)
            r2[y, a, q, core, pl.ds(part[0], size)] = value

    def sweep_two(rows, kc, start):
        for q in rows:
            total = None if start else acc[q]
            for m in range(4):
                for h in range(2):
                    part = jnp.dot(lhs(q, m, h, kc), r2[m, h, kc].reshape(256, HALF), preferred_element_type=F32)
                    total = part if total is None else total + part
            acc[q] = total

    def project(dst, src, first_col, n):
        def body(t, _):
            cols = pl.ds(pl.multiple_of(t * 256, 256), 256)
            w = w_all[:, pl.ds(pl.multiple_of(first_col + t * 256, 256), 256)]
            dst[:, cols] = jnp.dot(src, w, preferred_element_type=F32).astype(BF16)
            return 0

        lax.fori_loop(n, n + 1, body, 0)

    lane = lax.broadcasted_iota(jnp.int32, (BLK, BLK), 1)

    def score_block(t):
        pair, row = t // QC, t % QC
        cols = pl.ds(pl.multiple_of(pair * BLK, BLK), BLK)
        rows = pl.ds(pl.multiple_of(row * BLK, BLK), BLK)
        q2 = query[rows, cols]
        k2 = key_proj[:, cols]
        away = [jnp.where(mboth[c, pl.ds(core * 3 + row, 1), :] > 0.5, F32(0.0), F32(-BIG)) for c in range(2)]
        away = jnp.concatenate(away, axis=1)
        kept = stats[rows, :]
        for side in range(2):
            head = pair * 2 + side
            q1 = jnp.where(lane // HDIM == side, q2, jnp.zeros_like(q2))
            s = lax.dot_general(q1, k2, (((1,), (1,)), ((), ())), preferred_element_type=F32)
            s = s * F32(LOG2E / math.sqrt(HDIM)) + away
            top = jnp.maximum(jnp.max(s, axis=1, keepdims=True), F32(-1e29))
            scores[head, rows, :] = s - top
            kept = jnp.where(lane == HEADS + head, top, kept)
        stats[rows, :] = kept

    def score_blocks(low, high):
        def body(t, _):
            score_block(t)
            return 0

        lax.fori_loop(low, high, body, 0)

    def expo_block(pair, row):
        cols = pl.ds(pl.multiple_of(pair * BLK, BLK), BLK)
        rows = pl.ds(pl.multiple_of(row * BLK, BLK), BLK)
        v2 = value_proj[:, cols]
        spread = bias_in[rows, :]
        both = []
        kept = stats[rows, :]
        for side in range(2):
            head = pair * 2 + side
            bias = (gain[head] * F32(LOG2E)) * jnp.tanh(spread * rate[head])
            e = jnp.exp2(scores[head, rows, :] + bias)
            kept = jnp.where(lane == head, jnp.sum(e, axis=1, keepdims=True), kept)
            both.append(jnp.dot(e.astype(BF16), v2, preferred_element_type=F32))
        stats[rows, :] = kept
        numer[rows, cols] = jnp.where(lane < HDIM, both[0], both[1]).astype(BF16)

    events = []

    def plan(when, what):
        events.append((when, len(events), what))

    def load_weights():
        loads["feat"].wait()
        loads["w"].wait()
        stats[...] = jnp.zeros_like(stats)

    def begin_ranks(base, a):
        pltpu.make_async_copy(first.at[0], r1.at[y, a, :, core], i_recv.at[a]).wait()
        y_begin(base, cut1(a))

    def begin_keys():
        for block in range(2):
            arrived(keys.at[block, y, core], f_recv.at[block])
        y_begin(4, cutk)

    plan(T_LOAD, load_weights)
    for n in range(4):
        plan(T_QUERY[n], lambda n=n: project(query, own_feat[...], 0, n))
        plan(T_KEY[n], lambda n=n: project(key_proj, keys[...].reshape(ROWS, D), D, n))
        plan(T_VALUE[n], lambda n=n: project(value_proj, keys[...].reshape(ROWS, D), 2 * D, n))
    for base, times in ((0, T_OWN), (5, T_FAR)):
        a = base // 5
        plan(times[0], lambda base=base, a=a: begin_ranks(base, a))
        for k, when in zip((1, 3, 2), times[1:]):
            relay = None
            plan(when, lambda base=base, a=a, k=k, relay=relay: y_pass(base, cut1(a), k, relay))
    plan(T_FEAT[0], scatter_keys)
    for qc in range(QC):
        plan(T_FIRST, lambda qc=qc: send_first(qc))
    plan(T_FEAT[1], begin_keys)
    for k, when in zip((1, 3, 2), T_FEAT[2:5]):
        relay = None
        plan(when, lambda k=k, relay=relay: y_pass(4, cutk, k, relay))
    plan(T_FEAT[5], lambda: y_done(4, keys.at[:, :, 0]))
    for j in range(CHUNKS):
        for stage in range(5):
            plan(T_PANEL[stage][j], lambda j=j, stage=stage: a_stage(j, stage))

    def ready():
        y_done(0, r1.at[:, 0, :, 0])
        y_done(5, r1.at[:, 0, :, 0])
        for a in range(2):
            pltpu.make_async_copy(mask, mrows.at[a], m_recv.at[a]).wait()

    plan(T_SCORE[0] - 0.1, lambda: remote(mask, mboth.at[1 - core], on_send.at[1], on_recv.at[1], sibling).wait_recv())
    for n, when in enumerate(T_SCORE):
        plan(when, lambda n=n: score_blocks(2 * n, 2 * n + 2))
    plan(T_READY, ready)
    for base, q, part, when in T_ONE:
        peers = (1, 3) if base in RELAYED else (1, 3, 2)

        def first_sweep(base=base, q=q, part=part, peers=peers):
            sweep_one(q, part)
            y_begin(base, cut2(q, part), peers)

        plan(when, first_sweep)
        for k, late in zip((1, 3, 2), T_LATE[base]):
            relay = cut2(q, part, k // 2) if k != 2 and len(peers) == 2 else None
            plan(late, lambda base=base, q=q, part=part, k=k, relay=relay: y_pass(base, cut2(q, part), k, relay))
        rows = pl.ds(part[0], part[1])
        plan(T_LATE[base][3], lambda base=base, q=q, rows=rows: y_done(base, r2.at[:, :, q, 0, rows]))
    for rows, kc, start, when in T_TWO:
        plan(when, lambda rows=rows, kc=kc, start=start: sweep_two(rows, kc, start))

    def send_weights():
        for k in range(8):
            ref = w_cols.at[spot, core]
            if k == 0:
                remote(w_out_t, ref, w_send.at[1], w_recv.at[1], sibling).start()
            else:
                remote(w_out_t, ref, w_send.at[0], w_recv.at[0], chip(k)[1]).start()
        pltpu.make_async_copy(w_out_t, w_cols.at[spot, core], loc_sem.at[4]).start()

    plan(T_PANEL[3][5] + 0.01, send_weights)
    for _, _, what in sorted(events, key=lambda e: e[:2]):
        what()

    for q in range(QC):
        sweep_two((q,), 2, False)
        for a in range(2):
            staged[a, q] = masked_ranks(a, q, acc[q, a * BLK:(a + 1) * BLK])
        for a in range(2):
            dst = landed.at[zh, q]
            go(remote(staged.at[a, q], dst, o_send.at[2 * q + a], o_recv.at[2 * q + zh], me.at(z=2 * a + 1 - zl)))

    def forward_weights():
        pltpu.make_async_copy(w_out_t, w_cols.at[spot, core], loc_sem.at[4]).wait()
        arrived(w_cols.at[pl.ds(0, 7), 0], w_recv.at[0])
        for k in range(1, 8):
            ref = w_cols.at[(spot + k) % 8, core]
            remote(ref, ref, w_send.at[1], w_recv.at[1], sibling).start()

    def widen(ref, half, q):
        cols = pl.ds(half * HALF, HALF)
        bias_in[pl.ds(q * BLK, BLK), cols] = ref[q].astype(F32) * F32(math.sqrt(NODES))

    def owned(q, at):
        return pl.ds(pl.multiple_of(q * BLK + at * OWNROWS, OWNROWS), OWNROWS)

    def attend(q):
        for half in range(2):
            arrived(landed.at[half, q], o_recv.at[2 * q + half])
            widen(landed.at[half], half, q)

        def body(t, _):
            expo_block(t, q)
            return 0

        lax.fori_loop(0, HEADS // 2, body, 0)
        for k in range(1, 8):
            other, device = chip(k)
            rows = owned(q, other)
            remote(numer.at[rows], numer_all.at[spot, q], n_send.at[0], n_recv.at[q], device).start()
            remote(stats.at[rows], stats_all.at[spot, q], t_send.at[0], t_recv.at[q], device).start()
        numer_all[spot, q] = numer[owned(q, spot), :]
        stats_all[spot, q] = stats[owned(q, spot), :]

    low = lax.broadcasted_iota(jnp.int32, (OWNROWS, BLK), 1) < HDIM

    def combine(q):
        arrived(stats_all.at[pl.ds(0, 7), q], t_recv.at[q])
        arrived(numer_all.at[pl.ds(0, 7), q], n_recv.at[q])
        table = [stats_all[s, q] for s in range(8)]
        tops = [t[:, HEADS:2 * HEADS] for t in table]
        peak = tops[0]
        for t in tops[1:]:
            peak = jnp.maximum(peak, t)
        weights = [jnp.exp2(t - peak) for t in tops]
        total = weights[0] * table[0][:, :HEADS]
        for s in range(1, 8):
            total = total + weights[s] * table[s][:, :HEADS]
        weights = [w / total for w in weights]
        for pair in range(HEADS // 2):
            cols = pl.ds(pair * BLK, BLK)
            value = jnp.zeros((OWNROWS, BLK), F32)
            for s in range(8):
                w = jnp.where(low, weights[s][:, 2 * pair:2 * pair + 1], weights[s][:, 2 * pair + 1:2 * pair + 2])
                value = value + w * numer_all[s, q, :, cols].astype(F32)
            att[q, :, cols] = value.astype(BF16)

    for q in range(QC):
        attend(q)
    forward_weights()
    for q in range(QC):
        combine(q)

    arrived(w_cols.at[:, 0], w_recv.at[1])
    mixed = lax.dot_general(
        att[...].reshape(KEYROWS, D), w_cols[...].reshape(D, D), (((1,), (1,)), ((), ())), preferred_element_type=F32
    ).astype(BF16)
    for c in range(2 * 8):
        mix[c // 2, c % 2] = mixed[:, c * HDIM:(c + 1) * HDIM].reshape(QC, OWNROWS, HDIM)

    def rows_of(who, at):
        return out.at[who, :, pl.ds(pl.multiple_of(at * OWNROWS, OWNROWS), OWNROWS)]

    for k in range(8):
        for flip in range(2):
            if k == 0 and flip == 0:
                continue
            other, device = chip(k, (core + flip) % 2)
            src = mix.at[other, (core + flip) % 2]
            remote(src, rows_of(core, spot), x_send.at[flip], x_recv.at[flip], device).start()
    last = pltpu.make_async_copy(mix.at[spot, core], rows_of(core, spot), loc_sem.at[5])
    last.start()
    for flip in range(2):
        arrived(mix.at[pl.ds(0, 7 + flip), 0], x_recv.at[flip])
    last.wait()
    for send in sends:
        send.wait_send()
    for flip in range(2):
        arrived(mix.at[pl.ds(0, 7 + flip), 0], x_send.at[flip])
        arrived(w_cols.at[pl.ds(0, 7 + flip), 0], w_send.at[flip])
    arrived(panel.at[:, 0, pl.ds(0, 9)], a_send.at[0])
    arrived(panel.at[:, pl.ds(0, 3)], a_send.at[1])
    three = pl.ds(0, 3)
    for n, ref in enumerate((r1.at[three, :, :, 0], r2.at[three, :, :, 0], keys.at[:, three, 0])):
        arrived(ref, y_send.at[n])
    for n, ref in enumerate((r1.at[:, :, :, 0], r2.at[:, :, :, 0], keys.at[:, :, 0])):
        arrived(ref, s_send.at[n])
    arrived(numer_all.at[pl.ds(0, 7)], n_send.at[0])
    arrived(stats_all.at[pl.ds(0, 7)], t_send.at[0])
    first_sent()

    scatter_keys(waiting=True)


def shards(node_features, edge_weight, pattern, w_qkv, w_out, bias_gain, bias_rate):
    dma = pltpu.SemaphoreType.DMA
    anywhere = pl.BlockSpec(memory_space=pl.ANY)
    vmem = pl.BlockSpec(memory_space=pltpu.VMEM)
    smem = pl.BlockSpec(memory_space=pltpu.SMEM)
    counts = (2, 4 * CHUNKS, 2, 2, 2, 2, 2, 2, 3, 21, 3, 7, 2, 2, 6, 6, 1, QC, 1, QC, 2, 2, 2, 2)
    sems = [dma((n,)) for n in counts]
    mixed = pl.pallas_call(
        fused_kernel,
        name="fused",
        out_shape=jax.ShapeDtypeStruct((2, QC, BLK, HDIM), BF16),
        in_specs=[anywhere, smem, anywhere, anywhere, anywhere, smem, smem],
        out_specs=vmem,
        scratch_shapes=[
            pltpu.VMEM((CHUNKS * CLS, 4, 12, PIECE, 256), BF16),
            pltpu.VMEM((4, 2, QC, 2, BLK, HALF), BF16),
            pltpu.VMEM((4, 2, QC, 2, BLK, HALF), BF16),
            pltpu.VMEM((QC, 2 * BLK, HALF), F32),
            pltpu.VMEM((2, QC, BLK, HALF), BF16),
            pltpu.VMEM((2, QC, BLK, HALF), BF16),
            pltpu.VMEM((2 * CHUNKS * CLS, 3, PIECE, BLK), BF16),
            pltpu.VMEM((2, QC, BLK, HALF), BF16),
            pltpu.VMEM((2, 8, HALF), F32),
            pltpu.VMEM((2, 8, HALF), F32),
            pltpu.VMEM((2, 4, 2, KEYROWS, D), BF16),
            pltpu.VMEM((HALF, D), BF16),
            pltpu.VMEM((D, 3 * D), BF16),
            pltpu.VMEM((ROWS, HALF), BF16),
            pltpu.VMEM((HALF, D), BF16),
            pltpu.VMEM((ROWS, D), BF16),
            pltpu.VMEM((ROWS, D), BF16),
            pltpu.VMEM((HEADS, HALF, ROWS), F32),
            pltpu.VMEM((HALF, ROWS), F32),
            pltpu.VMEM((HALF, D), BF16),
            pltpu.VMEM((8, QC, OWNROWS, D), BF16),
            pltpu.VMEM((HALF, BLK), F32),
            pltpu.VMEM((8, QC, OWNROWS, BLK), F32),
            pltpu.VMEM((QC, OWNROWS, D), BF16),
            pltpu.VMEM((8, 2, HDIM, D), BF16),
            pltpu.VMEM((8, 2, QC, OWNROWS, HDIM), BF16),
            dma((6,)),
            *sems,
        ],
        compiler_params=pltpu.CompilerParams(
            collective_id=0, has_side_effects=True, vmem_limit_bytes=65 * 1000 * 1000
        ),
    )(edge_weight, pattern.T, node_features, w_qkv, w_out.T, bias_gain, bias_rate)
    return mixed.reshape(ROWS, HDIM)


def solution(mesh):
    in_specs = (P("row", None), P("row", "col"), P("row", "col"), P(), P(None, "col"), P(), P())
    return jax.shard_map(shards, mesh=mesh, in_specs=in_specs, out_specs=P("row", "col"), check_vma=False)
```

```python
import math

import jax
import jax.numpy as jnp
from jax import lax
from jax.experimental import pallas as pl
from jax.experimental.pallas import tpu as pltpu
from jax.sharding import PartitionSpec as P

D = 1024
HEADS = 16
BLK = 128
HDIM = 64
NODES = 6144
ROWS = 768
HALF = 384
QC = 3
CHUNKS = 6
CLS = 4
X_FIRST = (2, 2, 2, 2, 2, 2)
RELAYED = (0, 1, 2, 4, 5)
T_LOAD = 3.9
T_QUERY = (5.0, 4.0, 5.5, 4.5)
T_KEY = (23.5, 19.5, 21.0, 22.0)
T_VALUE = (18.5, 20.0, 20.5, 36.5)
T_FIRST = (0.0, 1.0, 1.5)
T_OWN = (6.5, 14.0, 14.5, 23.0)
T_FAR = (7.0, 17.0, 16.5, 22.5)
T_FEAT = (0.5, 6.0, 12.0, 11.5, 17.5, 18.0)
T_PANEL = (
    (2.0, 2.5, 3.0, 3.5, 10.0, 11.0),
    (7.5, 8.0, 8.5, 9.0, 15.0, 16.0),
    (9.5, 10.5, 12.5, 13.0, 25.0, 28.5),
    (13.5, 15.5, 19.0, 21.5, 34.5, 37.0),
    (24.0, 27.5, 30.0, 31.5, 38.5, 41.0),
)
T_SCORE = (24.5, 26.0, 27.0, 29.0, 29.5, 30.5, 31.0, 32.5, 33.0, 33.5, 34.0, 36.0)
T_READY = 26.5
T_ONE = (
    (1, 0, (0, 128), 28.0), (2, 1, (0, 128), 32.0), (3, 2, (0, 64), 39.0), (6, 2, (64, 64), 41.5)
)
T_LATE = {
    1: (35.5, 35.0, 39.5, 40.0),
    2: (37.5, 38.0, 42.5, 44.0),
    3: (43.0, 43.5, 45.0, 46.5),
    6: (46.0, 45.5, 47.0, 47.5),
}
T_TWO = (((0, 1), 0, True, 40.5), ((2,), 0, True, 42.0), ((0, 1, 2), 1, False, 44.5))
FAMILY = (0, 1, 1, 1, 2, 0, 1)
PIECE = 16
KEYROWS = 48
OWNROWS = 16
LOG2E = 1.4426950408889634
BIG = 1e30
MESH = pl.DeviceIdType.MESH
F32 = jnp.float32
BF16 = jnp.bfloat16


class Place:
    def __init__(self):
        r = lax.axis_index("row")
        c = lax.axis_index("col")
        self.zh, self.y = r // 4, r % 4
        self.zl, self.x, self.core = c // 8, (c // 2) % 4, c % 2
        self.z = 2 * self.zh + self.zl

    def at(self, x=None, y=None, z=None, core=None):
        x = self.x if x is None else x
        y = self.y if y is None else y
        z = self.z if z is None else z
        core = self.core if core is None else core
        return ((z // 2) * 4 + y, ((z % 2) * 4 + x) * 2 + core)


def remote(src, dst, send, recv, device):
    return pltpu.make_async_remote_copy(
        src_ref=src, dst_ref=dst, send_sem=send, recv_sem=recv, device_id=device, device_id_type=MESH
    )


def fused_kernel(
    edge, pattern, feat, w_qkv, w_out_t, gain, rate, out,
    panel, r1, r2, acc, staged, landed, adj, first, mrows, mboth, first_sib, keys, own_feat, w_all, edge_v,
    query, key_proj, value_proj, scores, bias_in, numer, numer_all, stats, stats_all, att, w_cols, mix,
    loc_sem, a_send, a_recv, on_send, on_recv, i_send, i_recv, m_send, m_recv,
    y_send, y_recv, s_send, s_recv, f_send, f_recv, o_send, o_recv,
    n_send, n_recv, t_send, t_recv, w_send, w_recv, x_send, x_recv,
):
    me = Place()
    x, y, z, zh, zl, core = me.x, me.y, me.z, me.zh, me.zl, me.core
    sibling = me.at(core=1 - core)
    spot = zl * 4 + x
    ring = {
        "x+": me.at(x=(x + 1) % 4), "x-": me.at(x=(x + 3) % 4),
        "z+": me.at(z=(z + 1) % 4), "z-": me.at(z=(z + 3) % 4),
    }
    turned = (zl * 4 + x, (zh * 4 + y) * 2 + core)
    turned_self = (zl == zh) & (x == y)

    def chip(k, who=None):
        other = (spot + k) % 8
        return other, me.at(x=other % 4, z=2 * zh + other // 4, core=who)

    def y_peer(k):
        return me.at(y=(y + k) % 4)

    cross = (z + 2 * zl + 3) % 4
    friends = [sibling, me.at(z=cross, core=0), me.at(z=cross, core=1)]
    friends += [((1 - zl) * 4 + x, (zh * 4 + y) * 2 + core), (zl * 4 + x, ((1 - zh) * 4 + y) * 2 + core)]
    friends += [y_peer(k) for k in (1, 2, 3)]
    friends += [chip(k, who)[1] for k in range(1, 8) for who in (core, 1 - core)]
    barrier = pltpu.get_barrier_semaphore()
    for device in friends:
        pl.semaphore_signal(barrier, inc=1, device_id=device, device_id_type=MESH)

    @pl.when(jnp.logical_not(turned_self))
    def _():
        pl.semaphore_signal(barrier, inc=1, device_id=turned, device_id_type=MESH)

    sends = []

    def go(copy):
        copy.start()
        sends.append(copy)

    def arrived(ref, sem):
        pltpu.make_async_copy(ref, ref, sem).wait()

    loads = {
        "edge": pltpu.make_async_copy(edge, edge_v, loc_sem.at[0]),
        "feat": pltpu.make_async_copy(
            feat.at[pl.ds(pl.multiple_of(core * HALF, HALF), HALF)], own_feat, loc_sem.at[1]
        ),
        "w": pltpu.make_async_copy(w_qkv, w_all, loc_sem.at[2]),
    }
    for load in loads.values():
        load.start()
    loads["edge"].wait()

    same = (zl * 4 + x == zh * 4 + y)
    for rb in range(6):
        for cb in range(3):
            on = jnp.where(pattern[cb, rb] > 0, F32(1.0), F32(0.0))
            kept = edge_v[pl.ds(rb * BLK, BLK), pl.ds(cb * BLK, BLK)] * on.astype(BF16)
            adj[pl.ds(rb * 8, 8), cb] = kept.reshape(8, PIECE, BLK)
            row = lax.broadcasted_iota(jnp.int32, (BLK, BLK), 0) + rb * BLK
            col = lax.broadcasted_iota(jnp.int32, (BLK, BLK), 1) + cb * BLK + core * HALF
            diagonal = jnp.where((row == col) & same, F32(0.15), F32(0.0))
            value = (diagonal + F32(0.1275) * kept.astype(F32)) * on
            first[rb // 3, rb % 3, :, pl.ds(cb * BLK, BLK)] = value.astype(BF16)
            mboth[core, pl.ds(rb, 1), pl.ds(cb * BLK, BLK)] = jnp.full((1, BLK), on, F32)
    mask = mboth.at[core]

    pl.semaphore_wait(barrier, len(friends) + jnp.where(turned_self, 0, 1))

    goal = 2 * core + 1 - zl

    def first_copy(qc, mine):
        src = first.at[core, qc] if mine else first_sib.at[qc]
        way = core if mine else 1 - core
        dst = r1.at[y, zh, qc, core]
        return remote(src, dst, i_send.at[0 if mine else 1], i_recv.at[zh], me.at(z=2 * way + 1 - zl))

    def send_first(qc):
        if qc == 0:
            arrived(first_sib, on_recv.at[2])
        for mine in (True, False):
            first_copy(qc, mine).start()

    def first_sent():
        for n in range(2):
            arrived(first.at[0], i_send.at[n])
        for half in range(2):
            remote(mask, mrows.at[zh], m_send.at[half], m_recv.at[zh], me.at(z=goal, core=half)).wait_send()

    for half in range(2):
        remote(mask, mrows.at[zh], m_send.at[half], m_recv.at[zh], me.at(z=goal, core=half)).start()

    def own(who):
        return panel.at[:, z, pl.ds(x * 3, 3), :, pl.ds(pl.multiple_of(who * 128, 128), 128)]

    rows24 = CHUNKS * CLS
    here = pltpu.make_async_copy(adj.at[pl.ds(core * rows24, rows24)], own(core), loc_sem.at[3])
    here.start()
    over = remote(adj.at[pl.ds((1 - core) * rows24, rows24)], own(core), on_send.at[0], on_recv.at[0], sibling)
    go(over)
    go(remote(first.at[1 - core], first_sib, on_send.at[2], on_recv.at[2], sibling))
    go(remote(mask, mask, on_send.at[1], on_recv.at[1], sibling))

    mine = pl.ds(pl.multiple_of(spot * 2 * KEYROWS + core * KEYROWS, KEYROWS), KEYROWS)

    def scatter_keys(waiting=False):
        for block in range(2):
            is_self = turned_self & (zh == block)
            dst = keys.at[zl, x, core]
            if not waiting:
                @pl.when(is_self)
                def _():
                    pltpu.make_async_copy(feat.at[mine], dst, f_recv.at[zl]).start()

            @pl.when(jnp.logical_not(is_self))
            def _():
                device = (block * 4 + x, (zh * 4 + y) * 2 + core)
                copy = remote(feat.at[mine], dst, f_send.at[block], f_recv.at[zl], device)
                if waiting:
                    copy.wait_send()
                else:
                    copy.start()

    here.wait()
    over.wait_recv()

    def a_copy(j, cls, leg, kind):
        sign = 1 if cls % 2 == 0 else -1
        along_x = (cls < X_FIRST[j]) == (leg == 0)
        head = sign if kind != 1 else -sign
        device = ring[("x" if along_x else "z") + ("+" if head == 1 else "-")]
        hop = -sign if kind == 2 else 0
        jc = j * CLS + cls
        if along_x:
            at_x = (x + hop + 8) % 4
            cols = pl.ds(at_x * 3, 3)
            ref = panel.at[jc, z, cols] if leg == 0 else panel.at[jc, :, cols]
        else:
            at_z = (z + hop + 8) % 4
            ref = panel.at[jc, at_z, pl.ds(x * 3, 3)] if leg == 0 else panel.at[jc, at_z]
        step = j * 4 + leg * 2 + (0 if kind == 0 else 1)
        return remote(ref, ref, a_send.at[leg], a_recv.at[step], device)

    def a_stage(j, stage):
        if stage > 0:
            four = pl.ds(j * CLS, CLS)
            ref = {
                1: panel.at[four, 0, pl.ds(0, 3)], 2: panel.at[four, 0, pl.ds(0, 6)],
                3: panel.at[four, 0], 4: panel.at[four, pl.ds(0, 2)],
            }[stage]
            arrived(ref, a_recv.at[j * 4 + stage - 1])
        for cls in range(CLS):
            for kind in ((), (2,), (0, 1), (2,), ())[stage] if stage else (0, 1):
                a_copy(j, cls, stage // 2, kind).start()

    def y_copy(base, cut, k, arriving):
        ref = cut((y - k + 4) % 4 if arriving else y, core)
        return remote(ref, ref, y_send.at[FAMILY[base]], y_recv.at[base * 3 + k - 1], y_peer(k))

    def y_share(base, cut, k):
        ref = cut((y - k + 4) % 4, core)
        remote(ref, ref, s_send.at[FAMILY[base]], s_recv.at[base], sibling).start()

    def y_begin(base, cut, peers=(1, 3, 2)):
        for k in peers:
            y_copy(base, cut, k, False).start()
        y_share(base, cut, 0)

    def y_pass(base, cut, k, relay=None):
        y_copy(base, cut, k, True).wait_recv()
        if relay is not None:
            ref = relay((y - k + 4) % 4, core)
            remote(ref, ref, y_send.at[FAMILY[base]], y_recv.at[base * 3 + 1], y_peer(k)).start()
        y_share(base, cut, k)

    def y_done(base, ref):
        arrived(ref, s_recv.at[base])

    def cut1(a):
        return lambda at_y, who: r1.at[at_y, a, :, who]

    def cut2(q, part, a=slice(None)):
        rows = pl.ds(part[0], part[1])
        return lambda at_y, who: r2.at[at_y, a, q, who, rows]

    def cutk(at_y, who, a=slice(None)):
        return keys.at[a, at_y, who]

    def lhs(q, m, h, kc, part=(0, BLK)):
        pieces = pl.ds(q * 8 + part[0] // PIECE, part[1] // PIECE)
        top = panel[pieces, h, m * 3 + kc].reshape(part[1], 256)
        low = panel[pieces, 2 + h, m * 3 + kc].reshape(part[1], 256)
        return jnp.concatenate([top, low], axis=0)

    def diag(a, q, part):
        row = lax.broadcasted_iota(jnp.int32, (part[1], HALF), 0) + (q * BLK + part[0])
        col = lax.broadcasted_iota(jnp.int32, (part[1], HALF), 1)
        own_block = (1 - zl == a) & (y == x) & (core == zh)
        return jnp.where((row == col) & own_block, F32(0.15), F32(0.0))

    def masked_ranks(a, q, total, part=(0, BLK)):
        keep = mrows[a, pl.ds(core * 3 + q, 1), :] > 0.5
        return jnp.where(keep, diag(a, q, part) + 0.85 * total, 0.0).astype(BF16)

    def sweep_one(q, part):
        size = part[1]

        total = None
        for m in range(4):
            for h in range(2):
                for kc in range(3):
                    rhs = r1[m, h, kc].reshape(256, HALF)
                    product = jnp.dot(lhs(q, m, h, kc, part), rhs, preferred_element_type=F32)
                    total = product if total is None else total + product
        for a in range(2):
            value = masked_ranks(a, q, total[a * size:(a + 1) * size], part)
            r2[y, a, q, core, pl.ds(part[0], size)] = value

    def sweep_two(rows, kc, start):
        for q in rows:
            total = None if start else acc[q]
            for m in range(4):
                for h in range(2):
                    part = jnp.dot(lhs(q, m, h, kc), r2[m, h, kc].reshape(256, HALF), preferred_element_type=F32)
                    total = part if total is None else total + part
            acc[q] = total

    def project(dst, src, first_col, n):
        def body(t, _):
            cols = pl.ds(pl.multiple_of(t * 256, 256), 256)
            w = w_all[:, pl.ds(pl.multiple_of(first_col + t * 256, 256), 256)]
            dst[:, cols] = jnp.dot(src, w, preferred_element_type=F32).astype(BF16)
            return 0

        lax.fori_loop(n, n + 1, body, 0)

    lane = lax.broadcasted_iota(jnp.int32, (BLK, BLK), 1)

    def score_block(t):
        pair, row = t // QC, t % QC
        cols = pl.ds(pl.multiple_of(pair * BLK, BLK), BLK)
        rows = pl.ds(pl.multiple_of(row * BLK, BLK), BLK)
        q2 = query[rows, cols]
        k2 = key_proj[:, cols]
        away = [jnp.where(mboth[c, pl.ds(core * 3 + row, 1), :] > 0.5, F32(0.0), F32(-BIG)) for c in range(2)]
        away = jnp.concatenate(away, axis=1)
        kept = stats[rows, :]
        for side in range(2):
            head = pair * 2 + side
            q1 = jnp.where(lane // HDIM == side, q2, jnp.zeros_like(q2))
            s = lax.dot_general(q1, k2, (((1,), (1,)), ((), ())), preferred_element_type=F32)
            s = s * F32(LOG2E / math.sqrt(HDIM)) + away
            top = jnp.maximum(jnp.max(s, axis=1, keepdims=True), F32(-1e29))
            scores[head, rows, :] = s - top
            kept = jnp.where(lane == HEADS + head, top, kept)
        stats[rows, :] = kept

    def score_blocks(low, high):
        def body(t, _):
            score_block(t)
            return 0

        lax.fori_loop(low, high, body, 0)

    def expo_block(pair, row):
        cols = pl.ds(pl.multiple_of(pair * BLK, BLK), BLK)
        rows = pl.ds(pl.multiple_of(row * BLK, BLK), BLK)
        v2 = value_proj[:, cols]
        spread = bias_in[rows, :]
        both = []
        kept = stats[rows, :]
        for side in range(2):
            head = pair * 2 + side
            bias = (gain[head] * F32(LOG2E)) * jnp.tanh(spread * rate[head])
            e = jnp.exp2(scores[head, rows, :] + bias)
            kept = jnp.where(lane == head, jnp.sum(e, axis=1, keepdims=True), kept)
            both.append(jnp.dot(e.astype(BF16), v2, preferred_element_type=F32))
        stats[rows, :] = kept
        numer[rows, cols] = jnp.where(lane < HDIM, both[0], both[1]).astype(BF16)

    events = []

    def plan(when, what):
        events.append((when, len(events), what))

    def load_weights():
        loads["feat"].wait()
        loads["w"].wait()
        stats[...] = jnp.zeros_like(stats)

    def begin_ranks(base, a):
        pltpu.make_async_copy(first.at[0], r1.at[y, a, :, core], i_recv.at[a]).wait()
        y_begin(base, cut1(a), (1, 3) if base in RELAYED else (1, 3, 2))

    def begin_keys():
        for block in range(2):
            arrived(keys.at[block, y, core], f_recv.at[block])
        y_begin(4, cutk, (1, 3) if 4 in RELAYED else (1, 3, 2))

    plan(T_LOAD, load_weights)
    for n in range(4):
        plan(T_QUERY[n], lambda n=n: project(query, own_feat[...], 0, n))
        plan(T_KEY[n], lambda n=n: project(key_proj, keys[...].reshape(ROWS, D), D, n))
        plan(T_VALUE[n], lambda n=n: project(value_proj, keys[...].reshape(ROWS, D), 2 * D, n))
    for base, times in ((0, T_OWN), (5, T_FAR)):
        a = base // 5
        plan(times[0], lambda base=base, a=a: begin_ranks(base, a))
        for k, when in zip((1, 3, 2), times[1:]):
            relay = cut1(a) if base in RELAYED and k == 1 + 2 * a else None
            plan(when, lambda base=base, a=a, k=k, relay=relay: y_pass(base, cut1(a), k, relay))
    plan(T_FEAT[0], scatter_keys)
    for qc in range(QC):
        plan(T_FIRST[qc], lambda qc=qc: send_first(qc))
    plan(T_FEAT[1], begin_keys)
    for k, when in zip((1, 3, 2), T_FEAT[2:5]):
        relay = None
        if 4 in RELAYED and k != 2:
            relay = lambda at_y, who, k=k: cutk(at_y, who, k // 2)
        plan(when, lambda k=k, relay=relay: y_pass(4, cutk, k, relay))
    plan(T_FEAT[5], lambda: y_done(4, keys.at[:, :, 0]))
    for j in range(CHUNKS):
        for stage in range(5):
            plan(T_PANEL[stage][j], lambda j=j, stage=stage: a_stage(j, stage))

    def ready():
        y_done(0, r1.at[:, 0, :, 0])
        y_done(5, r1.at[:, 0, :, 0])
        for a in range(2):
            pltpu.make_async_copy(mask, mrows.at[a], m_recv.at[a]).wait()

    plan(T_SCORE[0] - 0.1, lambda: remote(mask, mboth.at[1 - core], on_send.at[1], on_recv.at[1], sibling).wait_recv())
    for n, when in enumerate(T_SCORE):
        plan(when, lambda n=n: score_blocks(2 * n, 2 * n + 2))
    plan(T_READY, ready)
    for base, q, part, when in T_ONE:
        peers = (1, 3) if base in RELAYED else (1, 3, 2)

        def first_sweep(base=base, q=q, part=part, peers=peers):
            sweep_one(q, part)
            y_begin(base, cut2(q, part), peers)

        plan(when, first_sweep)
        for k, late in zip((1, 3, 2), T_LATE[base]):
            relay = cut2(q, part, k // 2) if k != 2 and len(peers) == 2 else None
            plan(late, lambda base=base, q=q, part=part, k=k, relay=relay: y_pass(base, cut2(q, part), k, relay))
        rows = pl.ds(part[0], part[1])
        plan(T_LATE[base][3], lambda base=base, q=q, rows=rows: y_done(base, r2.at[:, :, q, 0, rows]))
    for rows, kc, start, when in T_TWO:
        plan(when, lambda rows=rows, kc=kc, start=start: sweep_two(rows, kc, start))

    def send_weights():
        for k in range(8):
            ref = w_cols.at[spot, core]
            if k == 0:
                remote(w_out_t, ref, w_send.at[1], w_recv.at[1], sibling).start()
            else:
                remote(w_out_t, ref, w_send.at[0], w_recv.at[0], chip(k)[1]).start()
        pltpu.make_async_copy(w_out_t, w_cols.at[spot, core], loc_sem.at[4]).start()

    plan(T_PANEL[3][5] + 0.01, send_weights)
    for _, _, what in sorted(events, key=lambda e: e[:2]):
        what()

    for q in range(QC):
        sweep_two((q,), 2, False)
        for a in range(2):
            staged[a, q] = masked_ranks(a, q, acc[q, a * BLK:(a + 1) * BLK])
        for a in range(2):
            dst = landed.at[zh, q]
            go(remote(staged.at[a, q], dst, o_send.at[2 * q + a], o_recv.at[2 * q + zh], me.at(z=2 * a + 1 - zl)))

    def forward_weights():
        pltpu.make_async_copy(w_out_t, w_cols.at[spot, core], loc_sem.at[4]).wait()
        arrived(w_cols.at[pl.ds(0, 7), 0], w_recv.at[0])
        for k in range(1, 8):
            ref = w_cols.at[(spot + k) % 8, core]
            remote(ref, ref, w_send.at[1], w_recv.at[1], sibling).start()

    def widen(ref, half, q):
        cols = pl.ds(half * HALF, HALF)
        bias_in[pl.ds(q * BLK, BLK), cols] = ref[q].astype(F32) * F32(math.sqrt(NODES))

    def owned(q, at):
        return pl.ds(pl.multiple_of(q * BLK + at * OWNROWS, OWNROWS), OWNROWS)

    def attend(q):
        for half in range(2):
            arrived(landed.at[half, q], o_recv.at[2 * q + half])
            widen(landed.at[half], half, q)

        def body(t, _):
            expo_block(t, q)
            return 0

        lax.fori_loop(0, HEADS // 2, body, 0)
        for k in range(1, 8):
            other, device = chip(k)
            rows = owned(q, other)
            remote(numer.at[rows], numer_all.at[spot, q], n_send.at[0], n_recv.at[q], device).start()
            remote(stats.at[rows], stats_all.at[spot, q], t_send.at[0], t_recv.at[q], device).start()
        numer_all[spot, q] = numer[owned(q, spot), :]
        stats_all[spot, q] = stats[owned(q, spot), :]

    low = lax.broadcasted_iota(jnp.int32, (OWNROWS, BLK), 1) < HDIM

    def combine(q):
        arrived(stats_all.at[pl.ds(0, 7), q], t_recv.at[q])
        arrived(numer_all.at[pl.ds(0, 7), q], n_recv.at[q])
        table = [stats_all[s, q] for s in range(8)]
        tops = [t[:, HEADS:2 * HEADS] for t in table]
        peak = tops[0]
        for t in tops[1:]:
            peak = jnp.maximum(peak, t)
        weights = [jnp.exp2(t - peak) for t in tops]
        total = weights[0] * table[0][:, :HEADS]
        for s in range(1, 8):
            total = total + weights[s] * table[s][:, :HEADS]
        weights = [w / total for w in weights]
        for pair in range(HEADS // 2):
            cols = pl.ds(pair * BLK, BLK)
            value = jnp.zeros((OWNROWS, BLK), F32)
            for s in range(8):
                w = jnp.where(low, weights[s][:, 2 * pair:2 * pair + 1], weights[s][:, 2 * pair + 1:2 * pair + 2])
                value = value + w * numer_all[s, q, :, cols].astype(F32)
            att[q, :, cols] = value.astype(BF16)

    for q in range(QC):
        attend(q)
    forward_weights()
    for q in range(QC):
        combine(q)

    arrived(w_cols.at[:, 0], w_recv.at[1])
    mixed = lax.dot_general(
        att[...].reshape(KEYROWS, D), w_cols[...].reshape(D, D), (((1,), (1,)), ((), ())), preferred_element_type=F32
    ).astype(BF16)
    for c in range(2 * 8):
        mix[c // 2, c % 2] = mixed[:, c * HDIM:(c + 1) * HDIM].reshape(QC, OWNROWS, HDIM)

    def rows_of(who, at):
        return out.at[who, :, pl.ds(pl.multiple_of(at * OWNROWS, OWNROWS), OWNROWS)]

    for k in range(8):
        for flip in range(2):
            if k == 0 and flip == 0:
                continue
            other, device = chip(k, (core + flip) % 2)
            src = mix.at[other, (core + flip) % 2]
            remote(src, rows_of(core, spot), x_send.at[flip], x_recv.at[flip], device).start()
    last = pltpu.make_async_copy(mix.at[spot, core], rows_of(core, spot), loc_sem.at[5])
    last.start()
    for flip in range(2):
        arrived(mix.at[pl.ds(0, 7 + flip), 0], x_recv.at[flip])
    last.wait()
    for send in sends:
        send.wait_send()
    for flip in range(2):
        arrived(mix.at[pl.ds(0, 7 + flip), 0], x_send.at[flip])
        arrived(w_cols.at[pl.ds(0, 7 + flip), 0], w_send.at[flip])
    arrived(panel.at[:, 0, pl.ds(0, 9)], a_send.at[0])
    arrived(panel.at[:, pl.ds(0, 3)], a_send.at[1])
    three = pl.ds(0, 3)
    for n, ref in enumerate((r1.at[three, :, :, 0], r2.at[three, :, :, 0], keys.at[:, three, 0])):
        arrived(ref, y_send.at[n])
    for n, ref in enumerate((r1.at[:, :, :, 0], r2.at[:, :, :, 0], keys.at[:, :, 0])):
        arrived(ref, s_send.at[n])
    arrived(numer_all.at[pl.ds(0, 7)], n_send.at[0])
    arrived(stats_all.at[pl.ds(0, 7)], t_send.at[0])
    first_sent()

    scatter_keys(waiting=True)


def shards(node_features, edge_weight, pattern, w_qkv, w_out, bias_gain, bias_rate):
    dma = pltpu.SemaphoreType.DMA
    anywhere = pl.BlockSpec(memory_space=pl.ANY)
    vmem = pl.BlockSpec(memory_space=pltpu.VMEM)
    smem = pl.BlockSpec(memory_space=pltpu.SMEM)
    counts = (2, 4 * CHUNKS, 3, 3, 2, 2, 2, 2, 3, 21, 3, 7, 2, 2, 6, 6, 1, QC, 1, QC, 2, 2, 2, 2)
    sems = [dma((n,)) for n in counts]
    mixed = pl.pallas_call(
        fused_kernel,
        name="fused",
        out_shape=jax.ShapeDtypeStruct((2, QC, BLK, HDIM), BF16),
        in_specs=[anywhere, smem, anywhere, anywhere, anywhere, smem, smem],
        out_specs=vmem,
        scratch_shapes=[
            pltpu.VMEM((CHUNKS * CLS, 4, 12, PIECE, 256), BF16),
            pltpu.VMEM((4, 2, QC, 2, BLK, HALF), BF16),
            pltpu.VMEM((4, 2, QC, 2, BLK, HALF), BF16),
            pltpu.VMEM((QC, 2 * BLK, HALF), F32),
            pltpu.VMEM((2, QC, BLK, HALF), BF16),
            pltpu.VMEM((2, QC, BLK, HALF), BF16),
            pltpu.VMEM((2 * CHUNKS * CLS, 3, PIECE, BLK), BF16),
            pltpu.VMEM((2, QC, BLK, HALF), BF16),
            pltpu.VMEM((2, 8, HALF), F32),
            pltpu.VMEM((2, 8, HALF), F32),
            pltpu.VMEM((QC, BLK, HALF), BF16),
            pltpu.VMEM((2, 4, 2, KEYROWS, D), BF16),
            pltpu.VMEM((HALF, D), BF16),
            pltpu.VMEM((D, 3 * D), BF16),
            pltpu.VMEM((ROWS, HALF), BF16),
            pltpu.VMEM((HALF, D), BF16),
            pltpu.VMEM((ROWS, D), BF16),
            pltpu.VMEM((ROWS, D), BF16),
            pltpu.VMEM((HEADS, HALF, ROWS), F32),
            pltpu.VMEM((HALF, ROWS), F32),
            pltpu.VMEM((HALF, D), BF16),
            pltpu.VMEM((8, QC, OWNROWS, D), BF16),
            pltpu.VMEM((HALF, BLK), F32),
            pltpu.VMEM((8, QC, OWNROWS, BLK), F32),
            pltpu.VMEM((QC, OWNROWS, D), BF16),
            pltpu.VMEM((8, 2, HDIM, D), BF16),
            pltpu.VMEM((8, 2, QC, OWNROWS, HDIM), BF16),
            dma((6,)),
            *sems,
        ],
        compiler_params=pltpu.CompilerParams(
            collective_id=0, has_side_effects=True, vmem_limit_bytes=65 * 1000 * 1000
        ),
    )(edge_weight, pattern.T, node_features, w_qkv, w_out.T, bias_gain, bias_rate)
    return mixed.reshape(ROWS, HDIM)


def solution(mesh):
    in_specs = (P("row", None), P("row", "col"), P("row", "col"), P(), P(None, "col"), P(), P())
    return jax.shard_map(shards, mesh=mesh, in_specs=in_specs, out_specs=P("row", "col"), check_vma=False)
```

```python
import math

import jax
import jax.numpy as jnp
from jax import lax
from jax.experimental import pallas as pl
from jax.experimental.pallas import tpu as pltpu
from jax.sharding import PartitionSpec as P

D = 1024
HEADS = 16
BLK = 128
HDIM = 64
NODES = 6144
ROWS = 768
HALF = 384
QC = 3
CHUNKS = 6
CLS = 4
X_FIRST = (2, 2, 2, 2, 2, 2)
RELAYED = (0, 1, 2, 4, 5)
T_LOAD = 3.9
T_QUERY = (5.0, 4.0, 5.5, 4.5)
T_KEY = (23.5, 19.5, 21.0, 22.0)
T_VALUE = (18.5, 20.0, 20.5, 36.5)
T_FIRST = (0.0, 1.0, 1.5)
T_OWN = (6.5, 14.0, 14.5, 23.0)
T_FAR = (7.0, 17.0, 16.5, 22.5)
T_FEAT = (0.5, 6.0, 12.0, 11.5, 17.5, 18.0)
T_PANEL = (
    (2.0, 2.5, 3.0, 3.5, 10.0, 11.0),
    (7.5, 8.0, 8.5, 9.0, 15.0, 16.0),
    (9.5, 10.5, 12.5, 13.0, 25.0, 28.5),
    (13.5, 15.5, 19.0, 21.5, 34.5, 37.0),
    (24.0, 27.5, 30.0, 31.5, 38.5, 41.0),
)
T_SCORE = (24.5, 26.0, 27.0, 29.0, 29.5, 30.5, 31.0, 32.5, 33.0, 33.5, 34.0, 36.0)
T_READY = 26.5
T_ONE = (
    (1, 0, (0, 128), 28.0), (2, 1, (0, 128), 32.0), (3, 2, (0, 64), 39.0), (6, 2, (64, 64), 41.5)
)
T_LATE = {
    1: (35.5, 35.0, 39.5, 40.0),
    2: (37.5, 38.0, 42.5, 44.0),
    3: (43.0, 43.5, 45.0, 46.5),
    6: (46.0, 45.5, 47.0, 47.5),
}
T_TWO = (((0, 1), 0, True, 40.5), ((2,), 0, True, 42.0), ((0, 1, 2), 1, False, 44.5))
FAMILY = (0, 1, 1, 1, 2, 0, 1)
PIECE = 16
KEYROWS = 48
OWNROWS = 16
LOG2E = 1.4426950408889634
BIG = 1e30
MESH = pl.DeviceIdType.MESH
F32 = jnp.float32
BF16 = jnp.bfloat16


class Place:
    def __init__(self):
        r = lax.axis_index("row")
        c = lax.axis_index("col")
        self.zh, self.y = r // 4, r % 4
        self.zl, self.x, self.core = c // 8, (c // 2) % 4, c % 2
        self.z = 2 * self.zh + self.zl

    def at(self, x=None, y=None, z=None, core=None):
        x = self.x if x is None else x
        y = self.y if y is None else y
        z = self.z if z is None else z
        core = self.core if core is None else core
        return ((z // 2) * 4 + y, ((z % 2) * 4 + x) * 2 + core)


def remote(src, dst, send, recv, device):
    return pltpu.make_async_remote_copy(
        src_ref=src, dst_ref=dst, send_sem=send, recv_sem=recv, device_id=device, device_id_type=MESH
    )


def fused_kernel(
    edge, pattern, feat, w_qkv, w_out_t, gain, rate, out,
    panel, r1, r2, acc, staged, landed, adj, first, mrows, mboth, first_sib, keys, own_feat, w_all, edge_v,
    query, key_proj, value_proj, scores, bias_in, numer, numer_all, stats, stats_all, att, w_cols, mix,
    loc_sem, a_send, a_recv, on_send, on_recv, i_send, i_recv, m_send, m_recv,
    y_send, y_recv, s_send, s_recv, f_send, f_recv, o_send, o_recv,
    n_send, n_recv, t_send, t_recv, w_send, w_recv, x_send, x_recv,
):
    me = Place()
    x, y, z, zh, zl, core = me.x, me.y, me.z, me.zh, me.zl, me.core
    sibling = me.at(core=1 - core)
    spot = zl * 4 + x
    ring = {
        "x+": me.at(x=(x + 1) % 4), "x-": me.at(x=(x + 3) % 4),
        "z+": me.at(z=(z + 1) % 4), "z-": me.at(z=(z + 3) % 4),
    }
    turned = (zl * 4 + x, (zh * 4 + y) * 2 + core)
    turned_self = (zl == zh) & (x == y)

    def chip(k, who=None):
        other = (spot + k) % 8
        return other, me.at(x=other % 4, z=2 * zh + other // 4, core=who)

    def y_peer(k):
        return me.at(y=(y + k) % 4)

    cross = (z + 2 * zl + 3) % 4
    friends = [sibling, me.at(z=cross, core=0), me.at(z=cross, core=1)]
    friends += [((1 - zl) * 4 + x, (zh * 4 + y) * 2 + core), (zl * 4 + x, ((1 - zh) * 4 + y) * 2 + core)]
    friends += [y_peer(k) for k in (1, 2, 3)]
    friends += [chip(k, who)[1] for k in range(1, 8) for who in (core, 1 - core)]
    barrier = pltpu.get_barrier_semaphore()
    for device in friends:
        pl.semaphore_signal(barrier, inc=1, device_id=device, device_id_type=MESH)

    @pl.when(jnp.logical_not(turned_self))
    def _():
        pl.semaphore_signal(barrier, inc=1, device_id=turned, device_id_type=MESH)

    sends = []

    def go(copy):
        copy.start()
        sends.append(copy)

    def arrived(ref, sem):
        pltpu.make_async_copy(ref, ref, sem).wait()

    loads = {
        "edge": pltpu.make_async_copy(edge, edge_v, loc_sem.at[0]),
        "feat": pltpu.make_async_copy(
            feat.at[pl.ds(pl.multiple_of(core * HALF, HALF), HALF)], own_feat, loc_sem.at[1]
        ),
        "w": pltpu.make_async_copy(w_qkv, w_all, loc_sem.at[2]),
    }
    for load in loads.values():
        load.start()
    loads["edge"].wait()

    same = (zl * 4 + x == zh * 4 + y)
    for rb in range(6):
        for cb in range(3):
            on = jnp.where(pattern[cb, rb] > 0, F32(1.0), F32(0.0))
            kept = edge_v[pl.ds(rb * BLK, BLK), pl.ds(cb * BLK, BLK)] * on.astype(BF16)
            adj[pl.ds(rb * 8, 8), cb] = kept.reshape(8, PIECE, BLK)
            row = lax.broadcasted_iota(jnp.int32, (BLK, BLK), 0) + rb * BLK
            col = lax.broadcasted_iota(jnp.int32, (BLK, BLK), 1) + cb * BLK + core * HALF
            diagonal = jnp.where((row == col) & same, F32(0.15), F32(0.0))
            value = (diagonal + F32(0.1275) * kept.astype(F32)) * on
            first[rb // 3, rb % 3, :, pl.ds(cb * BLK, BLK)] = value.astype(BF16)
            mboth[core, pl.ds(rb, 1), pl.ds(cb * BLK, BLK)] = jnp.full((1, BLK), on, F32)
    mask = mboth.at[core]

    pl.semaphore_wait(barrier, len(friends) + jnp.where(turned_self, 0, 1))

    goal = 2 * core + 1 - zl

    def first_copy(qc, mine):
        src = first.at[core, qc] if mine else first_sib.at[qc]
        way = core if mine else 1 - core
        dst = r1.at[y, zh, qc, core]
        return remote(src, dst, i_send.at[0 if mine else 1], i_recv.at[zh], me.at(z=2 * way + 1 - zl))

    def send_first(qc):
        if qc == 0:
            arrived(first_sib, on_recv.at[2])
        for mine in (True, False):
            first_copy(qc, mine).start()

    def first_sent():
        for n in range(2):
            arrived(first.at[0], i_send.at[n])
        for half in range(2):
            remote(mask, mrows.at[zh], m_send.at[half], m_recv.at[zh], me.at(z=goal, core=half)).wait_send()

    for half in range(2):
        remote(mask, mrows.at[zh], m_send.at[half], m_recv.at[zh], me.at(z=goal, core=half)).start()

    def own(who):
        return panel.at[:, z, pl.ds(x * 3, 3), :, pl.ds(pl.multiple_of(who * 128, 128), 128)]

    rows24 = CHUNKS * CLS
    here = pltpu.make_async_copy(adj.at[pl.ds(core * rows24, rows24)], own(core), loc_sem.at[3])
    here.start()
    over = remote(adj.at[pl.ds((1 - core) * rows24, rows24)], own(core), on_send.at[0], on_recv.at[0], sibling)
    go(over)
    go(remote(first.at[1 - core], first_sib, on_send.at[2], on_recv.at[2], sibling))
    go(remote(mask, mask, on_send.at[1], on_recv.at[1], sibling))

    mine = pl.ds(pl.multiple_of(spot * 2 * KEYROWS + core * KEYROWS, KEYROWS), KEYROWS)

    def scatter_keys(waiting=False):
        for block in range(2):
            is_self = turned_self & (zh == block)
            dst = keys.at[zl, x, core]
            if not waiting:
                @pl.when(is_self)
                def _():
                    pltpu.make_async_copy(feat.at[mine], dst, f_recv.at[zl]).start()

            @pl.when(jnp.logical_not(is_self))
            def _():
                device = (block * 4 + x, (zh * 4 + y) * 2 + core)
                copy = remote(feat.at[mine], dst, f_send.at[block], f_recv.at[zl], device)
                if waiting:
                    copy.wait_send()
                else:
                    copy.start()

    here.wait()
    over.wait_recv()

    def a_copy(j, cls, leg, kind):
        sign = 1 if cls % 2 == 0 else -1
        along_x = (cls < X_FIRST[j]) == (leg == 0)
        head = sign if kind != 1 else -sign
        device = ring[("x" if along_x else "z") + ("+" if head == 1 else "-")]
        hop = -sign if kind == 2 else 0
        jc = j * CLS + cls
        if along_x:
            at_x = (x + hop + 8) % 4
            cols = pl.ds(at_x * 3, 3)
            ref = panel.at[jc, z, cols] if leg == 0 else panel.at[jc, :, cols]
        else:
            at_z = (z + hop + 8) % 4
            ref = panel.at[jc, at_z, pl.ds(x * 3, 3)] if leg == 0 else panel.at[jc, at_z]
        step = j * 4 + leg * 2 + (0 if kind == 0 else 1)
        return remote(ref, ref, a_send.at[leg], a_recv.at[step], device)

    def a_stage(j, stage):
        if stage > 0:
            four = pl.ds(j * CLS, CLS)
            ref = {
                1: panel.at[four, 0, pl.ds(0, 3)], 2: panel.at[four, 0, pl.ds(0, 6)],
                3: panel.at[four, 0], 4: panel.at[four, pl.ds(0, 2)],
            }[stage]
            arrived(ref, a_recv.at[j * 4 + stage - 1])
        for cls in range(CLS):
            for kind in ((), (2,), (0, 1), (2,), ())[stage] if stage else (0, 1):
                a_copy(j, cls, stage // 2, kind).start()

    def y_copy(base, cut, k, arriving):
        ref = cut((y - k + 4) % 4 if arriving else y, core)
        return remote(ref, ref, y_send.at[FAMILY[base]], y_recv.at[base * 3 + k - 1], y_peer(k))

    def y_share(base, cut, k):
        ref = cut((y - k + 4) % 4, core)
        remote(ref, ref, s_send.at[FAMILY[base]], s_recv.at[base], sibling).start()

    def y_begin(base, cut, peers=(1, 3, 2)):
        for k in peers:
            y_copy(base, cut, k, False).start()
        y_share(base, cut, 0)

    def y_pass(base, cut, k, relay=None):
        y_copy(base, cut, k, True).wait_recv()
        if relay is not None:
            ref = relay((y - k + 4) % 4, core)
            remote(ref, ref, y_send.at[FAMILY[base]], y_recv.at[base * 3 + 1], y_peer(k)).start()
        y_share(base, cut, k)

    def y_done(base, ref):
        arrived(ref, s_recv.at[base])

    def cut1(a):
        return lambda at_y, who: r1.at[at_y, a, :, who]

    def cut2(q, part, a=slice(None)):
        rows = pl.ds(part[0], part[1])
        return lambda at_y, who: r2.at[at_y, a, q, who, rows]

    def cutk(at_y, who, a=slice(None)):
        return keys.at[a, at_y, who]

    def lhs(q, m, h, kc, part=(0, BLK)):
        pieces = pl.ds(q * 8 + part[0] // PIECE, part[1] // PIECE)
        top = panel[pieces, h, m * 3 + kc].reshape(part[1], 256)
        low = panel[pieces, 2 + h, m * 3 + kc].reshape(part[1], 256)
        return jnp.concatenate([top, low], axis=0)

    def diag(a, q, part):
        row = lax.broadcasted_iota(jnp.int32, (part[1], HALF), 0) + (q * BLK + part[0])
        col = lax.broadcasted_iota(jnp.int32, (part[1], HALF), 1)
        own_block = (1 - zl == a) & (y == x) & (core == zh)
        return jnp.where((row == col) & own_block, F32(0.15), F32(0.0))

    def masked_ranks(a, q, total, part=(0, BLK)):
        keep = mrows[a, pl.ds(core * 3 + q, 1), :] > 0.5
        return jnp.where(keep, diag(a, q, part) + 0.85 * total, 0.0).astype(BF16)

    def sweep_one(q, part):
        size = part[1]

        total = None
        for m in range(4):
            for h in range(2):
                for kc in range(3):
                    rhs = r1[m, h, kc].reshape(256, HALF)
                    product = jnp.dot(lhs(q, m, h, kc, part), rhs, preferred_element_type=F32)
                    total = product if total is None else total + product
        for a in range(2):
            value = masked_ranks(a, q, total[a * size:(a + 1) * size], part)
            r2[y, a, q, core, pl.ds(part[0], size)] = value

    def sweep_two(rows, kc, start):
        for q in rows:
            total = None if start else acc[q]
            for m in range(4):
                for h in range(2):
                    part = jnp.dot(lhs(q, m, h, kc), r2[m, h, kc].reshape(256, HALF), preferred_element_type=F32)
                    total = part if total is None else total + part
            acc[q] = total

    def project(dst, src, first_col, n):
        def body(t, _):
            cols = pl.ds(pl.multiple_of(t * 256, 256), 256)
            w = w_all[:, pl.ds(pl.multiple_of(first_col + t * 256, 256), 256)]
            dst[:, cols] = jnp.dot(src, w, preferred_element_type=F32).astype(BF16)
            return 0

        lax.fori_loop(n, n + 1, body, 0)

    lane = lax.broadcasted_iota(jnp.int32, (BLK, BLK), 1)

    def score_block(t):
        pair, row = t // QC, t % QC
        cols = pl.ds(pl.multiple_of(pair * BLK, BLK), BLK)
        rows = pl.ds(pl.multiple_of(row * BLK, BLK), BLK)
        q2 = query[rows, cols]
        k2 = key_proj[:, cols]
        away = [jnp.where(mboth[c, pl.ds(core * 3 + row, 1), :] > 0.5, F32(0.0), F32(-BIG)) for c in range(2)]
        away = jnp.concatenate(away, axis=1)
        kept = stats[rows, :]
        for side in range(2):
            head = pair * 2 + side
            q1 = jnp.where(lane // HDIM == side, q2, jnp.zeros_like(q2))
            s = lax.dot_general(q1, k2, (((1,), (1,)), ((), ())), preferred_element_type=F32)
            s = s * F32(LOG2E / math.sqrt(HDIM)) + away
            top = jnp.maximum(jnp.max(s, axis=1, keepdims=True), F32(-1e29))
            scores[head, rows, :] = s - top
            kept = jnp.where(lane == HEADS + head, top, kept)
        stats[rows, :] = kept

    def score_blocks(low, high):
        def body(t, _):
            score_block(t)
            return 0

        lax.fori_loop(low, high, body, 0)

    def expo_block(pair, row):
        cols = pl.ds(pl.multiple_of(pair * BLK, BLK), BLK)
        rows = pl.ds(pl.multiple_of(row * BLK, BLK), BLK)
        v2 = value_proj[:, cols]
        spread = bias_in[rows, :]
        both = []
        kept = stats[rows, :]
        for side in range(2):
            head = pair * 2 + side
            bias = (gain[head] * F32(LOG2E)) * jnp.tanh(spread * rate[head])
            e = jnp.exp2(scores[head, rows, :] + bias)
            kept = jnp.where(lane == head, jnp.sum(e, axis=1, keepdims=True), kept)
            both.append(jnp.dot(e.astype(BF16), v2, preferred_element_type=F32))
        stats[rows, :] = kept
        numer[rows, cols] = jnp.where(lane < HDIM, both[0], both[1]).astype(BF16)

    events = []

    def plan(when, what):
        events.append((when, len(events), what))

    def load_weights():
        loads["feat"].wait()
        loads["w"].wait()
        stats[...] = jnp.zeros_like(stats)

    def begin_ranks(base, a):
        pltpu.make_async_copy(first.at[0], r1.at[y, a, :, core], i_recv.at[a]).wait()
        y_begin(base, cut1(a), (1, 3) if base in RELAYED else (1, 3, 2))

    def begin_keys():
        for block in range(2):
            arrived(keys.at[block, y, core], f_recv.at[block])
        y_begin(4, cutk, (1, 3) if 4 in RELAYED else (1, 3, 2))

    plan(T_LOAD, load_weights)
    for n in range(4):
        plan(T_QUERY[n], lambda n=n: project(query, own_feat[...], 0, n))
        plan(T_KEY[n], lambda n=n: project(key_proj, keys[...].reshape(ROWS, D), D, n))
        plan(T_VALUE[n], lambda n=n: project(value_proj, keys[...].reshape(ROWS, D), 2 * D, n))
    for base, times in ((0, T_OWN), (5, T_FAR)):
        a = base // 5
        plan(times[0], lambda base=base, a=a: begin_ranks(base, a))
        for k, when in zip((1, 3, 2), times[1:]):
            relay = cut1(a) if base in RELAYED and k == 1 + 2 * a else None
            plan(when, lambda base=base, a=a, k=k, relay=relay: y_pass(base, cut1(a), k, relay))
    plan(T_FEAT[0], scatter_keys)
    for qc in range(QC):
        plan(T_FIRST[qc], lambda qc=qc: send_first(qc))
    plan(T_FEAT[1], begin_keys)
    for k, when in zip((1, 3, 2), T_FEAT[2:5]):
        relay = None
        if 4 in RELAYED and k != 2:
            relay = lambda at_y, who, k=k: cutk(at_y, who, k // 2)
        plan(when, lambda k=k, relay=relay: y_pass(4, cutk, k, relay))
    plan(T_FEAT[5], lambda: y_done(4, keys.at[:, :, 0]))
    for j in range(CHUNKS):
        for stage in range(5):
            plan(T_PANEL[stage][j], lambda j=j, stage=stage: a_stage(j, stage))

    def ready():
        y_done(0, r1.at[:, 0, :, 0])
        y_done(5, r1.at[:, 0, :, 0])
        for a in range(2):
            pltpu.make_async_copy(mask, mrows.at[a], m_recv.at[a]).wait()

    plan(T_SCORE[0] - 0.1, lambda: remote(mask, mboth.at[1 - core], on_send.at[1], on_recv.at[1], sibling).wait_recv())
    for n, when in enumerate(T_SCORE):
        plan(when, lambda n=n: score_blocks(2 * n, 2 * n + 2))
    plan(T_READY, ready)
    for base, q, part, when in T_ONE:
        peers = (1, 3) if base in RELAYED else (1, 3, 2)

        def first_sweep(base=base, q=q, part=part, peers=peers):
            sweep_one(q, part)
            y_begin(base, cut2(q, part), peers)

        plan(when, first_sweep)
        for k, late in zip((1, 3, 2), T_LATE[base]):
            relay = cut2(q, part, k // 2) if k != 2 and len(peers) == 2 else None
            plan(late, lambda base=base, q=q, part=part, k=k, relay=relay: y_pass(base, cut2(q, part), k, relay))
        rows = pl.ds(part[0], part[1])
        plan(T_LATE[base][3], lambda base=base, q=q, rows=rows: y_done(base, r2.at[:, :, q, 0, rows]))
    for rows, kc, start, when in T_TWO:
        plan(when, lambda rows=rows, kc=kc, start=start: sweep_two(rows, kc, start))

    quarter = pl.ds(pl.multiple_of(y * 256, 256), 256)

    def send_weights():
        src, dst = w_out_t.at[:, quarter], w_cols.at[spot, core, :, quarter]
        for k in range(1, 8):
            remote(src, dst, w_send.at[0], w_recv.at[0], chip(k)[1]).start()
        pltpu.make_async_copy(src, dst, loc_sem.at[4]).start()

    def cross_weights():
        ref = w_cols.at[:, core, :, quarter]
        arrived(w_cols.at[spot, core, :, quarter], loc_sem.at[4])
        arrived(w_cols.at[pl.ds(0, 7), 0, :, pl.ds(0, 256)], w_recv.at[0])
        for k in (1, 3, 2):
            remote(ref, ref, w_send.at[2], w_recv.at[2], y_peer(k)).start()

    plan(T_PANEL[3][5] + 0.01, send_weights)
    for _, _, what in sorted(events, key=lambda e: e[:2]):
        what()

    for q in range(QC):
        sweep_two((q,), 2, False)
        for a in range(2):
            staged[a, q] = masked_ranks(a, q, acc[q, a * BLK:(a + 1) * BLK])
        for a in range(2):
            dst = landed.at[zh, q]
            go(remote(staged.at[a, q], dst, o_send.at[2 * q + a], o_recv.at[2 * q + zh], me.at(z=2 * a + 1 - zl)))

    cross_weights()

    def forward_weights():
        arrived(w_cols.at[:, 0, :, pl.ds(0, 768)], w_recv.at[2])
        ref = w_cols.at[:, core]
        remote(ref, ref, w_send.at[1], w_recv.at[1], sibling).start()

    def widen(ref, half, q):
        cols = pl.ds(half * HALF, HALF)
        bias_in[pl.ds(q * BLK, BLK), cols] = ref[q].astype(F32) * F32(math.sqrt(NODES))

    def owned(q, at):
        return pl.ds(pl.multiple_of(q * BLK + at * OWNROWS, OWNROWS), OWNROWS)

    def attend(q):
        for half in range(2):
            arrived(landed.at[half, q], o_recv.at[2 * q + half])
            widen(landed.at[half], half, q)

        def body(t, _):
            expo_block(t, q)
            return 0

        lax.fori_loop(0, HEADS // 2, body, 0)
        for k in range(1, 8):
            other, device = chip(k)
            rows = owned(q, other)
            remote(numer.at[rows], numer_all.at[spot, q], n_send.at[0], n_recv.at[q], device).start()
            remote(stats.at[rows], stats_all.at[spot, q], t_send.at[0], t_recv.at[q], device).start()
        numer_all[spot, q] = numer[owned(q, spot), :]
        stats_all[spot, q] = stats[owned(q, spot), :]

    low = lax.broadcasted_iota(jnp.int32, (OWNROWS, BLK), 1) < HDIM

    def combine(q):
        arrived(stats_all.at[pl.ds(0, 7), q], t_recv.at[q])
        arrived(numer_all.at[pl.ds(0, 7), q], n_recv.at[q])
        table = [stats_all[s, q] for s in range(8)]
        tops = [t[:, HEADS:2 * HEADS] for t in table]
        peak = tops[0]
        for t in tops[1:]:
            peak = jnp.maximum(peak, t)
        weights = [jnp.exp2(t - peak) for t in tops]
        total = weights[0] * table[0][:, :HEADS]
        for s in range(1, 8):
            total = total + weights[s] * table[s][:, :HEADS]
        weights = [w / total for w in weights]
        for pair in range(HEADS // 2):
            cols = pl.ds(pair * BLK, BLK)
            value = jnp.zeros((OWNROWS, BLK), F32)
            for s in range(8):
                w = jnp.where(low, weights[s][:, 2 * pair:2 * pair + 1], weights[s][:, 2 * pair + 1:2 * pair + 2])
                value = value + w * numer_all[s, q, :, cols].astype(F32)
            att[q, :, cols] = value.astype(BF16)

    for q in range(QC):
        attend(q)
    forward_weights()
    for q in range(QC):
        combine(q)

    arrived(w_cols.at[:, 0], w_recv.at[1])
    mixed = lax.dot_general(
        att[...].reshape(KEYROWS, D), w_cols[...].reshape(D, D), (((1,), (1,)), ((), ())), preferred_element_type=F32
    ).astype(BF16)
    for c in range(2 * 8):
        mix[c // 2, c % 2] = mixed[:, c * HDIM:(c + 1) * HDIM].reshape(QC, OWNROWS, HDIM)

    def rows_of(who, at):
        return out.at[who, :, pl.ds(pl.multiple_of(at * OWNROWS, OWNROWS), OWNROWS)]

    for k in range(8):
        for flip in range(2):
            if k == 0 and flip == 0:
                continue
            other, device = chip(k, (core + flip) % 2)
            src = mix.at[other, (core + flip) % 2]
            remote(src, rows_of(core, spot), x_send.at[flip], x_recv.at[flip], device).start()
    last = pltpu.make_async_copy(mix.at[spot, core], rows_of(core, spot), loc_sem.at[5])
    last.start()
    for flip in range(2):
        arrived(mix.at[pl.ds(0, 7 + flip), 0], x_recv.at[flip])
    last.wait()
    for send in sends:
        send.wait_send()
    for flip in range(2):
        arrived(mix.at[pl.ds(0, 7 + flip), 0], x_send.at[flip])
    arrived(panel.at[:, 0, pl.ds(0, 9)], a_send.at[0])
    arrived(panel.at[:, pl.ds(0, 3)], a_send.at[1])
    arrived(w_cols.at[pl.ds(0, 7), 0, :, pl.ds(0, 256)], w_send.at[0])
    arrived(w_cols.at[:, 0], w_send.at[1])
    arrived(w_cols.at[:, 0, :, pl.ds(0, 768)], w_send.at[2])
    three = pl.ds(0, 3)
    for n, ref in enumerate((r1.at[three, :, :, 0], r2.at[three, :, :, 0], keys.at[:, three, 0])):
        arrived(ref, y_send.at[n])
    for n, ref in enumerate((r1.at[:, :, :, 0], r2.at[:, :, :, 0], keys.at[:, :, 0])):
        arrived(ref, s_send.at[n])
    arrived(numer_all.at[pl.ds(0, 7)], n_send.at[0])
    arrived(stats_all.at[pl.ds(0, 7)], t_send.at[0])
    first_sent()

    scatter_keys(waiting=True)


def shards(node_features, edge_weight, pattern, w_qkv, w_out, bias_gain, bias_rate):
    dma = pltpu.SemaphoreType.DMA
    anywhere = pl.BlockSpec(memory_space=pl.ANY)
    vmem = pl.BlockSpec(memory_space=pltpu.VMEM)
    smem = pl.BlockSpec(memory_space=pltpu.SMEM)
    counts = (2, 4 * CHUNKS, 3, 3, 2, 2, 2, 2, 3, 21, 3, 7, 2, 2, 6, 6, 1, QC, 1, QC, 3, 3, 2, 2)
    sems = [dma((n,)) for n in counts]
    mixed = pl.pallas_call(
        fused_kernel,
        name="fused",
        out_shape=jax.ShapeDtypeStruct((2, QC, BLK, HDIM), BF16),
        in_specs=[anywhere, smem, anywhere, anywhere, anywhere, smem, smem],
        out_specs=vmem,
        scratch_shapes=[
            pltpu.VMEM((CHUNKS * CLS, 4, 12, PIECE, 256), BF16),
            pltpu.VMEM((4, 2, QC, 2, BLK, HALF), BF16),
            pltpu.VMEM((4, 2, QC, 2, BLK, HALF), BF16),
            pltpu.VMEM((QC, 2 * BLK, HALF), F32),
            pltpu.VMEM((2, QC, BLK, HALF), BF16),
            pltpu.VMEM((2, QC, BLK, HALF), BF16),
            pltpu.VMEM((2 * CHUNKS * CLS, 3, PIECE, BLK), BF16),
            pltpu.VMEM((2, QC, BLK, HALF), BF16),
            pltpu.VMEM((2, 8, HALF), F32),
            pltpu.VMEM((2, 8, HALF), F32),
            pltpu.VMEM((QC, BLK, HALF), BF16),
            pltpu.VMEM((2, 4, 2, KEYROWS, D), BF16),
            pltpu.VMEM((HALF, D), BF16),
            pltpu.VMEM((D, 3 * D), BF16),
            pltpu.VMEM((ROWS, HALF), BF16),
            pltpu.VMEM((HALF, D), BF16),
            pltpu.VMEM((ROWS, D), BF16),
            pltpu.VMEM((ROWS, D), BF16),
            pltpu.VMEM((HEADS, HALF, ROWS), F32),
            pltpu.VMEM((HALF, ROWS), F32),
            pltpu.VMEM((HALF, D), BF16),
            pltpu.VMEM((8, QC, OWNROWS, D), BF16),
            pltpu.VMEM((HALF, BLK), F32),
            pltpu.VMEM((8, QC, OWNROWS, BLK), F32),
            pltpu.VMEM((QC, OWNROWS, D), BF16),
            pltpu.VMEM((8, 2, HDIM, D), BF16),
            pltpu.VMEM((8, 2, QC, OWNROWS, HDIM), BF16),
            dma((6,)),
            *sems,
        ],
        compiler_params=pltpu.CompilerParams(
            collective_id=0, has_side_effects=True, vmem_limit_bytes=65 * 1000 * 1000
        ),
    )(edge_weight, pattern.T, node_features, w_qkv, w_out.T, bias_gain, bias_rate)
    return mixed.reshape(ROWS, HDIM)


def solution(mesh):
    in_specs = (P("row", None), P("row", "col"), P("row", "col"), P(), P(None, "col"), P(), P())
    return jax.shard_map(shards, mesh=mesh, in_specs=in_specs, out_specs=P("row", "col"), check_vma=False)
```

```python
import math

import jax
import jax.numpy as jnp
from jax import lax
from jax.experimental import pallas as pl
from jax.experimental.pallas import tpu as pltpu
from jax.sharding import PartitionSpec as P

D = 1024
HEADS = 16
BLK = 128
HDIM = 64
NODES = 6144
ROWS = 768
HALF = 384
QC = 3
CHUNKS = 6
CLS = 4
X_FIRST = (2, 2, 2, 2, 2, 2)
RELAYED = (0, 1, 2, 4, 5)
T_LOAD = 3.9
T_QUERY = (5.0, 4.0, 5.5, 4.5)
T_KEY = (23.5, 19.5, 21.0, 22.0)
T_VALUE = (18.5, 20.0, 20.5, 36.5)
T_FIRST = (0.0, 1.0, 1.5)
T_OWN = (9.7, 14.0, 14.5, 23.0)
T_FAR = (9.8, 17.0, 16.5, 22.5)
T_FEAT = (0.5, 9.6, 12.0, 11.5, 17.5, 18.0)
T_PANEL = (
    (2.0, 2.5, 3.0, 3.5, 10.0, 11.0),
    (7.5, 8.0, 8.5, 9.0, 15.0, 16.0),
    (9.5, 10.5, 12.5, 13.0, 25.0, 28.5),
    (13.5, 15.5, 19.0, 21.5, 34.5, 37.0),
    (24.0, 27.5, 30.0, 31.5, 38.5, 41.0),
)
T_SCORE = (24.5, 26.0, 27.0, 29.0, 29.5, 30.5, 31.0, 32.5, 33.0, 33.5, 34.0, 36.0)
T_READY = 26.5
T_ONE = (
    (1, 0, (0, 128), 28.0), (2, 1, (0, 128), 32.0), (3, 2, (0, 64), 39.0), (6, 2, (64, 64), 41.5)
)
T_LATE = {
    1: (35.5, 35.0, 39.5, 40.0),
    2: (37.5, 38.0, 42.5, 44.0),
    3: (43.0, 43.5, 45.0, 46.5),
    6: (46.0, 45.5, 47.0, 47.5),
}
T_TWO = (((0, 1), 0, True, 40.5), ((2,), 0, True, 42.0), ((0, 1, 2), 1, False, 44.5))
FAMILY = (0, 1, 1, 1, 2, 0, 1)
PIECE = 16
KEYROWS = 48
OWNROWS = 16
LOG2E = 1.4426950408889634
BIG = 1e30
MESH = pl.DeviceIdType.MESH
F32 = jnp.float32
BF16 = jnp.bfloat16


class Place:
    def __init__(self):
        r = lax.axis_index("row")
        c = lax.axis_index("col")
        self.zh, self.y = r // 4, r % 4
        self.zl, self.x, self.core = c // 8, (c // 2) % 4, c % 2
        self.z = 2 * self.zh + self.zl

    def at(self, x=None, y=None, z=None, core=None):
        x = self.x if x is None else x
        y = self.y if y is None else y
        z = self.z if z is None else z
        core = self.core if core is None else core
        return ((z // 2) * 4 + y, ((z % 2) * 4 + x) * 2 + core)


def remote(src, dst, send, recv, device):
    return pltpu.make_async_remote_copy(
        src_ref=src, dst_ref=dst, send_sem=send, recv_sem=recv, device_id=device, device_id_type=MESH
    )


def fused_kernel(
    edge, pattern, feat, w_qkv, w_out_t, gain, rate, out,
    panel, r1, r2, acc, staged, landed, adj, first, mrows, mboth, first_sib, keys, own_feat, w_all, edge_v,
    query, key_proj, value_proj, scores, bias_in, numer, numer_all, stats, stats_all, att, w_cols, mix,
    loc_sem, a_send, a_recv, on_send, on_recv, i_send, i_recv, m_send, m_recv,
    y_send, y_recv, s_send, s_recv, f_send, f_recv, o_send, o_recv,
    n_send, n_recv, t_send, t_recv, w_send, w_recv, x_send, x_recv,
):
    me = Place()
    x, y, z, zh, zl, core = me.x, me.y, me.z, me.zh, me.zl, me.core
    sibling = me.at(core=1 - core)
    spot = zl * 4 + x
    ring = {
        "x+": me.at(x=(x + 1) % 4), "x-": me.at(x=(x + 3) % 4),
        "z+": me.at(z=(z + 1) % 4), "z-": me.at(z=(z + 3) % 4),
    }
    turned = (zl * 4 + x, (zh * 4 + y) * 2 + core)
    turned_self = (zl == zh) & (x == y)

    def chip(k, who=None):
        other = (spot + k) % 8
        return other, me.at(x=other % 4, z=2 * zh + other // 4, core=who)

    def y_peer(k):
        return me.at(y=(y + k) % 4)

    cross = (z + 2 * zl + 3) % 4
    friends = [sibling, me.at(z=cross, core=0), me.at(z=cross, core=1)]
    friends += [((1 - zl) * 4 + x, (zh * 4 + y) * 2 + core), (zl * 4 + x, ((1 - zh) * 4 + y) * 2 + core)]
    friends += [y_peer(k) for k in (1, 2, 3)]
    friends += [chip(k, who)[1] for k in range(1, 8) for who in (core, 1 - core)]
    barrier = pltpu.get_barrier_semaphore()
    for device in friends:
        pl.semaphore_signal(barrier, inc=1, device_id=device, device_id_type=MESH)

    @pl.when(jnp.logical_not(turned_self))
    def _():
        pl.semaphore_signal(barrier, inc=1, device_id=turned, device_id_type=MESH)

    sends = []

    def go(copy):
        copy.start()
        sends.append(copy)

    def arrived(ref, sem):
        pltpu.make_async_copy(ref, ref, sem).wait()

    loads = {
        "edge": pltpu.make_async_copy(edge, edge_v, loc_sem.at[0]),
        "feat": pltpu.make_async_copy(
            feat.at[pl.ds(pl.multiple_of(core * HALF, HALF), HALF)], own_feat, loc_sem.at[1]
        ),
        "w": pltpu.make_async_copy(w_qkv, w_all, loc_sem.at[2]),
    }
    for load in loads.values():
        load.start()
    loads["edge"].wait()

    same = (zl * 4 + x == zh * 4 + y)
    for rb in range(6):
        for cb in range(3):
            on = jnp.where(pattern[cb, rb] > 0, F32(1.0), F32(0.0))
            kept = edge_v[pl.ds(rb * BLK, BLK), pl.ds(cb * BLK, BLK)] * on.astype(BF16)
            adj[pl.ds(rb * 8, 8), cb] = kept.reshape(8, PIECE, BLK)
            row = lax.broadcasted_iota(jnp.int32, (BLK, BLK), 0) + rb * BLK
            col = lax.broadcasted_iota(jnp.int32, (BLK, BLK), 1) + cb * BLK + core * HALF
            diagonal = jnp.where((row == col) & same, F32(0.15), F32(0.0))
            value = (diagonal + F32(0.1275) * kept.astype(F32)) * on
            first[rb // 3, rb % 3, :, pl.ds(cb * BLK, BLK)] = value.astype(BF16)
            mboth[core, pl.ds(rb, 1), pl.ds(cb * BLK, BLK)] = jnp.full((1, BLK), on, F32)
    mask = mboth.at[core]

    pl.semaphore_wait(barrier, len(friends) + jnp.where(turned_self, 0, 1))

    goal = 2 * core + 1 - zl

    def first_copy(qc, mine):
        src = first.at[core, qc] if mine else first_sib.at[qc]
        way = core if mine else 1 - core
        dst = r1.at[y, zh, qc, core]
        return remote(src, dst, i_send.at[0 if mine else 1], i_recv.at[zh], me.at(z=2 * way + 1 - zl))

    def send_first(qc):
        if qc == 0:
            arrived(first_sib, on_recv.at[2])
        for mine in (True, False):
            first_copy(qc, mine).start()

    def first_sent():
        for n in range(2):
            arrived(first.at[0], i_send.at[n])
        for half in range(2):
            remote(mask, mrows.at[zh], m_send.at[half], m_recv.at[zh], me.at(z=goal, core=half)).wait_send()

    for half in range(2):
        remote(mask, mrows.at[zh], m_send.at[half], m_recv.at[zh], me.at(z=goal, core=half)).start()

    def own(who):
        return panel.at[:, z, pl.ds(x * 3, 3), :, pl.ds(pl.multiple_of(who * 128, 128), 128)]

    rows24 = CHUNKS * CLS
    here = pltpu.make_async_copy(adj.at[pl.ds(core * rows24, rows24)], own(core), loc_sem.at[3])
    here.start()
    over = remote(adj.at[pl.ds((1 - core) * rows24, rows24)], own(core), on_send.at[0], on_recv.at[0], sibling)
    go(over)
    go(remote(first.at[1 - core], first_sib, on_send.at[2], on_recv.at[2], sibling))
    go(remote(mask, mask, on_send.at[1], on_recv.at[1], sibling))

    mine = pl.ds(pl.multiple_of(spot * 2 * KEYROWS + core * KEYROWS, KEYROWS), KEYROWS)

    def scatter_keys(waiting=False):
        for block in range(2):
            is_self = turned_self & (zh == block)
            dst = keys.at[zl, x, core]
            if not waiting:
                @pl.when(is_self)
                def _():
                    pltpu.make_async_copy(feat.at[mine], dst, f_recv.at[zl]).start()

            @pl.when(jnp.logical_not(is_self))
            def _():
                device = (block * 4 + x, (zh * 4 + y) * 2 + core)
                copy = remote(feat.at[mine], dst, f_send.at[block], f_recv.at[zl], device)
                if waiting:
                    copy.wait_send()
                else:
                    copy.start()

    here.wait()
    over.wait_recv()

    def a_copy(j, cls, leg, kind):
        sign = 1 if cls % 2 == 0 else -1
        along_x = (cls < X_FIRST[j]) == (leg == 0)
        head = sign if kind != 1 else -sign
        device = ring[("x" if along_x else "z") + ("+" if head == 1 else "-")]
        hop = -sign if kind == 2 else 0
        jc = j * CLS + cls
        if along_x:
            at_x = (x + hop + 8) % 4
            cols = pl.ds(at_x * 3, 3)
            ref = panel.at[jc, z, cols] if leg == 0 else panel.at[jc, :, cols]
        else:
            at_z = (z + hop + 8) % 4
            ref = panel.at[jc, at_z, pl.ds(x * 3, 3)] if leg == 0 else panel.at[jc, at_z]
        step = j * 4 + leg * 2 + (0 if kind == 0 else 1)
        return remote(ref, ref, a_send.at[leg], a_recv.at[step], device)

    def a_stage(j, stage):
        if stage > 0:
            four = pl.ds(j * CLS, CLS)
            ref = {
                1: panel.at[four, 0, pl.ds(0, 3)], 2: panel.at[four, 0, pl.ds(0, 6)],
                3: panel.at[four, 0], 4: panel.at[four, pl.ds(0, 2)],
            }[stage]
            arrived(ref, a_recv.at[j * 4 + stage - 1])
        for cls in range(CLS):
            for kind in ((), (2,), (0, 1), (2,), ())[stage] if stage else (0, 1):
                a_copy(j, cls, stage // 2, kind).start()

    def y_copy(base, cut, k, arriving):
        ref = cut((y - k + 4) % 4 if arriving else y, core)
        return remote(ref, ref, y_send.at[FAMILY[base]], y_recv.at[base * 3 + k - 1], y_peer(k))

    def y_share(base, cut, k):
        ref = cut((y - k + 4) % 4, core)
        remote(ref, ref, s_send.at[FAMILY[base]], s_recv.at[base], sibling).start()

    def y_begin(base, cut, peers=(1, 3, 2)):
        for k in peers:
            y_copy(base, cut, k, False).start()
        y_share(base, cut, 0)

    def y_pass(base, cut, k, relay=None):
        y_copy(base, cut, k, True).wait_recv()
        if relay is not None:
            ref = relay((y - k + 4) % 4, core)
            remote(ref, ref, y_send.at[FAMILY[base]], y_recv.at[base * 3 + 1], y_peer(k)).start()
        y_share(base, cut, k)

    def y_done(base, ref):
        arrived(ref, s_recv.at[base])

    def cut1(a):
        return lambda at_y, who: r1.at[at_y, a, :, who]

    def cut2(q, part, a=slice(None)):
        rows = pl.ds(part[0], part[1])
        return lambda at_y, who: r2.at[at_y, a, q, who, rows]

    def cutk(at_y, who, a=slice(None)):
        return keys.at[a, at_y, who]

    def lhs(q, m, h, kc, part=(0, BLK)):
        pieces = pl.ds(q * 8 + part[0] // PIECE, part[1] // PIECE)
        top = panel[pieces, h, m * 3 + kc].reshape(part[1], 256)
        low = panel[pieces, 2 + h, m * 3 + kc].reshape(part[1], 256)
        return jnp.concatenate([top, low], axis=0)

    def diag(a, q, part):
        row = lax.broadcasted_iota(jnp.int32, (part[1], HALF), 0) + (q * BLK + part[0])
        col = lax.broadcasted_iota(jnp.int32, (part[1], HALF), 1)
        own_block = (1 - zl == a) & (y == x) & (core == zh)
        return jnp.where((row == col) & own_block, F32(0.15), F32(0.0))

    def masked_ranks(a, q, total, part=(0, BLK)):
        keep = mrows[a, pl.ds(core * 3 + q, 1), :] > 0.5
        return jnp.where(keep, diag(a, q, part) + 0.85 * total, 0.0).astype(BF16)

    def sweep_one(q, part):
        size = part[1]

        total = None
        for m in range(4):
            for h in range(2):
                for kc in range(3):
                    rhs = r1[m, h, kc].reshape(256, HALF)
                    product = jnp.dot(lhs(q, m, h, kc, part), rhs, preferred_element_type=F32)
                    total = product if total is None else total + product
        for a in range(2):
            value = masked_ranks(a, q, total[a * size:(a + 1) * size], part)
            r2[y, a, q, core, pl.ds(part[0], size)] = value

    def sweep_two(rows, kc, start):
        for q in rows:
            total = None if start else acc[q]
            for m in range(4):
                for h in range(2):
                    part = jnp.dot(lhs(q, m, h, kc), r2[m, h, kc].reshape(256, HALF), preferred_element_type=F32)
                    total = part if total is None else total + part
            acc[q] = total

    def project(dst, src, first_col, n):
        def body(t, _):
            cols = pl.ds(pl.multiple_of(t * 256, 256), 256)
            w = w_all[:, pl.ds(pl.multiple_of(first_col + t * 256, 256), 256)]
            dst[:, cols] = jnp.dot(src, w, preferred_element_type=F32).astype(BF16)
            return 0

        lax.fori_loop(n, n + 1, body, 0)

    lane = lax.broadcasted_iota(jnp.int32, (BLK, BLK), 1)

    def score_block(t):
        pair, row = t // QC, t % QC
        cols = pl.ds(pl.multiple_of(pair * BLK, BLK), BLK)
        rows = pl.ds(pl.multiple_of(row * BLK, BLK), BLK)
        q2 = query[rows, cols]
        k2 = key_proj[:, cols]
        away = [jnp.where(mboth[c, pl.ds(core * 3 + row, 1), :] > 0.5, F32(0.0), F32(-BIG)) for c in range(2)]
        away = jnp.concatenate(away, axis=1)
        kept = stats[rows, :]
        for side in range(2):
            head = pair * 2 + side
            q1 = jnp.where(lane // HDIM == side, q2, jnp.zeros_like(q2))
            s = lax.dot_general(q1, k2, (((1,), (1,)), ((), ())), preferred_element_type=F32)
            s = s * F32(LOG2E / math.sqrt(HDIM)) + away
            top = jnp.maximum(jnp.max(s, axis=1, keepdims=True), F32(-1e29))
            scores[head, rows, :] = s - top
            kept = jnp.where(lane == HEADS + head, top, kept)
        stats[rows, :] = kept

    def score_blocks(low, high):
        def body(t, _):
            score_block(t)
            return 0

        lax.fori_loop(low, high, body, 0)

    def expo_block(pair, row):
        cols = pl.ds(pl.multiple_of(pair * BLK, BLK), BLK)
        rows = pl.ds(pl.multiple_of(row * BLK, BLK), BLK)
        v2 = value_proj[:, cols]
        spread = bias_in[rows, :]
        both = []
        kept = stats[rows, :]
        for side in range(2):
            head = pair * 2 + side
            bias = (gain[head] * F32(LOG2E)) * jnp.tanh(spread * rate[head])
            e = jnp.exp2(scores[head, rows, :] + bias)
            kept = jnp.where(lane == head, jnp.sum(e, axis=1, keepdims=True), kept)
            both.append(jnp.dot(e.astype(BF16), v2, preferred_element_type=F32))
        stats[rows, :] = kept
        numer[rows, cols] = jnp.where(lane < HDIM, both[0], both[1]).astype(BF16)

    events = []

    def plan(when, what):
        events.append((when, len(events), what))

    def load_weights():
        loads["feat"].wait()
        loads["w"].wait()
        stats[...] = jnp.zeros_like(stats)

    def begin_ranks(base, a):
        pltpu.make_async_copy(first.at[0], r1.at[y, a, :, core], i_recv.at[a]).wait()
        y_begin(base, cut1(a), (1, 3) if base in RELAYED else (1, 3, 2))

    def begin_keys():
        for block in range(2):
            arrived(keys.at[block, y, core], f_recv.at[block])
        y_begin(4, cutk, (1, 3) if 4 in RELAYED else (1, 3, 2))

    plan(T_LOAD, load_weights)
    for n in range(4):
        plan(T_QUERY[n], lambda n=n: project(query, own_feat[...], 0, n))
        plan(T_KEY[n], lambda n=n: project(key_proj, keys[...].reshape(ROWS, D), D, n))
        plan(T_VALUE[n], lambda n=n: project(value_proj, keys[...].reshape(ROWS, D), 2 * D, n))
    for base, times in ((0, T_OWN), (5, T_FAR)):
        a = base // 5
        plan(times[0], lambda base=base, a=a: begin_ranks(base, a))
        for k, when in zip((1, 3, 2), times[1:]):
            relay = cut1(a) if base in RELAYED and k == 1 + 2 * a else None
            plan(when, lambda base=base, a=a, k=k, relay=relay: y_pass(base, cut1(a), k, relay))
    plan(T_FEAT[0], scatter_keys)
    for qc in range(QC):
        plan(T_FIRST[qc], lambda qc=qc: send_first(qc))
    plan(T_FEAT[1], begin_keys)
    for k, when in zip((1, 3, 2), T_FEAT[2:5]):
        relay = None
        if 4 in RELAYED and k != 2:
            relay = lambda at_y, who, k=k: cutk(at_y, who, k // 2)
        plan(when, lambda k=k, relay=relay: y_pass(4, cutk, k, relay))
    plan(T_FEAT[5], lambda: y_done(4, keys.at[:, :, 0]))
    for j in range(CHUNKS):
        for stage in range(5):
            plan(T_PANEL[stage][j], lambda j=j, stage=stage: a_stage(j, stage))

    def ready():
        y_done(0, r1.at[:, 0, :, 0])
        y_done(5, r1.at[:, 0, :, 0])
        for a in range(2):
            pltpu.make_async_copy(mask, mrows.at[a], m_recv.at[a]).wait()

    plan(T_SCORE[0] - 0.1, lambda: remote(mask, mboth.at[1 - core], on_send.at[1], on_recv.at[1], sibling).wait_recv())
    for n, when in enumerate(T_SCORE):
        plan(when, lambda n=n: score_blocks(2 * n, 2 * n + 2))
    plan(T_READY, ready)
    for base, q, part, when in T_ONE:
        peers = (1, 3) if base in RELAYED else (1, 3, 2)

        def first_sweep(base=base, q=q, part=part, peers=peers):
            sweep_one(q, part)
            y_begin(base, cut2(q, part), peers)

        plan(when, first_sweep)
        for k, late in zip((1, 3, 2), T_LATE[base]):
            relay = cut2(q, part, k // 2) if k != 2 and len(peers) == 2 else None
            plan(late, lambda base=base, q=q, part=part, k=k, relay=relay: y_pass(base, cut2(q, part), k, relay))
        rows = pl.ds(part[0], part[1])
        plan(T_LATE[base][3], lambda base=base, q=q, rows=rows: y_done(base, r2.at[:, :, q, 0, rows]))
    for rows, kc, start, when in T_TWO:
        plan(when, lambda rows=rows, kc=kc, start=start: sweep_two(rows, kc, start))

    quarter = pl.ds(pl.multiple_of(y * 256, 256), 256)

    def send_weights():
        src, dst = w_out_t.at[:, quarter], w_cols.at[spot, core, :, quarter]
        for k in range(1, 8):
            remote(src, dst, w_send.at[0], w_recv.at[0], chip(k)[1]).start()
        pltpu.make_async_copy(src, dst, loc_sem.at[4]).start()

    def cross_weights():
        ref = w_cols.at[:, core, :, quarter]
        arrived(w_cols.at[spot, core, :, quarter], loc_sem.at[4])
        arrived(w_cols.at[pl.ds(0, 7), 0, :, pl.ds(0, 256)], w_recv.at[0])
        for k in (1, 3, 2):
            remote(ref, ref, w_send.at[2], w_recv.at[2], y_peer(k)).start()

    plan(T_PANEL[3][5] + 0.01, send_weights)
    for _, _, what in sorted(events, key=lambda e: e[:2]):
        what()

    for q in range(QC):
        sweep_two((q,), 2, False)
        for a in range(2):
            staged[a, q] = masked_ranks(a, q, acc[q, a * BLK:(a + 1) * BLK])
        for a in range(2):
            dst = landed.at[zh, q]
            go(remote(staged.at[a, q], dst, o_send.at[2 * q + a], o_recv.at[2 * q + zh], me.at(z=2 * a + 1 - zl)))

    cross_weights()

    def forward_weights():
        arrived(w_cols.at[:, 0, :, pl.ds(0, 768)], w_recv.at[2])
        ref = w_cols.at[:, core]
        remote(ref, ref, w_send.at[1], w_recv.at[1], sibling).start()

    def widen(ref, half, q):
        cols = pl.ds(half * HALF, HALF)
        bias_in[pl.ds(q * BLK, BLK), cols] = ref[q].astype(F32) * F32(math.sqrt(NODES))

    def owned(q, at):
        return pl.ds(pl.multiple_of(q * BLK + at * OWNROWS, OWNROWS), OWNROWS)

    def attend(q):
        for half in range(2):
            arrived(landed.at[half, q], o_recv.at[2 * q + half])
            widen(landed.at[half], half, q)

        def body(t, _):
            expo_block(t, q)
            return 0

        lax.fori_loop(0, HEADS // 2, body, 0)
        for k in range(1, 8):
            other, device = chip(k)
            rows = owned(q, other)
            remote(numer.at[rows], numer_all.at[spot, q], n_send.at[0], n_recv.at[q], device).start()
            remote(stats.at[rows], stats_all.at[spot, q], t_send.at[0], t_recv.at[q], device).start()
        numer_all[spot, q] = numer[owned(q, spot), :]
        stats_all[spot, q] = stats[owned(q, spot), :]

    low = lax.broadcasted_iota(jnp.int32, (OWNROWS, BLK), 1) < HDIM

    def combine(q):
        arrived(stats_all.at[pl.ds(0, 7), q], t_recv.at[q])
        arrived(numer_all.at[pl.ds(0, 7), q], n_recv.at[q])
        table = [stats_all[s, q] for s in range(8)]
        tops = [t[:, HEADS:2 * HEADS] for t in table]
        peak = tops[0]
        for t in tops[1:]:
            peak = jnp.maximum(peak, t)
        weights = [jnp.exp2(t - peak) for t in tops]
        total = weights[0] * table[0][:, :HEADS]
        for s in range(1, 8):
            total = total + weights[s] * table[s][:, :HEADS]
        weights = [w / total for w in weights]
        for pair in range(HEADS // 2):
            cols = pl.ds(pair * BLK, BLK)
            value = jnp.zeros((OWNROWS, BLK), F32)
            for s in range(8):
                w = jnp.where(low, weights[s][:, 2 * pair:2 * pair + 1], weights[s][:, 2 * pair + 1:2 * pair + 2])
                value = value + w * numer_all[s, q, :, cols].astype(F32)
            att[q, :, cols] = value.astype(BF16)

    for q in range(QC):
        attend(q)
    forward_weights()
    for q in range(QC):
        combine(q)

    arrived(w_cols.at[:, 0], w_recv.at[1])
    mixed = lax.dot_general(
        att[...].reshape(KEYROWS, D), w_cols[...].reshape(D, D), (((1,), (1,)), ((), ())), preferred_element_type=F32
    ).astype(BF16)
    for c in range(2 * 8):
        mix[c // 2, c % 2] = mixed[:, c * HDIM:(c + 1) * HDIM].reshape(QC, OWNROWS, HDIM)

    def rows_of(who, at):
        return out.at[who, :, pl.ds(pl.multiple_of(at * OWNROWS, OWNROWS), OWNROWS)]

    for k in range(8):
        for flip in range(2):
            if k == 0 and flip == 0:
                continue
            other, device = chip(k, (core + flip) % 2)
            src = mix.at[other, (core + flip) % 2]
            remote(src, rows_of(core, spot), x_send.at[flip], x_recv.at[flip], device).start()
    last = pltpu.make_async_copy(mix.at[spot, core], rows_of(core, spot), loc_sem.at[5])
    last.start()
    for flip in range(2):
        arrived(mix.at[pl.ds(0, 7 + flip), 0], x_recv.at[flip])
    last.wait()
    for send in sends:
        send.wait_send()
    for flip in range(2):
        arrived(mix.at[pl.ds(0, 7 + flip), 0], x_send.at[flip])
    arrived(panel.at[:, 0, pl.ds(0, 9)], a_send.at[0])
    arrived(panel.at[:, pl.ds(0, 3)], a_send.at[1])
    arrived(w_cols.at[pl.ds(0, 7), 0, :, pl.ds(0, 256)], w_send.at[0])
    arrived(w_cols.at[:, 0], w_send.at[1])
    arrived(w_cols.at[:, 0, :, pl.ds(0, 768)], w_send.at[2])
    three = pl.ds(0, 3)
    for n, ref in enumerate((r1.at[three, :, :, 0], r2.at[three, :, :, 0], keys.at[:, three, 0])):
        arrived(ref, y_send.at[n])
    for n, ref in enumerate((r1.at[:, :, :, 0], r2.at[:, :, :, 0], keys.at[:, :, 0])):
        arrived(ref, s_send.at[n])
    arrived(numer_all.at[pl.ds(0, 7)], n_send.at[0])
    arrived(stats_all.at[pl.ds(0, 7)], t_send.at[0])
    first_sent()

    scatter_keys(waiting=True)


def shards(node_features, edge_weight, pattern, w_qkv, w_out, bias_gain, bias_rate):
    dma = pltpu.SemaphoreType.DMA
    anywhere = pl.BlockSpec(memory_space=pl.ANY)
    vmem = pl.BlockSpec(memory_space=pltpu.VMEM)
    smem = pl.BlockSpec(memory_space=pltpu.SMEM)
    counts = (2, 4 * CHUNKS, 3, 3, 2, 2, 2, 2, 3, 21, 3, 7, 2, 2, 6, 6, 1, QC, 1, QC, 3, 3, 2, 2)
    sems = [dma((n,)) for n in counts]
    mixed = pl.pallas_call(
        fused_kernel,
        name="fused",
        out_shape=jax.ShapeDtypeStruct((2, QC, BLK, HDIM), BF16),
        in_specs=[anywhere, smem, anywhere, anywhere, anywhere, smem, smem],
        out_specs=vmem,
        scratch_shapes=[
            pltpu.VMEM((CHUNKS * CLS, 4, 12, PIECE, 256), BF16),
            pltpu.VMEM((4, 2, QC, 2, BLK, HALF), BF16),
            pltpu.VMEM((4, 2, QC, 2, BLK, HALF), BF16),
            pltpu.VMEM((QC, 2 * BLK, HALF), F32),
            pltpu.VMEM((2, QC, BLK, HALF), BF16),
            pltpu.VMEM((2, QC, BLK, HALF), BF16),
            pltpu.VMEM((2 * CHUNKS * CLS, 3, PIECE, BLK), BF16),
            pltpu.VMEM((2, QC, BLK, HALF), BF16),
            pltpu.VMEM((2, 8, HALF), F32),
            pltpu.VMEM((2, 8, HALF), F32),
            pltpu.VMEM((QC, BLK, HALF), BF16),
            pltpu.VMEM((2, 4, 2, KEYROWS, D), BF16),
            pltpu.VMEM((HALF, D), BF16),
            pltpu.VMEM((D, 3 * D), BF16),
            pltpu.VMEM((ROWS, HALF), BF16),
            pltpu.VMEM((HALF, D), BF16),
            pltpu.VMEM((ROWS, D), BF16),
            pltpu.VMEM((ROWS, D), BF16),
            pltpu.VMEM((HEADS, HALF, ROWS), F32),
            pltpu.VMEM((HALF, ROWS), F32),
            pltpu.VMEM((HALF, D), BF16),
            pltpu.VMEM((8, QC, OWNROWS, D), BF16),
            pltpu.VMEM((HALF, BLK), F32),
            pltpu.VMEM((8, QC, OWNROWS, BLK), F32),
            pltpu.VMEM((QC, OWNROWS, D), BF16),
            pltpu.VMEM((8, 2, HDIM, D), BF16),
            pltpu.VMEM((8, 2, QC, OWNROWS, HDIM), BF16),
            dma((6,)),
            *sems,
        ],
        compiler_params=pltpu.CompilerParams(
            collective_id=0, has_side_effects=True, vmem_limit_bytes=65 * 1000 * 1000
        ),
    )(edge_weight, pattern.T, node_features, w_qkv, w_out.T, bias_gain, bias_rate)
    return mixed.reshape(ROWS, HDIM)


def solution(mesh):
    in_specs = (P("row", None), P("row", "col"), P("row", "col"), P(), P(None, "col"), P(), P())
    return jax.shard_map(shards, mesh=mesh, in_specs=in_specs, out_specs=P("row", "col"), check_vma=False)
```

```python
import math

import jax
import jax.numpy as jnp
from jax import lax
from jax.experimental import pallas as pl
from jax.experimental.pallas import tpu as pltpu
from jax.sharding import PartitionSpec as P

D = 1024
HEADS = 16
BLK = 128
HDIM = 64
NODES = 6144
ROWS = 768
HALF = 384
QC = 3
CHUNKS = 6
CLS = 4
X_FIRST = (2, 2, 2, 2, 2, 2)
RELAYED = (0, 1, 2, 4, 5)
T_LOAD = 3.9
T_QUERY = (5.5, 4.0, 5.0, 4.5)
T_KEY = (21.5, 21.0, 20.5, 19.0)
T_VALUE = (19.5, 23.5, 36.5, 24.5)
T_FIRST = (0.0, 3.0, 3.5)
T_OWN = (9.0, 17.0, 16.5, 24.0)
T_FAR = (8.5, 14.5, 15.0, 23.0)
T_FEAT = (0.5, 8.0, 13.0, 12.5, 18.0, 18.5)
T_PANEL = (
    (1.0, 1.5, 2.0, 2.5, 10.0, 11.0),
    (6.0, 6.5, 7.0, 7.5, 14.0, 16.0),
    (9.5, 10.5, 11.5, 12.0, 22.0, 26.5),
    (13.5, 15.5, 17.5, 20.0, 33.0, 37.0),
    (22.5, 25.5, 28.0, 30.0, 38.5, 41.0),
)
T_SCORE = (26.0, 28.5, 29.0, 29.5, 31.0, 31.5, 32.0, 32.5, 33.5, 35.0, 35.5, 36.0)
T_READY = 27.0
T_ONE = (
    (1, 0, (0, 128), 27.5), (2, 1, (0, 128), 30.5), (3, 2, (0, 64), 39.0), (6, 2, (64, 64), 41.5)
)
T_LATE = {
    1: (34.5, 34.0, 39.5, 40.0),
    2: (38.0, 37.5, 42.5, 44.0),
    3: (43.5, 43.0, 45.0, 46.5),
    6: (45.5, 46.0, 47.0, 47.5),
}
T_TWO = (((0, 1), 0, True, 40.5), ((2,), 0, True, 42.0), ((0, 1, 2), 1, False, 44.5))
FAMILY = (0, 1, 1, 1, 2, 0, 1)
PIECE = 16
KEYROWS = 48
OWNROWS = 16
LOG2E = 1.4426950408889634
BIG = 1e30
MESH = pl.DeviceIdType.MESH
F32 = jnp.float32
BF16 = jnp.bfloat16


class Place:
    def __init__(self):
        r = lax.axis_index("row")
        c = lax.axis_index("col")
        self.zh, self.y = r // 4, r % 4
        self.zl, self.x, self.core = c // 8, (c // 2) % 4, c % 2
        self.z = 2 * self.zh + self.zl

    def at(self, x=None, y=None, z=None, core=None):
        x = self.x if x is None else x
        y = self.y if y is None else y
        z = self.z if z is None else z
        core = self.core if core is None else core
        return ((z // 2) * 4 + y, ((z % 2) * 4 + x) * 2 + core)


def remote(src, dst, send, recv, device):
    return pltpu.make_async_remote_copy(
        src_ref=src, dst_ref=dst, send_sem=send, recv_sem=recv, device_id=device, device_id_type=MESH
    )


def fused_kernel(
    edge, pattern, feat, w_qkv, w_out_t, gain, rate, out,
    panel, r1, r2, acc, staged, landed, adj, first, mrows, mboth, first_sib, keys, own_feat, w_all, edge_v,
    query, key_proj, value_proj, scores, bias_in, numer, numer_all, stats, stats_all, att, w_cols, mix,
    loc_sem, a_send, a_recv, on_send, on_recv, i_send, i_recv, m_send, m_recv,
    y_send, y_recv, s_send, s_recv, f_send, f_recv, o_send, o_recv,
    n_send, n_recv, t_send, t_recv, w_send, w_recv, x_send, x_recv,
):
    me = Place()
    x, y, z, zh, zl, core = me.x, me.y, me.z, me.zh, me.zl, me.core
    sibling = me.at(core=1 - core)
    spot = zl * 4 + x
    ring = {
        "x+": me.at(x=(x + 1) % 4), "x-": me.at(x=(x + 3) % 4),
        "z+": me.at(z=(z + 1) % 4), "z-": me.at(z=(z + 3) % 4),
    }
    turned = (zl * 4 + x, (zh * 4 + y) * 2 + core)
    turned_self = (zl == zh) & (x == y)

    def chip(k, who=None):
        other = (spot + k) % 8
        return other, me.at(x=other % 4, z=2 * zh + other // 4, core=who)

    def y_peer(k):
        return me.at(y=(y + k) % 4)

    cross = (z + 2 * zl + 3) % 4
    friends = [sibling, me.at(z=cross, core=0), me.at(z=cross, core=1)]
    friends += [((1 - zl) * 4 + x, (zh * 4 + y) * 2 + core), (zl * 4 + x, ((1 - zh) * 4 + y) * 2 + core)]
    friends += [y_peer(k) for k in (1, 2, 3)]
    friends += [chip(k, who)[1] for k in range(1, 8) for who in (core, 1 - core)]
    barrier = pltpu.get_barrier_semaphore()
    for device in friends:
        pl.semaphore_signal(barrier, inc=1, device_id=device, device_id_type=MESH)

    @pl.when(jnp.logical_not(turned_self))
    def _():
        pl.semaphore_signal(barrier, inc=1, device_id=turned, device_id_type=MESH)

    sends = []

    def go(copy):
        copy.start()
        sends.append(copy)

    def arrived(ref, sem):
        pltpu.make_async_copy(ref, ref, sem).wait()

    loads = {
        "edge": pltpu.make_async_copy(edge, edge_v, loc_sem.at[0]),
        "feat": pltpu.make_async_copy(
            feat.at[pl.ds(pl.multiple_of(core * HALF, HALF), HALF)], own_feat, loc_sem.at[1]
        ),
        "w": pltpu.make_async_copy(w_qkv, w_all, loc_sem.at[2]),
    }
    for load in loads.values():
        load.start()
    loads["edge"].wait()

    same = (zl * 4 + x == zh * 4 + y)
    for rb in range(6):
        for cb in range(3):
            on = jnp.where(pattern[cb, rb] > 0, F32(1.0), F32(0.0))
            kept = edge_v[pl.ds(rb * BLK, BLK), pl.ds(cb * BLK, BLK)] * on.astype(BF16)
            adj[pl.ds(rb * 8, 8), cb] = kept.reshape(8, PIECE, BLK)
            row = lax.broadcasted_iota(jnp.int32, (BLK, BLK), 0) + rb * BLK
            col = lax.broadcasted_iota(jnp.int32, (BLK, BLK), 1) + cb * BLK + core * HALF
            diagonal = jnp.where((row == col) & same, F32(0.15), F32(0.0))
            value = (diagonal + F32(0.1275) * kept.astype(F32)) * on
            first[rb // 3, rb % 3, :, pl.ds(cb * BLK, BLK)] = value.astype(BF16)
            mboth[core, pl.ds(rb, 1), pl.ds(cb * BLK, BLK)] = jnp.full((1, BLK), on, F32)
    mask = mboth.at[core]

    pl.semaphore_wait(barrier, len(friends) + jnp.where(turned_self, 0, 1))

    goal = 2 * core + 1 - zl

    def first_copy(qc, mine):
        src = first.at[core, qc] if mine else first_sib.at[qc]
        way = core if mine else 1 - core
        dst = r1.at[y, zh, qc, core]
        return remote(src, dst, i_send.at[0 if mine else 1], i_recv.at[zh], me.at(z=2 * way + 1 - zl))

    def send_first(qc):
        if qc == 0:
            arrived(first_sib, on_recv.at[2])
        for mine in (True, False):
            first_copy(qc, mine).start()

    def first_sent():
        for n in range(2):
            arrived(first.at[0], i_send.at[n])
        for half in range(2):
            remote(mask, mrows.at[zh], m_send.at[half], m_recv.at[zh], me.at(z=goal, core=half)).wait_send()

    for half in range(2):
        remote(mask, mrows.at[zh], m_send.at[half], m_recv.at[zh], me.at(z=goal, core=half)).start()

    def own(who):
        return panel.at[:, z, pl.ds(x * 3, 3), :, pl.ds(pl.multiple_of(who * 128, 128), 128)]

    rows24 = CHUNKS * CLS
    here = pltpu.make_async_copy(adj.at[pl.ds(core * rows24, rows24)], own(core), loc_sem.at[3])
    here.start()
    over = remote(adj.at[pl.ds((1 - core) * rows24, rows24)], own(core), on_send.at[0], on_recv.at[0], sibling)
    go(over)
    go(remote(first.at[1 - core], first_sib, on_send.at[2], on_recv.at[2], sibling))
    go(remote(mask, mask, on_send.at[1], on_recv.at[1], sibling))

    mine = pl.ds(pl.multiple_of(spot * 2 * KEYROWS + core * KEYROWS, KEYROWS), KEYROWS)

    def scatter_keys(waiting=False):
        for block in range(2):
            is_self = turned_self & (zh == block)
            dst = keys.at[zl, x, core]
            if not waiting:
                @pl.when(is_self)
                def _():
                    pltpu.make_async_copy(feat.at[mine], dst, f_recv.at[zl]).start()

            @pl.when(jnp.logical_not(is_self))
            def _():
                device = (block * 4 + x, (zh * 4 + y) * 2 + core)
                copy = remote(feat.at[mine], dst, f_send.at[block], f_recv.at[zl], device)
                if waiting:
                    copy.wait_send()
                else:
                    copy.start()

    here.wait()
    over.wait_recv()

    def a_copy(j, cls, leg, kind):
        sign = 1 if cls % 2 == 0 else -1
        along_x = (cls < X_FIRST[j]) == (leg == 0)
        head = sign if kind != 1 else -sign
        device = ring[("x" if along_x else "z") + ("+" if head == 1 else "-")]
        hop = -sign if kind == 2 else 0
        jc = j * CLS + cls
        if along_x:
            at_x = (x + hop + 8) % 4
            cols = pl.ds(at_x * 3, 3)
            ref = panel.at[jc, z, cols] if leg == 0 else panel.at[jc, :, cols]
        else:
            at_z = (z + hop + 8) % 4
            ref = panel.at[jc, at_z, pl.ds(x * 3, 3)] if leg == 0 else panel.at[jc, at_z]
        step = j * 4 + leg * 2 + (0 if kind == 0 else 1)
        return remote(ref, ref, a_send.at[leg], a_recv.at[step], device)

    def a_stage(j, stage):
        if stage > 0:
            four = pl.ds(j * CLS, CLS)
            ref = {
                1: panel.at[four, 0, pl.ds(0, 3)], 2: panel.at[four, 0, pl.ds(0, 6)],
                3: panel.at[four, 0], 4: panel.at[four, pl.ds(0, 2)],
            }[stage]
            arrived(ref, a_recv.at[j * 4 + stage - 1])
        for cls in range(CLS):
            for kind in ((), (2,), (0, 1), (2,), ())[stage] if stage else (0, 1):
                a_copy(j, cls, stage // 2, kind).start()

    def y_copy(base, cut, k, arriving):
        ref = cut((y - k + 4) % 4 if arriving else y, core)
        return remote(ref, ref, y_send.at[FAMILY[base]], y_recv.at[base * 3 + k - 1], y_peer(k))

    def y_share(base, cut, k):
        ref = cut((y - k + 4) % 4, core)
        remote(ref, ref, s_send.at[FAMILY[base]], s_recv.at[base], sibling).start()

    def y_begin(base, cut, peers=(1, 3, 2)):
        for k in peers:
            y_copy(base, cut, k, False).start()
        y_share(base, cut, 0)

    def y_pass(base, cut, k, relay=None):
        y_copy(base, cut, k, True).wait_recv()
        if relay is not None:
            ref = relay((y - k + 4) % 4, core)
            remote(ref, ref, y_send.at[FAMILY[base]], y_recv.at[base * 3 + 1], y_peer(k)).start()
        y_share(base, cut, k)

    def y_done(base, ref):
        arrived(ref, s_recv.at[base])

    def cut1(a):
        return lambda at_y, who: r1.at[at_y, a, :, who]

    def cut2(q, part, a=slice(None)):
        rows = pl.ds(part[0], part[1])
        return lambda at_y, who: r2.at[at_y, a, q, who, rows]

    def cutk(at_y, who, a=slice(None)):
        return keys.at[a, at_y, who]

    def lhs(q, m, h, kc, part=(0, BLK)):
        pieces = pl.ds(q * 8 + part[0] // PIECE, part[1] // PIECE)
        top = panel[pieces, h, m * 3 + kc].reshape(part[1], 256)
        low = panel[pieces, 2 + h, m * 3 + kc].reshape(part[1], 256)
        return jnp.concatenate([top, low], axis=0)

    def diag(a, q, part):
        row = lax.broadcasted_iota(jnp.int32, (part[1], HALF), 0) + (q * BLK + part[0])
        col = lax.broadcasted_iota(jnp.int32, (part[1], HALF), 1)
        own_block = (1 - zl == a) & (y == x) & (core == zh)
        return jnp.where((row == col) & own_block, F32(0.15), F32(0.0))

    def masked_ranks(a, q, total, part=(0, BLK)):
        keep = mrows[a, pl.ds(core * 3 + q, 1), :] > 0.5
        return jnp.where(keep, diag(a, q, part) + 0.85 * total, 0.0).astype(BF16)

    def sweep_one(q, part):
        size = part[1]

        total = None
        for m in range(4):
            for h in range(2):
                for kc in range(3):
                    rhs = r1[m, h, kc].reshape(256, HALF)
                    product = jnp.dot(lhs(q, m, h, kc, part), rhs, preferred_element_type=F32)
                    total = product if total is None else total + product
        for a in range(2):
            value = masked_ranks(a, q, total[a * size:(a + 1) * size], part)
            r2[y, a, q, core, pl.ds(part[0], size)] = value

    def sweep_two(rows, kc, start):
        for q in rows:
            total = None if start else acc[q]
            for m in range(4):
                for h in range(2):
                    part = jnp.dot(lhs(q, m, h, kc), r2[m, h, kc].reshape(256, HALF), preferred_element_type=F32)
                    total = part if total is None else total + part
            acc[q] = total

    def project(dst, src, first_col, n):
        def body(t, _):
            cols = pl.ds(pl.multiple_of(t * 256, 256), 256)
            w = w_all[:, pl.ds(pl.multiple_of(first_col + t * 256, 256), 256)]
            dst[:, cols] = jnp.dot(src, w, preferred_element_type=F32).astype(BF16)
            return 0

        lax.fori_loop(n, n + 1, body, 0)

    lane = lax.broadcasted_iota(jnp.int32, (BLK, BLK), 1)

    def score_block(t):
        pair, row = t // QC, t % QC
        cols = pl.ds(pl.multiple_of(pair * BLK, BLK), BLK)
        rows = pl.ds(pl.multiple_of(row * BLK, BLK), BLK)
        q2 = query[rows, cols]
        k2 = key_proj[:, cols]
        away = [jnp.where(mboth[c, pl.ds(core * 3 + row, 1), :] > 0.5, F32(0.0), F32(-BIG)) for c in range(2)]
        away = jnp.concatenate(away, axis=1)
        kept = stats[rows, :]
        for side in range(2):
            head = pair * 2 + side
            q1 = jnp.where(lane // HDIM == side, q2, jnp.zeros_like(q2))
            s = lax.dot_general(q1, k2, (((1,), (1,)), ((), ())), preferred_element_type=F32)
            s = s * F32(LOG2E / math.sqrt(HDIM)) + away
            top = jnp.maximum(jnp.max(s, axis=1, keepdims=True), F32(-1e29))
            scores[head, rows, :] = s - top
            kept = jnp.where(lane == HEADS + head, top, kept)
        stats[rows, :] = kept

    def score_blocks(low, high):
        def body(t, _):
            score_block(t)
            return 0

        lax.fori_loop(low, high, body, 0)

    def expo_block(pair, row):
        cols = pl.ds(pl.multiple_of(pair * BLK, BLK), BLK)
        rows = pl.ds(pl.multiple_of(row * BLK, BLK), BLK)
        v2 = value_proj[:, cols]
        spread = bias_in[rows, :]
        both = []
        kept = stats[rows, :]
        for side in range(2):
            head = pair * 2 + side
            bias = (gain[head] * F32(LOG2E)) * jnp.tanh(spread * rate[head])
            e = jnp.exp2(scores[head, rows, :] + bias)
            kept = jnp.where(lane == head, jnp.sum(e, axis=1, keepdims=True), kept)
            both.append(jnp.dot(e.astype(BF16), v2, preferred_element_type=F32))
        stats[rows, :] = kept
        numer[rows, cols] = jnp.where(lane < HDIM, both[0], both[1]).astype(BF16)

    events = []

    def plan(when, what):
        events.append((when, len(events), what))

    def load_weights():
        loads["feat"].wait()
        loads["w"].wait()
        stats[...] = jnp.zeros_like(stats)

    def begin_ranks(base, a):
        pltpu.make_async_copy(first.at[0], r1.at[y, a, :, core], i_recv.at[a]).wait()
        y_begin(base, cut1(a), (1, 3) if base in RELAYED else (1, 3, 2))

    def begin_keys():
        for block in range(2):
            arrived(keys.at[block, y, core], f_recv.at[block])
        y_begin(4, cutk, (1, 3) if 4 in RELAYED else (1, 3, 2))

    plan(T_LOAD, load_weights)
    for n in range(4):
        plan(T_QUERY[n], lambda n=n: project(query, own_feat[...], 0, n))
        plan(T_KEY[n], lambda n=n: project(key_proj, keys[...].reshape(ROWS, D), D, n))
        plan(T_VALUE[n], lambda n=n: project(value_proj, keys[...].reshape(ROWS, D), 2 * D, n))
    for base, times in ((0, T_OWN), (5, T_FAR)):
        a = base // 5
        plan(times[0], lambda base=base, a=a: begin_ranks(base, a))
        for k, when in zip((1, 3, 2), times[1:]):
            relay = cut1(a) if base in RELAYED and k == 1 + 2 * a else None
            plan(when, lambda base=base, a=a, k=k, relay=relay: y_pass(base, cut1(a), k, relay))
    plan(T_FEAT[0], scatter_keys)
    for qc in range(QC):
        plan(T_FIRST[qc], lambda qc=qc: send_first(qc))
    plan(T_FEAT[1], begin_keys)
    for k, when in zip((1, 3, 2), T_FEAT[2:5]):
        relay = None
        if 4 in RELAYED and k != 2:
            relay = lambda at_y, who, k=k: cutk(at_y, who, k // 2)
        plan(when, lambda k=k, relay=relay: y_pass(4, cutk, k, relay))
    plan(T_FEAT[5], lambda: y_done(4, keys.at[:, :, 0]))
    for j in range(CHUNKS):
        for stage in range(5):
            plan(T_PANEL[stage][j], lambda j=j, stage=stage: a_stage(j, stage))

    def ready():
        y_done(0, r1.at[:, 0, :, 0])
        y_done(5, r1.at[:, 0, :, 0])
        for a in range(2):
            pltpu.make_async_copy(mask, mrows.at[a], m_recv.at[a]).wait()

    plan(T_SCORE[0] - 0.1, lambda: remote(mask, mboth.at[1 - core], on_send.at[1], on_recv.at[1], sibling).wait_recv())
    for n, when in enumerate(T_SCORE):
        plan(when, lambda n=n: score_blocks(2 * n, 2 * n + 2))
    plan(T_READY, ready)
    for base, q, part, when in T_ONE:
        peers = (1, 3) if base in RELAYED else (1, 3, 2)

        def first_sweep(base=base, q=q, part=part, peers=peers):
            sweep_one(q, part)
            y_begin(base, cut2(q, part), peers)

        plan(when, first_sweep)
        for k, late in zip((1, 3, 2), T_LATE[base]):
            relay = cut2(q, part, k // 2) if k != 2 and len(peers) == 2 else None
            plan(late, lambda base=base, q=q, part=part, k=k, relay=relay: y_pass(base, cut2(q, part), k, relay))
        rows = pl.ds(part[0], part[1])
        plan(T_LATE[base][3], lambda base=base, q=q, rows=rows: y_done(base, r2.at[:, :, q, 0, rows]))
    for rows, kc, start, when in T_TWO:
        plan(when, lambda rows=rows, kc=kc, start=start: sweep_two(rows, kc, start))

    quarter = pl.ds(pl.multiple_of(y * 256, 256), 256)

    def send_weights():
        src, dst = w_out_t.at[:, quarter], w_cols.at[spot, core, :, quarter]
        for k in range(1, 8):
            remote(src, dst, w_send.at[0], w_recv.at[0], chip(k)[1]).start()
        pltpu.make_async_copy(src, dst, loc_sem.at[4]).start()

    def cross_weights():
        ref = w_cols.at[:, core, :, quarter]
        arrived(w_cols.at[spot, core, :, quarter], loc_sem.at[4])
        arrived(w_cols.at[pl.ds(0, 7), 0, :, pl.ds(0, 256)], w_recv.at[0])
        for k in (1, 3, 2):
            remote(ref, ref, w_send.at[2], w_recv.at[2], y_peer(k)).start()

    plan(T_PANEL[3][5] + 0.01, send_weights)
    for _, _, what in sorted(events, key=lambda e: e[:2]):
        what()

    for q in range(QC):
        sweep_two((q,), 2, False)
        for a in range(2):
            staged[a, q] = masked_ranks(a, q, acc[q, a * BLK:(a + 1) * BLK])
        for a in range(2):
            dst = landed.at[zh, q]
            go(remote(staged.at[a, q], dst, o_send.at[2 * q + a], o_recv.at[2 * q + zh], me.at(z=2 * a + 1 - zl)))

    cross_weights()

    def forward_weights():
        arrived(w_cols.at[:, 0, :, pl.ds(0, 768)], w_recv.at[2])
        ref = w_cols.at[:, core]
        remote(ref, ref, w_send.at[1], w_recv.at[1], sibling).start()

    def widen(ref, half, q):
        cols = pl.ds(half * HALF, HALF)
        bias_in[pl.ds(q * BLK, BLK), cols] = ref[q].astype(F32) * F32(math.sqrt(NODES))

    def owned(q, at):
        return pl.ds(pl.multiple_of(q * BLK + at * OWNROWS, OWNROWS), OWNROWS)

    def attend(q):
        for half in range(2):
            arrived(landed.at[half, q], o_recv.at[2 * q + half])
            widen(landed.at[half], half, q)

        def body(t, _):
            expo_block(t, q)
            return 0

        lax.fori_loop(0, HEADS // 2, body, 0)
        for k in range(1, 8):
            other, device = chip(k)
            rows = owned(q, other)
            remote(numer.at[rows], numer_all.at[spot, q], n_send.at[0], n_recv.at[q], device).start()
            remote(stats.at[rows], stats_all.at[spot, q], t_send.at[0], t_recv.at[q], device).start()
        numer_all[spot, q] = numer[owned(q, spot), :]
        stats_all[spot, q] = stats[owned(q, spot), :]

    low = lax.broadcasted_iota(jnp.int32, (OWNROWS, BLK), 1) < HDIM

    def combine(q):
        arrived(stats_all.at[pl.ds(0, 7), q], t_recv.at[q])
        arrived(numer_all.at[pl.ds(0, 7), q], n_recv.at[q])
        table = [stats_all[s, q] for s in range(8)]
        tops = [t[:, HEADS:2 * HEADS] for t in table]
        peak = tops[0]
        for t in tops[1:]:
            peak = jnp.maximum(peak, t)
        weights = [jnp.exp2(t - peak) for t in tops]
        total = weights[0] * table[0][:, :HEADS]
        for s in range(1, 8):
            total = total + weights[s] * table[s][:, :HEADS]
        weights = [w / total for w in weights]
        for pair in range(HEADS // 2):
            cols = pl.ds(pair * BLK, BLK)
            value = jnp.zeros((OWNROWS, BLK), F32)
            for s in range(8):
                w = jnp.where(low, weights[s][:, 2 * pair:2 * pair + 1], weights[s][:, 2 * pair + 1:2 * pair + 2])
                value = value + w * numer_all[s, q, :, cols].astype(F32)
            att[q, :, cols] = value.astype(BF16)

    for q in range(QC):
        attend(q)
    forward_weights()
    for q in range(QC):
        combine(q)

    arrived(w_cols.at[:, 0], w_recv.at[1])
    mixed = lax.dot_general(
        att[...].reshape(KEYROWS, D), w_cols[...].reshape(D, D), (((1,), (1,)), ((), ())), preferred_element_type=F32
    ).astype(BF16)
    for c in range(2 * 8):
        mix[c // 2, c % 2] = mixed[:, c * HDIM:(c + 1) * HDIM].reshape(QC, OWNROWS, HDIM)

    def rows_of(who, at):
        return out.at[who, :, pl.ds(pl.multiple_of(at * OWNROWS, OWNROWS), OWNROWS)]

    for k in range(8):
        for flip in range(2):
            if k == 0 and flip == 0:
                continue
            other, device = chip(k, (core + flip) % 2)
            src = mix.at[other, (core + flip) % 2]
            remote(src, rows_of(core, spot), x_send.at[flip], x_recv.at[flip], device).start()
    last = pltpu.make_async_copy(mix.at[spot, core], rows_of(core, spot), loc_sem.at[5])
    last.start()
    for flip in range(2):
        arrived(mix.at[pl.ds(0, 7 + flip), 0], x_recv.at[flip])
    last.wait()
    for send in sends:
        send.wait_send()
    for flip in range(2):
        arrived(mix.at[pl.ds(0, 7 + flip), 0], x_send.at[flip])
    arrived(panel.at[:, 0, pl.ds(0, 9)], a_send.at[0])
    arrived(panel.at[:, pl.ds(0, 3)], a_send.at[1])
    arrived(w_cols.at[pl.ds(0, 7), 0, :, pl.ds(0, 256)], w_send.at[0])
    arrived(w_cols.at[:, 0], w_send.at[1])
    arrived(w_cols.at[:, 0, :, pl.ds(0, 768)], w_send.at[2])
    three = pl.ds(0, 3)
    for n, ref in enumerate((r1.at[three, :, :, 0], r2.at[three, :, :, 0], keys.at[:, three, 0])):
        arrived(ref, y_send.at[n])
    for n, ref in enumerate((r1.at[:, :, :, 0], r2.at[:, :, :, 0], keys.at[:, :, 0])):
        arrived(ref, s_send.at[n])
    arrived(numer_all.at[pl.ds(0, 7)], n_send.at[0])
    arrived(stats_all.at[pl.ds(0, 7)], t_send.at[0])
    first_sent()

    scatter_keys(waiting=True)


def shards(node_features, edge_weight, pattern, w_qkv, w_out, bias_gain, bias_rate):
    dma = pltpu.SemaphoreType.DMA
    anywhere = pl.BlockSpec(memory_space=pl.ANY)
    vmem = pl.BlockSpec(memory_space=pltpu.VMEM)
    smem = pl.BlockSpec(memory_space=pltpu.SMEM)
    counts = (2, 4 * CHUNKS, 3, 3, 2, 2, 2, 2, 3, 21, 3, 7, 2, 2, 6, 6, 1, QC, 1, QC, 3, 3, 2, 2)
    sems = [dma((n,)) for n in counts]
    mixed = pl.pallas_call(
        fused_kernel,
        name="fused",
        out_shape=jax.ShapeDtypeStruct((2, QC, BLK, HDIM), BF16),
        in_specs=[anywhere, smem, anywhere, anywhere, anywhere, smem, smem],
        out_specs=vmem,
        scratch_shapes=[
            pltpu.VMEM((CHUNKS * CLS, 4, 12, PIECE, 256), BF16),
            pltpu.VMEM((4, 2, QC, 2, BLK, HALF), BF16),
            pltpu.VMEM((4, 2, QC, 2, BLK, HALF), BF16),
            pltpu.VMEM((QC, 2 * BLK, HALF), F32),
            pltpu.VMEM((2, QC, BLK, HALF), BF16),
            pltpu.VMEM((2, QC, BLK, HALF), BF16),
            pltpu.VMEM((2 * CHUNKS * CLS, 3, PIECE, BLK), BF16),
            pltpu.VMEM((2, QC, BLK, HALF), BF16),
            pltpu.VMEM((2, 8, HALF), F32),
            pltpu.VMEM((2, 8, HALF), F32),
            pltpu.VMEM((QC, BLK, HALF), BF16),
            pltpu.VMEM((2, 4, 2, KEYROWS, D), BF16),
            pltpu.VMEM((HALF, D), BF16),
            pltpu.VMEM((D, 3 * D), BF16),
            pltpu.VMEM((ROWS, HALF), BF16),
            pltpu.VMEM((HALF, D), BF16),
            pltpu.VMEM((ROWS, D), BF16),
            pltpu.VMEM((ROWS, D), BF16),
            pltpu.VMEM((HEADS, HALF, ROWS), F32),
            pltpu.VMEM((HALF, ROWS), F32),
            pltpu.VMEM((HALF, D), BF16),
            pltpu.VMEM((8, QC, OWNROWS, D), BF16),
            pltpu.VMEM((HALF, BLK), F32),
            pltpu.VMEM((8, QC, OWNROWS, BLK), F32),
            pltpu.VMEM((QC, OWNROWS, D), BF16),
            pltpu.VMEM((8, 2, HDIM, D), BF16),
            pltpu.VMEM((8, 2, QC, OWNROWS, HDIM), BF16),
            dma((6,)),
            *sems,
        ],
        compiler_params=pltpu.CompilerParams(
            collective_id=0, has_side_effects=True, vmem_limit_bytes=65 * 1000 * 1000
        ),
    )(edge_weight, pattern.T, node_features, w_qkv, w_out.T, bias_gain, bias_rate)
    return mixed.reshape(ROWS, HDIM)


def solution(mesh):
    in_specs = (P("row", None), P("row", "col"), P("row", "col"), P(), P(None, "col"), P(), P())
    return jax.shard_map(shards, mesh=mesh, in_specs=in_specs, out_specs=P("row", "col"), check_vma=False)
```
